256 devices in a mesh: gx: 32 (over z, y), gy: 8 (over x, core).
Axes of the slice: x: 4, y: 4, z: 8, core: 2. Of those that a mesh axis runs over, the one named last changes fastest.
Arguments:
- tracer: float32 [128, 1024, 1024], P(None, 'gx', 'gy'), may hold values from -11 to 11
- velocity: float32 [2, 1024, 1024], P(None, 'gx', 'gy'), may hold values from -0.25 to 0.25
- diffusivity: float32 [128], replicated, may hold values from 0.02 to 0.08
- singular: float32 [94], replicated, may hold values from 0.5 to 8
- basis_vectors: float32 [94, 2, 1024, 1024], P(None, None, 'gx', 'gy'), may hold values from -10 to 10, as said below
Outputs:
- tracer_next: float32 [128, 1024, 1024], P(None, 'gx', 'gy')
- basis_next: float32 [96, 2, 1024, 1024], P(None, None, 'gx', 'gy')
The draws below stay inside these ranges and needn't reach their ends.
Inputs may be any that keep to these rules, and one draw needn't show every extreme that they name: The 94 vectors basis_vectors[i], each over all 2 x 1024 x 1024 cells, are orthogonal with squared length 2097152, to float32 rounding.
All inputs are finite; a program needn't handle non-finite values.
Results may differ from the reference program's by a relative error of at most 0.0003.
Values sent between devices are 32-bit elements; how exact they have to be, the bound alone decides.
No kernel may reach another device: no remote copies, remote signals or barrier semaphores. Data moves between devices by JAX's collectives and lax.ppermute only.
A program may use at most 64 MiB of HBM per device.

```python
import math
import jax
import jax.numpy as jnp
from jax import lax

NZ = 128
WZ = 2
K = 94
ROOT_ITERS = 5
NX = 1024
NY = 1024
ROWS = 2097152


def joint_draw(key):
    key_noise = jax.random.fold_in(key, 101)
    key_rough = jax.random.fold_in(key, 102)
    key_weights = jax.random.fold_in(key, 103)
    key_mixture = jax.random.fold_in(key, 104)
    position = jnp.arange(NX, dtype=jnp.float32) / NX
    roughness = jax.random.uniform(key_rough, (NX,), jnp.float32, math.log(0.7), math.log(1.4))
    amplitude = 0.6 * jnp.exp(position * math.log(3.0) + roughness)
    noise_part = jax.random.truncated_normal(key_noise, -4.0, 4.0, (NZ, NX, NY), jnp.float32)
    tracer = noise_part * amplitude[None, :, None]
    window = tracer[:WZ].reshape(-1)
    weights = jax.random.normal(key_weights, (K,), jnp.float32)
    mixture = weights[:, None] * window[None, :] + jax.random.normal(key_mixture, (K, ROWS), jnp.float32)
    gram_matrix = jnp.dot(mixture, mixture.T, precision=lax.Precision.HIGHEST)
    lower_factor = jnp.linalg.cholesky(gram_matrix)
    vectors = lax.linalg.triangular_solve(lower_factor, mixture, left_side=True, lower=True) * math.sqrt(ROWS)
    return (tracer, vectors.reshape(K, WZ, NX, NY))


def draw_tracer(key, part):
    return joint_draw(key)[0]


def draw_basis_vectors(key, part):
    return joint_draw(key)[1]


def block_levels(own_key, extent, cuts, smallest, largest):
    def one(dim, shards_of):
        heights = jax.random.uniform(jax.random.fold_in(jax.random.fold_in(own_key, 6), dim), (shards_of,), jnp.float32, smallest / len(cuts), largest / len(cuts))
        return jnp.repeat(jnp.exp(heights), extent[dim] // shards_of).reshape((-1,) + (1,) * (len(extent) - dim - 1))

    factor_of = one(*cuts[0])
    for cut in cuts[1:]:
        factor_of = factor_of * one(*cut)
    return factor_of


def setup_inputs(seed: int = 0) -> dict:
    key_list = jax.random.split(jax.random.key(seed), 6)
    return {
        "tracer": draw_tracer(jax.random.fold_in(key_list[5], 71), 0),
        "velocity": jnp.clip(jax.random.uniform(key_list[1], (2, NX, NY), jnp.float32, -0.25, 0.25) * block_levels(key_list[1], (2, NX, NY), ((1, 32), (2, 8)), -0.4, 0.0), -0.25, 0.25),
        "diffusivity": jnp.clip(jnp.exp(jax.random.uniform(key_list[2], (NZ,), jnp.float32, math.log(0.02), math.log(0.08))), 0.02, 0.08),
        "singular": jnp.clip(jnp.exp(jax.random.uniform(key_list[3], (K,), jnp.float32, math.log(0.5), math.log(8.0))), 0.5, 8.0),
        "basis_vectors": draw_basis_vectors(jax.random.fold_in(key_list[5], 71), 0),
    }


def advance(state, velocity, diffusivity):
    speed_x = velocity[0]
    speed_y = velocity[1]

    def level(level_index):
        centre = state[level_index]
        level_below = state[(level_index + NZ - 1) % NZ]
        level_above = state[(level_index + 1) % NZ]
        west_cells = jnp.roll(centre, 1, 0)
        east_cells = jnp.roll(centre, -1, 0)
        south_cells = jnp.roll(centre, 1, 1)
        north_cells = jnp.roll(centre, -1, 1)
        spread = west_cells + east_cells + south_cells + north_cells + level_below + level_above - 6.0 * centre
        carried = jnp.maximum(speed_x, 0.0) * (centre - west_cells) + jnp.minimum(speed_x, 0.0) * (east_cells - centre) + jnp.maximum(speed_y, 0.0) * (centre - south_cells) + jnp.minimum(speed_y, 0.0) * (north_cells - centre)
        return centre + diffusivity[level_index] * spread - carried
    return lax.map(level, jnp.arange(NZ, dtype=jnp.int32))

def upper_factor(gram_matrix):
    first_entry = jnp.sqrt(gram_matrix[0, 0])
    cross_entry = gram_matrix[0, 1] / first_entry
    second_entry = jnp.sqrt(gram_matrix[1, 1] - cross_entry * cross_entry)
    zero_entry = jnp.zeros_like(first_entry)
    return jnp.stack([jnp.stack([first_entry, cross_entry]), jnp.stack([zero_entry, second_entry])])

def orthonormal_columns(residual, factor):
    first_column = residual[0] / factor[0, 0]
    second_column = (residual[1] - factor[0, 1] * first_column) / factor[1, 1]
    return jnp.stack([first_column, second_column])

def inverse_spd(matrix):
    lower_factor = jnp.linalg.cholesky(matrix)
    identity = jnp.eye(matrix.shape[0], dtype=matrix.dtype)
    solved = lax.linalg.triangular_solve(lower_factor, identity, left_side=True, lower=True)
    return jnp.dot(solved.T, solved, precision=lax.Precision.HIGHEST)

def square_root_core(singular, projections, factor):
    vector_count = singular.shape[0]
    core_matrix = jnp.block([[jnp.diag(singular), projections], [jnp.zeros((2, vector_count), jnp.float32), factor]])
    squared = jnp.dot(core_matrix, core_matrix.T, precision=lax.Precision.HIGHEST)
    scale_factor = jnp.trace(squared) / (vector_count + 2)
    current = squared / scale_factor
    partner = jnp.eye(vector_count + 2, dtype=squared.dtype)
    for repeat in range(ROOT_ITERS):
        new_current = 0.5 * (current + inverse_spd(partner))
        new_partner = 0.5 * (partner + inverse_spd(current))
        current = 0.5 * (new_current + new_current.T)
        partner = 0.5 * (new_partner + new_partner.T)
    return jnp.sqrt(scale_factor) * current

def reference(tracer, velocity, diffusivity, singular, basis_vectors):
    after_one = advance(tracer, velocity, diffusivity)
    after_two = advance(after_one, velocity, diffusivity)
    snapshots = jnp.stack([after_one[:WZ].reshape(-1), after_two[:WZ].reshape(-1)])
    flat_basis = basis_vectors.reshape(K, -1)
    projections = jnp.dot(flat_basis, snapshots.T, precision=lax.Precision.HIGHEST) / ROWS
    residual = snapshots - jnp.dot(projections.T, flat_basis, precision=lax.Precision.HIGHEST)
    gram_matrix = jnp.dot(residual, residual.T, precision=lax.Precision.HIGHEST) / ROWS + 1e-06 * jnp.eye(2, dtype=jnp.float32)
    factor = upper_factor(gram_matrix)
    columns = orthonormal_columns(residual, factor)
    core_root = square_root_core(singular, projections, factor)
    rotated = jnp.dot(core_root[:K].T, flat_basis, precision=lax.Precision.HIGHEST) + jnp.dot(core_root[K:].T, columns, precision=lax.Precision.HIGHEST)
    return (after_two, rotated.reshape(K + 2, WZ, NX, NY))
```

```python
import math

import jax
import jax.numpy as jnp
from jax import lax
from jax.experimental import pallas as pl
from jax.experimental.pallas import tpu as pltpu
from jax.sharding import Mesh
from jax.sharding import PartitionSpec as P

F32 = jnp.float32
BF16 = jnp.bfloat16
GX = ("z", "y")
GY = ("x", "c")
CHIPS = ("z", "y", "x")
ROOT_ITERS = 5
SHIFTS = 2**ROOT_ITERS
POLES = SHIFTS // 2 - 1
VMEM = pltpu.VMEM


def lanes_of(shape):
    return lax.broadcasted_iota(jnp.int32, shape, len(shape) - 1)


def rows_of(shape):
    return lax.broadcasted_iota(jnp.int32, shape, len(shape) - 2)


def step(c, xm, xp, ym, yp, zm, zp, d, vxp, vxn, vyp, vyn):
    spread = (xm + xp) + (ym + yp) + (zm + zp) - 6.0 * c
    carried = (vxp * (c - xm) + vxn * (xp - c)) + (vyp * (c - ym) + vyn * (yp - c))
    return c + d * spread - carried


def signed_parts(vx, vy):
    return jnp.maximum(vx, 0.0), jnp.minimum(vx, 0.0), jnp.maximum(vy, 0.0), jnp.minimum(vy, 0.0)


def before(c, ghost, axis):
    n = c.shape[axis]
    at = lax.broadcasted_iota(jnp.int32, c.shape, axis)
    return jnp.where(at == 0, ghost, pltpu.roll(c, 1, axis))


def after(c, ghost, axis):
    n = c.shape[axis]
    at = lax.broadcasted_iota(jnp.int32, c.shape, axis)
    return jnp.where(at == n - 1, ghost, pltpu.roll(c, n - 1, axis))


def pack_columns_kernel(levels, tracer, velocity, left, right):
    nx, ny = tracer.shape[1], tracer.shape[2]
    lane = lanes_of((nx, ny))

    def level(z, carry):
        a, b, y, w = carry
        r = pltpu.roll(tracer[z], z, 1)
        rel = (lane - z) & (ny - 1)
        a = jnp.where(rel == 0, r, a)
        b = jnp.where(rel == 1, r, b)
        y = jnp.where(rel == ny - 1, r, y)
        w = jnp.where(rel == ny - 2, r, w)
        return a, b, y, w

    zero = jnp.zeros((nx, ny), F32)
    a, b, y, w = lax.fori_loop(0, levels, level, (zero,) * 4, unroll=8)
    left[0] = a
    left[1] = pltpu.roll(b, ny - 1, 1)
    right[0] = pltpu.roll(y, 1, 1)
    right[1] = pltpu.roll(w, 2, 1)
    vx, vy = velocity[0], velocity[1]
    left[2] = jnp.where(lane == 0, vx, pltpu.roll(vy, 1, 1))
    right[2] = jnp.where(lane == ny - 1, vx, pltpu.roll(vy, ny - 1, 1))


def pack_rows_kernel(low, high, velocity, from_left, from_right, up, down):
    nx = low.shape[1]
    for edge, inner, out in ((0, 1, up), (nx - 1, nx - 2, down)):
        for s in range(6):
            ref, z = (high, s) if s < 2 else (low, s - 2)
            out[s : s + 1, :] = ref[z, edge : edge + 1, :]
            out[8 + s : 9 + s, :] = ref[z, inner : inner + 1, :]
        for s in (6, 7, 14, 15, 20, 21, 22, 23):
            out[s : s + 1, :] = jnp.zeros((1, low.shape[2]), F32)
        out[16:17, :] = velocity[0, edge : edge + 1, :]
        out[17:18, :] = velocity[1, edge : edge + 1, :]
        out[18:19, :] = from_left[0, edge : edge + 1, :]
        out[19:20, :] = from_right[0, edge : edge + 1, :]


def window_kernel(
    diff, low, high, velocity, diff_row, own_left, own_right, from_left, from_right,
    own_up, own_down, from_up, from_down, basis,
    snaps, sums, ghost_left, ghost_right, q0, q1,
):
    nz, nx, ny = diff.shape[0], low.shape[1], low.shape[2]
    count = basis.shape[0]
    dz = diff_row[...]
    for gin, inner, outer, corner, vx_at, vy_at, out in (
        (from_left, None, own_left, 18, ny - 1, ny - 2, ghost_left),
        (from_right, own_right, None, 19, 0, 1, ghost_right),
    ):
        c = gin[0]
        ym = gin[1] if inner is None else inner[0]
        yp = gin[1] if outer is None else outer[0]
        vx = gin[2][:, vx_at : vx_at + 1]
        vy = gin[2][:, vy_at : vy_at + 1]
        parts = signed_parts(vx, vy)
        xm = before(c, from_up[corner : corner + 1, :], 0)
        xp = after(c, from_down[corner : corner + 1, :], 0)
        out[...] = step(c, xm, xp, ym, yp, pltpu.roll(c, 1, 1), pltpu.roll(c, nz - 1, 1), dz, *parts)

    sub = rows_of((8, ny))
    lane = lanes_of((8, ny))
    d_rows = jnp.where(sub == 2, diff[0], diff[1])
    ghost_rows = []
    for gin, own, top in ((from_up, own_up, True), (from_down, own_down, False)):
        c = gin[0:8, :]
        beyond, near = gin[8:16, :], own[0:8, :]
        xm, xp = (beyond, near) if top else (near, beyond)
        west = jnp.where(sub == 2, gin[18:19, 0:1], gin[18:19, 1:2])
        east = jnp.where(sub == 2, gin[19:20, 0:1], gin[19:20, 1:2])
        parts = signed_parts(gin[16:17, :], gin[17:18, :])
        ghost_rows.append(
            step(c, xm, xp, before(c, west, 1), after(c, east, 1),
                 pltpu.roll(c, 1, 0), pltpu.roll(c, 7, 0), d_rows, *parts)
        )

    parts = signed_parts(velocity[0], velocity[1])
    u = [high[0], high[1], low[0], low[1], low[2], low[3]]
    first = []
    for s in range(1, 5):
        z = (s - 2) % nz
        c = u[s]
        xm = before(c, from_up[s : s + 1, :], 0)
        xp = after(c, from_down[s : s + 1, :], 0)
        ym = before(c, from_left[0][:, z : z + 1], 1)
        yp = after(c, from_right[0][:, z : z + 1], 1)
        first.append(step(c, xm, xp, ym, yp, u[s - 1], u[s + 1], diff[z], *parts))
    for z in range(2):
        c = first[z + 1]
        snaps[0, z * nx : (z + 1) * nx, :] = c
        xm = before(c, ghost_rows[0][z + 2 : z + 3, :], 0)
        xp = after(c, ghost_rows[1][z + 2 : z + 3, :], 0)
        ym = before(c, ghost_left[:, z : z + 1], 1)
        yp = after(c, ghost_right[:, z : z + 1], 1)
        snaps[1, z * nx : (z + 1) * nx, :] = step(
            c, xm, xp, ym, yp, first[z], first[z + 2], diff[z], *parts
        )

    rows = 2 * nx
    pieces = rows // 8

    def folded(a, b):
        total = a[0:8, :] * b[0:8, :]
        for i in range(1, pieces):
            total = total + a[8 * i : 8 * i + 8, :] * b[8 * i : 8 * i + 8, :]
        return jnp.sum(total, axis=0, keepdims=True)

    q0[...] = jnp.zeros_like(q0)
    q1[...] = jnp.zeros_like(q1)

    def product(k, carry):
        b = basis[k]
        q0[pl.ds(k, 1), :] = folded(b, snaps[0])
        q1[pl.ds(k, 1), :] = folded(b, snaps[1])
        return carry

    lax.fori_loop(0, count, product, 0, unroll=2)
    cross = folded(snaps[0], snaps[1])
    q0[count : count + 1, :] = folded(snaps[0], snaps[0])
    q0[count + 1 : count + 2, :] = cross
    q1[count : count + 1, :] = cross
    q1[count + 1 : count + 2, :] = folded(snaps[1], snaps[1])
    ones = jnp.ones((8, ny), F32)
    over_lanes = (((1,), (1,)), ((), ()))
    for m, q in enumerate((q0, q1)):
        line = lax.dot_general(
            ones, q[...], over_lanes, precision=lax.Precision.HIGHEST, preferred_element_type=F32
        )
        sums[m : m + 1, :] = line[0:1, :]


def bulk_kernel(
    diff, tracer, velocity, diff_rows, from_left, from_right, ghost_left, ghost_right,
    from_up, from_down, top, bottom, out, first, above, below,
):
    nz, nx, ny = tracer.shape
    eye = rows_of((nz, nz)) == lanes_of((nz, nz))
    d_all = diff_rows[...]

    for gin, bulk, own, is_top, res in (
        (from_up, top, 0, True, above),
        (from_down, bottom, nx - 1, False, below),
    ):
        c, beyond, near = bulk[0], bulk[1], tracer[:, own, :]
        xm, xp = (beyond, near) if is_top else (near, beyond)
        west = jnp.sum(jnp.where(eye, gin[18:19, :], 0.0), axis=1, keepdims=True)
        east = jnp.sum(jnp.where(eye, gin[19:20, :], 0.0), axis=1, keepdims=True)
        parts = signed_parts(gin[16:17, :], gin[17:18, :])
        res[...] = step(c, xm, xp, before(c, west, 1), after(c, east, 1),
                        pltpu.roll(c, 1, 0), pltpu.roll(c, nz - 1, 0), d_all, *parts)

    parts = signed_parts(velocity[0], velocity[1])

    def sweep(src, dst, row_up, row_down, col_left, col_right):
        def level(z, carry):
            c = src[z]
            back = (nz - z) & (nz - 1)
            ym = before(c, pltpu.roll(col_left, back, 1), 1)
            yp = after(c, pltpu.roll(col_right, (nz - 1 - z) & (nz - 1), 1), 1)
            xm = before(c, row_up[pl.ds(z, 1), :], 0)
            xp = after(c, row_down[pl.ds(z, 1), :], 0)
            zm = src[(z + nz - 1) & (nz - 1)]
            zp = src[(z + 1) & (nz - 1)]
            dst[z] = step(c, xm, xp, ym, yp, zm, zp, diff[z], *parts)
            return carry

        lax.fori_loop(0, nz, level, 0, unroll=2)

    sweep(tracer, first, top.at[0], bottom.at[0], from_left[0], from_right[0])
    sweep(first, out, above, below, ghost_left[...], ghost_right[...])


def split_kernel(basis, snaps, upper, lower):
    count, rows, ny = basis.shape
    for b in range(rows // 8):
        part = slice(8 * b, 8 * b + 8)
        x = jnp.concatenate([basis[:, part, :], snaps[:, part, :]], axis=0)
        x = jnp.swapaxes(x, 0, 1)
        for i in range(8):
            pair, half = (8 * b + i) // 2, i % 2
            v = x[i]
            hi = v.astype(BF16)
            upper[pair, :, half * ny : (half + 1) * ny] = hi
            lower[pair, :, half * ny : (half + 1) * ny] = (v - hi.astype(F32)).astype(BF16)


def core_kernel(rows_all, parts, singular, upper, lower, out, block, sems):
    count = out.shape[0] - 2
    n = parts.shape[2]
    total = jnp.sum(parts[...], axis=0)
    total = total + pltpu.roll(total, 2, 0)
    total = total + pltpu.roll(total, 4, 0)
    total = total * (1.0 / rows_all)
    lane = lanes_of((1, n))
    zero = jnp.zeros((1, n), F32)

    def add(x):
        return jnp.sum(x, axis=1, keepdims=True)

    def pick(x, at):
        return add(jnp.where(lane == at, x, zero))

    p0 = jnp.where(lane < count, total[0:1, :], zero)
    p1 = jnp.where(lane < count, total[1:2, :], zero)
    g00 = pick(total[0:1, :], count) - add(p0 * p0) + 1e-06
    g01 = pick(total[0:1, :], count + 1) - add(p0 * p1)
    g11 = pick(total[1:2, :], count + 1) - add(p1 * p1) + 1e-06
    r11 = jnp.sqrt(g00)
    r12 = g01 / r11
    r22 = jnp.sqrt(g11 - r12 * r12)
    u0 = jnp.where(lane == count, r11, p0)
    u1 = jnp.where(lane == count, r12, jnp.where(lane == count + 1, r22, p1))
    s = singular[...]
    squares = s * s
    sigma = add(squares + u0 * u0 + u1 * u1) / (count + 2)
    root = jnp.sqrt(sigma)
    d = squares / sigma
    v0 = u0 / root
    v1 = u1 / root

    half = POLES + 1
    row = rows_of((half, n))
    pole = jnp.zeros((half, n), F32)
    for j in range(POLES):
        pole = jnp.where(row == j, math.tan(math.pi * (j + 1) / SHIFTS) ** 2, pole)
    last = row == POLES
    pole = jnp.where(last, 1.0, pole)
    inverse = jnp.where(last, 1.0, 1.0 / (d + pole))
    weight = 2.0 * (1.0 + pole)
    w0 = inverse * v0
    w1 = inverse * v1
    last_one = last[:, 0:1]
    a = jnp.where(last_one, 1.0, 1.0 + add(w0 * v0))
    b = jnp.where(last_one, 0.0, add(w0 * v1))
    c = jnp.where(last_one, 1.0, 1.0 + add(w1 * v1))
    e = b / a
    c = c - b * e
    strength = jnp.where(last, 1.0, weight * pole)
    w1 = jnp.sqrt(strength / c) * (w1 - e * w0)
    w0 = jnp.sqrt(strength / a) * w0
    low_rank = jnp.concatenate([w0, w1], axis=0)
    gains = 1.0 + d + jnp.sum(jnp.where(last, 0.0, weight * d * inverse), axis=0, keepdims=True)
    square = (n, n)
    core = lax.dot_general(
        low_rank, low_rank, (((0,), (0,)), ((), ())),
        precision=lax.Precision.HIGHEST, preferred_element_type=F32,
    )
    core = core + jnp.where(rows_of(square) == lanes_of(square), gains, 0.0)
    core = core * (root * (1.0 / SHIFTS))
    t0 = jnp.where(lane == count, 1.0, -p0) / r11
    q_lane = jnp.where(lane == count + 1, 1.0, -p1)
    t1 = (q_lane - r12 * t0) / r22
    full = jnp.where(lanes_of(square) < count, core, 0.0)
    full = full + core[:, count : count + 1] * t0 + core[:, count + 1 : count + 2] * t1
    full = full[: count + 2, : count + 2]
    hi = full.astype(BF16)
    lo = (full - hi.astype(F32)).astype(BF16)
    both = jnp.concatenate([hi, lo], axis=0)

    blocks = block.shape[1] // 8
    size = count + 2
    copies = []
    for b in range(blocks):
        tiles = []
        for pair in range(4 * b, 4 * b + 4):
            top = upper[pair]
            r = jnp.dot(both, top, preferred_element_type=F32)
            r = r[:size] + r[size:] + jnp.dot(hi, lower[pair], preferred_element_type=F32)
            tiles.append(r[:, :n])
            tiles.append(r[:, n:])
        block[:, 8 * b : 8 * b + 8, :] = jnp.swapaxes(jnp.stack(tiles), 0, 1)
        copy = pltpu.make_async_copy(
            block.at[:, pl.ds(8 * b, 8), :], out.at[:, pl.ds(8 * b, 8), :], sems.at[b]
        )
        copy.start()
        copies.append(copy)
    for copy in copies:
        copy.wait()


def whole(n):
    return [pl.BlockSpec(memory_space=VMEM)] * n


SMEM_SPEC = pl.BlockSpec(memory_space=pltpu.SMEM)


def shaped(*shape, dtype=F32):
    return jax.ShapeDtypeStruct(shape, dtype)


def cost(flops, moved):
    return pl.CostEstimate(flops=flops, bytes_accessed=moved, transcendentals=0)


def limit(mib):
    return pltpu.CompilerParams(vmem_limit_bytes=mib * 2**20)


def ring(x, axes, by):
    count = lax.axis_size(axes)
    return lax.ppermute(x, axes, [(i, (i + by) % count) for i in range(count)])


def on_device(tracer, velocity, diffusivity, singular, basis_vectors):
    nz, nx, ny = tracer.shape
    count, window = basis_vectors.shape[:2]
    rows = window * nx
    basis = basis_vectors.reshape(count, rows, ny)
    rows_all = rows * ny * lax.axis_size(GX) * lax.axis_size(GY)
    chips = lax.axis_size(CHIPS)

    columns = shaped(3, nx, ny)
    own_left, own_right = pl.pallas_call(
        lambda *refs: pack_columns_kernel(nz, *refs),
        out_shape=(columns, columns), in_specs=whole(2), out_specs=tuple(whole(2)),
        compiler_params=limit(8), cost_estimate=cost(10**6, 2 * 2**20), name="columns",
    )(tracer, velocity)
    from_right = ring(own_left, GY, -1)
    from_left = ring(own_right, GY, 1)

    low_spec = pl.BlockSpec((4, nx, ny), lambda i: (0, 0, 0))
    high_spec = pl.BlockSpec((2, nx, ny), lambda i: (nz // 2 - 1, 0, 0))

    def full(*shape):
        return pl.BlockSpec(shape, lambda i: (0,) * len(shape))

    edge = shaped(24, ny)
    own_up, own_down = pl.pallas_call(
        pack_rows_kernel, grid=(1,),
        out_shape=(edge, edge),
        in_specs=[low_spec, high_spec, full(2, nx, ny), full(3, nx, ny), full(3, nx, ny)],
        out_specs=(full(24, ny), full(24, ny)),
        compiler_params=limit(8), cost_estimate=cost(10**4, 2**17), name="edges",
    )(tracer, tracer, velocity, from_left, from_right)
    from_down = ring(own_up, GX, -1)
    from_up = ring(own_down, GX, 1)

    low_now, high_now = tracer[:4], tracer[nz - 2 :]
    snaps, local, ghost_left, ghost_right = pl.pallas_call(
        window_kernel,
        out_shape=(shaped(2, rows, ny), shaped(2, ny), shaped(nx, nz), shaped(nx, nz)),
        in_specs=[SMEM_SPEC] + whole(13), out_specs=tuple(whole(4)),
        scratch_shapes=[VMEM((ny, ny), F32), VMEM((ny, ny), F32)],
        compiler_params=limit(10), cost_estimate=cost(10**7, 4 * 2**20), name="window",
    )(
        diffusivity, low_now, high_now, velocity, diffusivity.reshape(1, nz), own_left, own_right,
        from_left, from_right, own_up, own_down, from_up, from_down, basis,
    )

    pair = local + lax.ppermute(local, "c", [(0, 1), (1, 0)])
    sent = jnp.broadcast_to(pair[None], (chips, 2, ny))
    parts = lax.all_to_all(sent, CHIPS, 0, 0, tiled=True)

    up_rows = jnp.stack([tracer[:, 0], tracer[:, 1]])
    down_rows = jnp.stack([tracer[:, nx - 1], tracer[:, nx - 2]])
    up_rows, down_rows, _ = lax.optimization_barrier((up_rows, down_rows, from_up))
    bottom = ring(up_rows, GX, -1)
    top = ring(down_rows, GX, 1)

    tracer_next = pl.pallas_call(
        bulk_kernel,
        out_shape=shaped(nz, nx, ny),
        in_specs=[SMEM_SPEC] + whole(11), out_specs=whole(1)[0],
        scratch_shapes=[VMEM((nz, nx, ny), F32), VMEM((nz, ny), F32), VMEM((nz, ny), F32)],
        compiler_params=limit(16), cost_estimate=cost(10**8, 4 * 2**20), name="bulk",
    )(
        diffusivity, tracer, velocity, jnp.broadcast_to(diffusivity[:, None], (nz, ny)),
        from_left, from_right, ghost_left, ghost_right, from_up, from_down, top, bottom,
    )

    halves = shaped(rows // 2, count + 2, 2 * ny, dtype=BF16)
    upper, lower = pl.pallas_call(
        split_kernel,
        out_shape=(halves, halves), in_specs=whole(2), out_specs=tuple(whole(2)),
        compiler_params=limit(16), cost_estimate=cost(10**7, 6 * 2**20), name="split",
    )(basis, snaps)

    basis_next = pl.pallas_call(
        lambda *refs: core_kernel(rows_all, *refs),
        out_shape=shaped(count + 2, rows, ny),
        in_specs=whole(4), out_specs=pl.BlockSpec(memory_space=pl.ANY),
        scratch_shapes=[VMEM((count + 2, rows, ny), F32), pltpu.SemaphoreType.DMA((rows // 8,))],
        compiler_params=limit(16), cost_estimate=cost(10**8, 6 * 2**20), name="core",
    )(
        parts.reshape(chips // 4, 8, ny),
        jnp.pad(singular, (0, ny - count)).reshape(1, ny), upper, lower,
    )
    return tracer_next, basis_next.reshape(count + 2, window, nx, ny)


def solution(mesh):
    finer = Mesh(mesh.devices.reshape(8, 4, 4, 2), ("z", "y", "x", "c"))
    in_specs = (P(None, GX, GY), P(None, GX, GY), P(), P(), P(None, None, GX, GY))
    out_specs = (P(None, GX, GY), P(None, None, GX, GY))
    return jax.shard_map(
        on_device, mesh=finer, in_specs=in_specs, out_specs=out_specs, check_vma=False
    )
```

```python
import math

import jax
import jax.numpy as jnp
from jax import lax
from jax.experimental import pallas as pl
from jax.experimental.pallas import tpu as pltpu
from jax.sharding import Mesh
from jax.sharding import PartitionSpec as P


F32 = jnp.float32
BF16 = jnp.bfloat16
GX = ("z", "y")
GY = ("x", "c")
CHIPS = ("z", "y", "x")
ROOT_ITERS = 5
SHIFTS = 2**ROOT_ITERS
POLES = SHIFTS // 2 - 1
VMEM = pltpu.VMEM


def lanes_of(shape):
    return lax.broadcasted_iota(jnp.int32, shape, len(shape) - 1)


def rows_of(shape):
    return lax.broadcasted_iota(jnp.int32, shape, len(shape) - 2)


def step(c, xm, xp, ym, yp, zm, zp, d, vxp, vxn, vyp, vyn):
    spread = (xm + xp) + (ym + yp) + (zm + zp) - 6.0 * c
    carried = (vxp * (c - xm) + vxn * (xp - c)) + (vyp * (c - ym) + vyn * (yp - c))
    return c + d * spread - carried


def signed_parts(vx, vy):
    return jnp.maximum(vx, 0.0), jnp.minimum(vx, 0.0), jnp.maximum(vy, 0.0), jnp.minimum(vy, 0.0)


def before(c, ghost, axis):
    at = lax.broadcasted_iota(jnp.int32, c.shape, axis)
    return jnp.where(at == 0, ghost, pltpu.roll(c, 1, axis))


def after(c, ghost, axis):
    n = c.shape[axis]
    at = lax.broadcasted_iota(jnp.int32, c.shape, axis)
    return jnp.where(at == n - 1, ghost, pltpu.roll(c, n - 1, axis))


def pack_columns_kernel(
    chunks, tracer_hbm, velocity_hbm, left, right, near, top, bottom, tracer, velocity, sems
):
    nz, nx, ny = tracer.shape
    size = nz // chunks
    loads = [
        pltpu.make_async_copy(
            tracer_hbm.at[pl.ds(i * size, size)], tracer.at[pl.ds(i * size, size)], sems.at[i]
        )
        for i in range(chunks)
    ]
    loads.append(pltpu.make_async_copy(velocity_hbm, velocity, sems.at[chunks]))
    for load in loads:
        load.start()
    lane = lanes_of((nx, ny))

    def level(z, carry):
        a, b, y, w = carry
        r = pltpu.roll(tracer[z], z, 1)
        rel = (lane - z) & (ny - 1)
        a = jnp.where(rel == 0, r, a)
        b = jnp.where(rel == 1, r, b)
        y = jnp.where(rel == ny - 1, r, y)
        w = jnp.where(rel == ny - 2, r, w)
        return a, b, y, w

    carry = (jnp.zeros((nx, ny), F32),) * 4
    for i in range(chunks):
        loads[i].wait()
        carry = lax.fori_loop(i * size, (i + 1) * size, level, carry, unroll=8)
    a, b, y, w = carry
    left[0] = a
    left[1] = pltpu.roll(b, ny - 1, 1)
    right[0] = pltpu.roll(y, 1, 1)
    right[1] = pltpu.roll(w, 2, 1)
    loads[chunks].wait()
    vx, vy = velocity[0], velocity[1]
    left[2] = jnp.where(lane == 0, vx, pltpu.roll(vy, 1, 1))
    right[2] = jnp.where(lane == ny - 1, vx, pltpu.roll(vy, ny - 1, 1))
    near[0:2] = tracer[nz - 2 : nz]
    near[2:6] = tracer[0:4]
    for i in range(2):
        top[i] = tracer[:, i, :]
        bottom[i] = tracer[:, nx - 1 - i, :]


def pack_rows_kernel(near, velocity, from_left, from_right, up, down):
    nx, ny = near.shape[1:]
    for edge, inner, out in ((0, 1, up), (nx - 1, nx - 2, down)):
        for s in range(6):
            out[s : s + 1, :] = near[s, edge : edge + 1, :]
            out[8 + s : 9 + s, :] = near[s, inner : inner + 1, :]
        for s in (6, 7, 14, 15, 20, 21, 22, 23):
            out[s : s + 1, :] = jnp.zeros((1, ny), F32)
        out[16:17, :] = velocity[0, edge : edge + 1, :]
        out[17:18, :] = velocity[1, edge : edge + 1, :]
        out[18:19, :] = from_left[0, edge : edge + 1, :]
        out[19:20, :] = from_right[0, edge : edge + 1, :]


def window_kernel(
    diff, near, velocity, diff_row, own_left, own_right, from_left, from_right,
    own_up, own_down, from_up, from_down, basis,
    kept_hbm, sums, snaps, sides, q0, q1, sems,
):
    nz, nx, ny = diff.shape[0], near.shape[1], near.shape[2]
    count = basis.shape[0]
    dz = diff_row[...]
    for gin, inner, outer, corner, vx_at, vy_at, out in (
        (from_left, None, own_left, 18, ny - 1, ny - 2, sides.at[0:nx]),
        (from_right, own_right, None, 19, 0, 1, sides.at[nx : 2 * nx]),
    ):
        c = gin[0]
        ym = gin[1] if inner is None else inner[0]
        yp = gin[1] if outer is None else outer[0]
        vx = gin[2][:, vx_at : vx_at + 1]
        vy = gin[2][:, vy_at : vy_at + 1]
        parts = signed_parts(vx, vy)
        xm = before(c, from_up[corner : corner + 1, :], 0)
        xp = after(c, from_down[corner : corner + 1, :], 0)
        out[...] = step(c, xm, xp, ym, yp, pltpu.roll(c, 1, 1), pltpu.roll(c, nz - 1, 1), dz, *parts)

    sub = rows_of((8, ny))
    lane = lanes_of((8, ny))
    d_rows = jnp.where(sub == 2, diff[0], diff[1])
    ghost_rows = []
    for gin, own, top in ((from_up, own_up, True), (from_down, own_down, False)):
        c = gin[0:8, :]
        beyond, inside = gin[8:16, :], own[0:8, :]
        xm, xp = (beyond, inside) if top else (inside, beyond)
        west = jnp.where(sub == 2, gin[18:19, 0:1], gin[18:19, 1:2])
        east = jnp.where(sub == 2, gin[19:20, 0:1], gin[19:20, 1:2])
        parts = signed_parts(gin[16:17, :], gin[17:18, :])
        ghost_rows.append(
            step(c, xm, xp, before(c, west, 1), after(c, east, 1),
                 pltpu.roll(c, 1, 0), pltpu.roll(c, 7, 0), d_rows, *parts)
        )

    parts = signed_parts(velocity[0], velocity[1])
    u = [near[s] for s in range(6)]
    first = []
    for s in range(1, 5):
        z = (s - 2) % nz
        c = u[s]
        xm = before(c, from_up[s : s + 1, :], 0)
        xp = after(c, from_down[s : s + 1, :], 0)
        ym = before(c, from_left[0][:, z : z + 1], 1)
        yp = after(c, from_right[0][:, z : z + 1], 1)
        first.append(step(c, xm, xp, ym, yp, u[s - 1], u[s + 1], diff[z], *parts))
    for z in range(2):
        c = first[z + 1]
        snaps[0, z * nx : (z + 1) * nx, :] = c
        xm = before(c, ghost_rows[0][z + 2 : z + 3, :], 0)
        xp = after(c, ghost_rows[1][z + 2 : z + 3, :], 0)
        ym = before(c, sides[0:nx, z : z + 1], 1)
        yp = after(c, sides[nx : 2 * nx, z : z + 1], 1)
        snaps[1, z * nx : (z + 1) * nx, :] = step(
            c, xm, xp, ym, yp, first[z], first[z + 2], diff[z], *parts
        )

    rows = 2 * nx
    pieces = rows // 8
    sides[rows : rows + 8] = from_up[16:24, :]
    sides[rows + 8 : rows + 16] = from_down[16:24, :]
    keep = [
        pltpu.make_async_copy(ref, kept_hbm.at[pl.ds(at, ref.shape[0])], sems.at[i])
        for i, (ref, at) in enumerate(
            ((snaps.at[0], 0), (snaps.at[1], rows), (sides, 2 * rows))
        )
    ]
    for copy in keep:
        copy.start()

    def folded(a, b):
        total = a[0:8, :] * b[0:8, :]
        for i in range(1, pieces):
            total = total + a[8 * i : 8 * i + 8, :] * b[8 * i : 8 * i + 8, :]
        return jnp.sum(total, axis=0, keepdims=True)

    q0[...] = jnp.zeros_like(q0)
    q1[...] = jnp.zeros_like(q1)

    def product(k, carry):
        b = basis[k]
        q0[pl.ds(k, 1), :] = folded(b, snaps[0])
        q1[pl.ds(k, 1), :] = folded(b, snaps[1])
        return carry

    lax.fori_loop(0, count, product, 0, unroll=2)
    cross = folded(snaps[0], snaps[1])
    q0[count : count + 1, :] = folded(snaps[0], snaps[0])
    q0[count + 1 : count + 2, :] = cross
    q1[count : count + 1, :] = cross
    q1[count + 1 : count + 2, :] = folded(snaps[1], snaps[1])
    ones = jnp.ones((8, ny), F32)
    over_lanes = (((1,), (1,)), ((), ()))
    for m, q in enumerate((q0, q1)):
        line = lax.dot_general(
            ones, q[...], over_lanes, precision=lax.Precision.HIGHEST, preferred_element_type=F32
        )
        sums[m : m + 1, :] = line[0:1, :]
    for copy in keep:
        copy.wait()


def split(basis, snaps, upper, lower):
    _, rows, ny = basis.shape
    for b in range(rows // 8):
        part = slice(8 * b, 8 * b + 8)
        later = slice(rows + 8 * b, rows + 8 * b + 8)
        x = jnp.concatenate([basis[:, part, :], snaps[part, :][None], snaps[later, :][None]], axis=0)
        x = jnp.swapaxes(x, 0, 1)
        for i in range(8):
            pair, half = (8 * b + i) // 2, i % 2
            v = x[i]
            hi = v.astype(BF16)
            upper[pair, :, half * ny : (half + 1) * ny] = hi
            lower[pair, :, half * ny : (half + 1) * ny] = (v - hi.astype(F32)).astype(BF16)


def load_kernel(src, dst, sem):
    copy = pltpu.make_async_copy(src, dst, sem)
    copy.start()
    copy.wait()


def bulk_kernel(
    diff, tracer, basis, kept_hbm, top_hbm, bottom_hbm, velocity, diff_row, from_left, from_right,
    singular, out, upper, lower, line, now, then, vectors, kept, top, bottom, sems,
):
    nz, nx, ny = tracer.shape
    count, _ = basis.shape[:2]
    chunks = sems.shape[0] - 5
    size = nz // chunks
    tile = pl.ds(8, nx)
    loads = [
        pltpu.make_async_copy(src, dst, sems.at[chunks + i])
        for i, (src, dst) in enumerate((
            (tracer, now.at[:, tile, :]), (top_hbm, top), (bottom_hbm, bottom),
            (kept_hbm, kept), (basis, vectors),
        ))
    ]
    for load in loads:
        load.start()
    line[...] = jnp.zeros_like(line)
    line[0:1, :count] = singular[...]
    eye = rows_of((nz, nz)) == lanes_of((nz, nz))
    d_all = jnp.sum(jnp.where(eye, diff_row[...], 0.0), axis=1, keepdims=True)
    edges = ((top, 0, True, 6 * nx), (bottom, nx - 1, False, 6 * nx + 8))

    def ghost_rows():
        for bulk, own, is_top, at in edges:
            gin = kept[at : at + 8, :]
            c, beyond, inside = bulk[0], bulk[1], now[:, 8 + own, :]
            xm, xp = (beyond, inside) if is_top else (inside, beyond)
            west = jnp.sum(jnp.where(eye, gin[2:3, :], 0.0), axis=1, keepdims=True)
            east = jnp.sum(jnp.where(eye, gin[3:4, :], 0.0), axis=1, keepdims=True)
            parts = signed_parts(gin[0:1, :], gin[1:2, :])
            then[:, 7 if is_top else 8 + nx, :] = step(
                c, xm, xp, before(c, west, 1), after(c, east, 1),
                pltpu.roll(c, 1, 0), pltpu.roll(c, nz - 1, 0), d_all, *parts
            )

    xp_pull, xn_pull, yp_pull, yn_pull = signed_parts(velocity[0], velocity[1])
    stay = 1.0 - (xp_pull - xn_pull) - (yp_pull - yn_pull)
    xn_pull, yn_pull = -xn_pull, -yn_pull
    lane = lanes_of((nx, ny))
    is_even = (lane & 1) == 0

    def sweep(src, dst, col_left, col_right, after_chunk):
        shifted = pltpu.roll(col_right, nz - 1, 1)
        columns = (
            jnp.where(is_even, col_left, shifted), jnp.where(is_even, shifted, col_left),
        )

        def level(z, columns_now, zm, c):
            zp = src[(z + 1) & (nz - 1), tile, :]
            side = pltpu.roll(columns_now, (nz - z) & (nz - 1), 1)
            ym = jnp.where(lane == 0, side, pltpu.roll(c, 1, 1))
            yp = jnp.where(lane == ny - 1, side, pltpu.roll(c, ny - 1, 1))
            xm = src[z, pl.ds(7, nx), :]
            xp = src[z, pl.ds(9, nx), :]
            d = diff[z]
            moved = (xp_pull * xm + xn_pull * xp) + (yp_pull * ym + yn_pull * yp)
            spread = ((xm + xp) + (ym + yp)) + (zm + zp)
            dst[z, tile, :] = (c * (stay - 6.0 * d) + moved) + d * spread
            return c, zp

        def pair(i, carry):
            zm, c = carry
            zm, c = level(2 * i, columns[0], zm, c)
            return level(2 * i + 1, columns[1], zm, c)

        carry = (src[nz - 1, tile, :], src[0, tile, :])
        for k in range(chunks):
            carry = lax.fori_loop(k * size // 2, (k + 1) * size // 2, pair, carry, unroll=2)
            after_chunk(k)

    for load in loads[:4]:
        load.wait()
    now[:, 7, :] = top[0]
    now[:, 8 + nx, :] = bottom[0]
    sweep(now, then, from_left[0], from_right[0], lambda k: None)
    ghost_rows()
    stores = []

    def store(k):
        part = pl.ds(k * size, size)
        copy = pltpu.make_async_copy(now.at[part, tile, :], out.at[part], sems.at[k])
        copy.start()
        stores.append(copy)

    sweep(then, now, kept[4 * nx : 5 * nx, :], kept[5 * nx : 6 * nx, :], store)
    loads[4].wait()
    split(vectors, kept, upper, lower)
    for copy in stores:
        copy.wait()


def spread_kernel(mine, other, out):
    both = mine[...] + other[...]
    out[...] = jnp.broadcast_to(both[None], out.shape)


def core_kernel(rows_all, parts, singular, upper, lower, out, block, sems):
    count = out.shape[0] - 2
    n = parts.shape[2]
    total = jnp.sum(parts[...], axis=0)
    total = total + pltpu.roll(total, 2, 0)
    total = total + pltpu.roll(total, 4, 0)
    total = total * (1.0 / rows_all)
    lane = lanes_of((1, n))
    zero = jnp.zeros((1, n), F32)

    def add(x):
        return jnp.sum(x, axis=1, keepdims=True)

    def pick(x, at):
        return add(jnp.where(lane == at, x, zero))

    p0 = jnp.where(lane < count, total[0:1, :], zero)
    p1 = jnp.where(lane < count, total[1:2, :], zero)
    g00 = pick(total[0:1, :], count) - add(p0 * p0) + 1e-06
    g01 = pick(total[0:1, :], count + 1) - add(p0 * p1)
    g11 = pick(total[1:2, :], count + 1) - add(p1 * p1) + 1e-06
    r11 = jnp.sqrt(g00)
    r12 = g01 / r11
    r22 = jnp.sqrt(g11 - r12 * r12)
    u0 = jnp.where(lane == count, r11, p0)
    u1 = jnp.where(lane == count, r12, jnp.where(lane == count + 1, r22, p1))
    s = singular[0:1, :]
    squares = s * s
    sigma = add(squares + u0 * u0 + u1 * u1) / (count + 2)
    root = jnp.sqrt(sigma)
    d = squares / sigma
    v0 = u0 / root
    v1 = u1 / root

    half = POLES + 1
    row = rows_of((half, n))
    pole = jnp.zeros((half, n), F32)
    for j in range(POLES):
        pole = jnp.where(row == j, math.tan(math.pi * (j + 1) / SHIFTS) ** 2, pole)
    last = row == POLES
    pole = jnp.where(last, 1.0, pole)
    inverse = jnp.where(last, 1.0, 1.0 / (d + pole))
    weight = 2.0 * (1.0 + pole)
    w0 = inverse * v0
    w1 = inverse * v1
    last_one = last[:, 0:1]
    a = jnp.where(last_one, 1.0, 1.0 + add(w0 * v0))
    b = jnp.where(last_one, 0.0, add(w0 * v1))
    c = jnp.where(last_one, 1.0, 1.0 + add(w1 * v1))
    e = b / a
    c = c - b * e
    strength = jnp.where(last, 1.0, weight * pole)
    w1 = jnp.sqrt(strength / c) * (w1 - e * w0)
    w0 = jnp.sqrt(strength / a) * w0
    low_rank = jnp.concatenate([w0, w1], axis=0)
    gains = 1.0 + d + jnp.sum(jnp.where(last, 0.0, weight * d * inverse), axis=0, keepdims=True)
    square = (n, n)
    core = lax.dot_general(
        low_rank, low_rank, (((0,), (0,)), ((), ())),
        precision=lax.Precision.HIGHEST, preferred_element_type=F32,
    )
    core = core + jnp.where(rows_of(square) == lanes_of(square), gains, 0.0)
    core = core * (root * (1.0 / SHIFTS))
    t0 = jnp.where(lane == count, 1.0, -p0) / r11
    q_lane = jnp.where(lane == count + 1, 1.0, -p1)
    t1 = (q_lane - r12 * t0) / r22
    full = jnp.where(lanes_of(square) < count, core, 0.0)
    full = full + core[:, count : count + 1] * t0 + core[:, count + 1 : count + 2] * t1
    full = full[: count + 2, : count + 2]
    hi = full.astype(BF16)
    lo = (full - hi.astype(F32)).astype(BF16)
    both = jnp.concatenate([hi, lo], axis=0)

    blocks = block.shape[1] // 8
    size = count + 2
    copies = []
    for b in range(blocks):
        tiles = []
        for pair in range(4 * b, 4 * b + 4):
            top = upper[pair]
            r = jnp.dot(both, top, preferred_element_type=F32)
            r = r[:size] + r[size:] + jnp.dot(hi, lower[pair], preferred_element_type=F32)
            tiles.append(r[:, :n])
            tiles.append(r[:, n:])
        block[:, 8 * b : 8 * b + 8, :] = jnp.swapaxes(jnp.stack(tiles), 0, 1)
        copy = pltpu.make_async_copy(
            block.at[:, pl.ds(8 * b, 8), :], out.at[:, pl.ds(8 * b, 8), :], sems.at[b]
        )
        copy.start()
        copies.append(copy)
    for copy in copies:
        copy.wait()


def whole(n):
    return [pl.BlockSpec(memory_space=VMEM)] * n


SMEM_SPEC = pl.BlockSpec(memory_space=pltpu.SMEM)


def shaped(*shape, dtype=F32):
    return jax.ShapeDtypeStruct(shape, dtype)


def in_hbm(x):
    return pltpu.with_memory_space_constraint(x, pltpu.HBM)


def cost(flops, moved):
    return pl.CostEstimate(flops=flops, bytes_accessed=moved, transcendentals=0)


def limit(mib):
    return pltpu.CompilerParams(vmem_limit_bytes=mib * 2**20)


def ring(x, axes, by):
    count = lax.axis_size(axes)
    return lax.ppermute(x, axes, [(i, (i + by) % count) for i in range(count)])


def steps(tracer, velocity, diffusivity, singular, basis_vectors):
    nz, nx, ny = tracer.shape
    count, window = basis_vectors.shape[:2]
    rows = window * nx
    basis = basis_vectors.reshape(count, rows, ny)
    rows_all = rows * ny * lax.axis_size(GX) * lax.axis_size(GY)
    chips = lax.axis_size(CHIPS)
    diff_row = diffusivity.reshape(1, nz)

    columns = shaped(3, nx, ny)
    bulk_rows = shaped(2, nz, ny)
    own_left, own_right, near, top_rows, bottom_rows = pl.pallas_call(
        lambda *refs: pack_columns_kernel(4, *refs),
        out_shape=(columns, columns, shaped(6, nx, ny), bulk_rows, bulk_rows),
        in_specs=[pl.BlockSpec(memory_space=pltpu.HBM)] * 2, out_specs=tuple(whole(5)),
        scratch_shapes=[
            VMEM((nz, nx, ny), F32), VMEM((2, nx, ny), F32), pltpu.SemaphoreType.DMA((5,)),
        ],
        compiler_params=limit(8), cost_estimate=cost(10**6, 2 * 2**20), name="columns",
    )(in_hbm(tracer), in_hbm(velocity))
    from_right = ring(own_left, GY, -1)
    from_left = ring(own_right, GY, 1)
    vectors = pl.pallas_call(
        load_kernel, out_shape=shaped(count, rows, ny),
        in_specs=[pl.BlockSpec(memory_space=pltpu.HBM)], out_specs=whole(1)[0],
        scratch_shapes=[pltpu.SemaphoreType.DMA],
        compiler_params=limit(2), cost_estimate=cost(0, 6 * 2**20), name="load",
    )(in_hbm(basis))

    edge = shaped(24, ny)
    own_up, own_down = pl.pallas_call(
        pack_rows_kernel, out_shape=(edge, edge), in_specs=whole(4), out_specs=tuple(whole(2)),
        compiler_params=limit(4), cost_estimate=cost(10**4, 2**17), name="edges",
    )(near, velocity, from_left, from_right)
    from_down = ring(own_up, GX, -1)
    from_up = ring(own_down, GX, 1)
    top_sent, bottom_sent, _ = lax.optimization_barrier((top_rows, bottom_rows, own_up))
    bottom = ring(top_sent, GX, -1)
    top = ring(bottom_sent, GX, 1)

    kept, local = pl.pallas_call(
        window_kernel,
        out_shape=(pltpu.HBM((6 * nx + 16, ny), F32), shaped(2, ny)),
        in_specs=[SMEM_SPEC] + whole(12),
        out_specs=(pl.BlockSpec(memory_space=pltpu.HBM), *whole(1)),
        scratch_shapes=[
            VMEM((2, rows, ny), F32), VMEM((rows + 16, ny), F32), VMEM((ny, ny), F32),
            VMEM((ny, ny), F32), pltpu.SemaphoreType.DMA((3,)),
        ],
        compiler_params=limit(4), cost_estimate=cost(10**7, 4 * 2**20), name="window",
    )(
        diffusivity, near, velocity, diff_row, own_left, own_right,
        from_left, from_right, own_up, own_down, from_up, from_down, vectors,
    )

    other = lax.ppermute(local, "c", [(0, 1), (1, 0)])
    sent = pl.pallas_call(
        spread_kernel, out_shape=shaped(chips, 2, ny), in_specs=whole(2), out_specs=whole(1)[0],
        compiler_params=limit(4), cost_estimate=cost(10**4, 2**17), name="spread",
    )(local, other)
    parts = lax.all_to_all(sent, CHIPS, 0, 0, tiled=True)

    hbm_space, any_space = (pl.BlockSpec(memory_space=m) for m in (pltpu.HBM, pl.ANY))
    halves = shaped(rows // 2, count + 2, 2 * ny, dtype=BF16)
    padded = VMEM((nz, nx + 16, ny), F32)
    tracer_next, upper, lower, line = pl.pallas_call(
        bulk_kernel,
        out_shape=(shaped(nz, nx, ny), halves, halves, shaped(8, ny)),
        in_specs=[SMEM_SPEC] + [hbm_space] * 3 + [any_space] * 2 + whole(5),
        out_specs=(any_space, *whole(3)),
        scratch_shapes=[
            padded, padded, VMEM((count, rows, ny), F32), VMEM((6 * nx + 16, ny), F32),
            VMEM((2, nz, ny), F32), VMEM((2, nz, ny), F32), pltpu.SemaphoreType.DMA((9,)),
        ],
        compiler_params=limit(16), cost_estimate=cost(10**8, 10 * 2**20), name="bulk",
    )(
        diffusivity, in_hbm(tracer), in_hbm(basis), in_hbm(kept), top, bottom,
        velocity, diff_row, from_left, from_right, singular.reshape(1, count),
    )

    basis_next = pl.pallas_call(
        lambda *refs: core_kernel(rows_all, *refs),
        out_shape=shaped(count + 2, rows, ny),
        in_specs=whole(4), out_specs=pl.BlockSpec(memory_space=pl.ANY),
        scratch_shapes=[
            VMEM((count + 2, rows, ny), F32),
            pltpu.SemaphoreType.DMA((rows // 8,)),
        ],
        compiler_params=limit(16), cost_estimate=cost(10**8, 6 * 2**20), name="core",
    )(
        parts.reshape(chips // 4, 8, ny), line, upper, lower,
    )
    return tracer_next, basis_next.reshape(count + 2, window, nx, ny)


def solution(mesh):
    finer = Mesh(mesh.devices.reshape(8, 4, 4, 2), ("z", "y", "x", "c"))
    in_specs = (P(None, GX, GY), P(None, GX, GY), P(), P(), P(None, None, GX, GY))
    out_specs = (P(None, GX, GY), P(None, None, GX, GY))
    return jax.shard_map(steps, mesh=finer, in_specs=in_specs, out_specs=out_specs, check_vma=False)
```

```python
import math

import jax
import jax.numpy as jnp
from jax import lax
from jax.experimental import pallas as pl
from jax.experimental.pallas import tpu as pltpu
from jax.sharding import Mesh
from jax.sharding import PartitionSpec as P


F32 = jnp.float32
BF16 = jnp.bfloat16
GX = ("z", "y")
GY = ("x", "c")
CHIPS = ("z", "y", "x")
ROOT_ITERS = 5
SHIFTS = 2**ROOT_ITERS
POLES = SHIFTS // 2 - 1
VMEM = pltpu.VMEM


def lanes_of(shape):
    return lax.broadcasted_iota(jnp.int32, shape, len(shape) - 1)


def rows_of(shape):
    return lax.broadcasted_iota(jnp.int32, shape, len(shape) - 2)


def step(c, xm, xp, ym, yp, zm, zp, d, vxp, vxn, vyp, vyn):
    spread = (xm + xp) + (ym + yp) + (zm + zp) - 6.0 * c
    carried = (vxp * (c - xm) + vxn * (xp - c)) + (vyp * (c - ym) + vyn * (yp - c))
    return c + d * spread - carried


def signed_parts(vx, vy):
    return jnp.maximum(vx, 0.0), jnp.minimum(vx, 0.0), jnp.maximum(vy, 0.0), jnp.minimum(vy, 0.0)


def before(c, ghost, axis):
    at = lax.broadcasted_iota(jnp.int32, c.shape, axis)
    return jnp.where(at == 0, ghost, pltpu.roll(c, 1, axis))


def after(c, ghost, axis):
    n = c.shape[axis]
    at = lax.broadcasted_iota(jnp.int32, c.shape, axis)
    return jnp.where(at == n - 1, ghost, pltpu.roll(c, n - 1, axis))


def gx_is_even():
    return lax.axis_index("y") % 2 == 0


def gy_is_even():
    return lax.axis_index("c") == 0


def to_pairs(even, up, down):
    return jnp.where(even, down, up), jnp.where(even, up, down)


def from_pairs(even, near, far):
    return jnp.where(even, far, near), jnp.where(even, near, far)


def pack_columns_kernel(
    chunks, tracer_hbm, velocity_hbm, near, far, window, rows_near, rows_far, mine,
    tracer, velocity, sems,
):
    nx, ny = velocity.shape[1:]
    nz = tracer.shape[0] // nx
    size = nz // chunks
    loads = [
        pltpu.make_async_copy(
            tracer_hbm.at[pl.ds(i * size * nx, size * nx)],
            tracer.at[pl.ds(i * size * nx, size * nx)], sems.at[i],
        )
        for i in range(chunks)
    ]
    loads.append(pltpu.make_async_copy(velocity_hbm, velocity, sems.at[chunks]))
    for load in loads:
        load.start()
    lane = lanes_of((nx, ny))

    def level(z, carry):
        a, b, y, w = carry
        r = pltpu.roll(tracer[pl.ds(pl.multiple_of(z * nx, nx), nx), :], z, 1)
        rel = (lane - z) & (ny - 1)
        a = jnp.where(rel == 0, r, a)
        b = jnp.where(rel == 1, r, b)
        y = jnp.where(rel == ny - 1, r, y)
        w = jnp.where(rel == ny - 2, r, w)
        return a, b, y, w

    carry = (jnp.zeros((nx, ny), F32),) * 4
    for i in range(chunks):
        loads[i].wait()
        carry = lax.fori_loop(i * size, (i + 1) * size, level, carry, unroll=8)
    a, b, y, w = carry
    loads[chunks].wait()
    vx, vy = velocity[0], velocity[1]
    left = (a, pltpu.roll(b, ny - 1, 1), jnp.where(lane == 0, vx, pltpu.roll(vy, 1, 1)))
    right = (
        pltpu.roll(y, 1, 1), pltpu.roll(w, 2, 1),
        jnp.where(lane == ny - 1, vx, pltpu.roll(vy, ny - 1, 1)),
    )
    even = gy_is_even()
    for i in range(3):
        near[i], far[i] = to_pairs(even, left[i], right[i])
    mine[0], mine[1] = left[0], right[0]
    window[0 : 2 * nx] = tracer[(nz - 2) * nx : nz * nx]
    window[2 * nx : 6 * nx] = tracer[0 : 4 * nx]
    even = gx_is_even()
    for i in range(2):
        top = tracer[pl.ds(i, nz, stride=nx), :]
        bottom = tracer[pl.ds(nx - 1 - i, nz, stride=nx), :]
        rows_near[i], rows_far[i] = to_pairs(even, top, bottom)


def pack_rows_kernel(window, velocity, sides_near, sides_far, near, far, up, down):
    nx, ny = velocity.shape[1:]
    from_left, from_right = from_pairs(gy_is_even(), sides_near[0], sides_far[0])
    for edge, inner, out in ((0, 1, up), (nx - 1, nx - 2, down)):
        for s in range(6):
            out[s : s + 1, :] = window[s * nx + edge : s * nx + edge + 1, :]
            out[8 + s : 9 + s, :] = window[s * nx + inner : s * nx + inner + 1, :]
        for s in (6, 7, 14, 15, 20, 21, 22, 23):
            out[s : s + 1, :] = jnp.zeros((1, ny), F32)
        out[16:17, :] = velocity[0, edge : edge + 1, :]
        out[17:18, :] = velocity[1, edge : edge + 1, :]
        out[18:19, :] = from_left[edge : edge + 1, :]
        out[19:20, :] = from_right[edge : edge + 1, :]
    near[...], far[...] = to_pairs(gx_is_even(), up[...], down[...])


def window_kernel(
    diff, near, velocity, diff_row, mine, sides_near, sides_far,
    own_up, own_down, rows_near, rows_far, basis,
    kept_hbm, sums, snaps, sides, q0, q1, sems,
):
    nz, nx, ny = diff.shape[0], velocity.shape[1], velocity.shape[2]
    count = basis.shape[0]
    dz = diff_row[...]
    even = gy_is_even()
    pairs = [from_pairs(even, sides_near[i], sides_far[i]) for i in range(3)]
    from_left, from_right = [p[0] for p in pairs], [p[1] for p in pairs]
    from_up, from_down = from_pairs(gx_is_even(), rows_near[...], rows_far[...])
    for gin, inner, outer, corner, vx_at, vy_at, out in (
        (from_left, None, mine[0], 18, ny - 1, ny - 2, sides.at[0:nx]),
        (from_right, mine[1], None, 19, 0, 1, sides.at[nx : 2 * nx]),
    ):
        c = gin[0]
        ym = gin[1] if inner is None else inner
        yp = gin[1] if outer is None else outer
        vx = gin[2][:, vx_at : vx_at + 1]
        vy = gin[2][:, vy_at : vy_at + 1]
        parts = signed_parts(vx, vy)
        xm = before(c, from_up[corner : corner + 1, :], 0)
        xp = after(c, from_down[corner : corner + 1, :], 0)
        out[...] = step(c, xm, xp, ym, yp, pltpu.roll(c, 1, 1), pltpu.roll(c, nz - 1, 1), dz, *parts)

    sub = rows_of((8, ny))
    lane = lanes_of((8, ny))
    d_rows = jnp.where(sub == 2, diff[0], diff[1])
    ghost_rows = []
    for gin, own, top in ((from_up, own_up, True), (from_down, own_down, False)):
        c = gin[0:8, :]
        beyond, inside = gin[8:16, :], own[0:8, :]
        xm, xp = (beyond, inside) if top else (inside, beyond)
        west = jnp.where(sub == 2, gin[18:19, 0:1], gin[18:19, 1:2])
        east = jnp.where(sub == 2, gin[19:20, 0:1], gin[19:20, 1:2])
        parts = signed_parts(gin[16:17, :], gin[17:18, :])
        ghost_rows.append(
            step(c, xm, xp, before(c, west, 1), after(c, east, 1),
                 pltpu.roll(c, 1, 0), pltpu.roll(c, 7, 0), d_rows, *parts)
        )

    parts = signed_parts(velocity[0], velocity[1])
    u = [near[s * nx : (s + 1) * nx] for s in range(6)]
    first = []
    for s in range(1, 5):
        z = (s - 2) % nz
        c = u[s]
        xm = before(c, from_up[s : s + 1, :], 0)
        xp = after(c, from_down[s : s + 1, :], 0)
        ym = before(c, from_left[0][:, z : z + 1], 1)
        yp = after(c, from_right[0][:, z : z + 1], 1)
        first.append(step(c, xm, xp, ym, yp, u[s - 1], u[s + 1], diff[z], *parts))
    for z in range(2):
        c = first[z + 1]
        snaps[0, z * nx : (z + 1) * nx, :] = c
        xm = before(c, ghost_rows[0][z + 2 : z + 3, :], 0)
        xp = after(c, ghost_rows[1][z + 2 : z + 3, :], 0)
        ym = before(c, sides[0:nx, z : z + 1], 1)
        yp = after(c, sides[nx : 2 * nx, z : z + 1], 1)
        snaps[1, z * nx : (z + 1) * nx, :] = step(
            c, xm, xp, ym, yp, first[z], first[z + 2], diff[z], *parts
        )

    rows = 2 * nx
    pieces = rows // 8
    sides[rows : rows + 8] = from_up[16:24, :]
    sides[rows + 8 : rows + 16] = from_down[16:24, :]
    keep = [
        pltpu.make_async_copy(ref, kept_hbm.at[pl.ds(at, ref.shape[0])], sems.at[i])
        for i, (ref, at) in enumerate(
            ((snaps.at[0], 0), (snaps.at[1], rows), (sides, 2 * rows))
        )
    ]
    for copy in keep:
        copy.start()

    def folded(a, b):
        total = a[0:8, :] * b[0:8, :]
        for i in range(1, pieces):
            total = total + a[8 * i : 8 * i + 8, :] * b[8 * i : 8 * i + 8, :]
        return total

    def group(vectors, start, size):
        for m, q in enumerate((q0, q1)):
            lines = jnp.stack([folded(v, snaps[m]) for v in vectors])
            q[pl.ds(start, size), :] = jnp.sum(lines, axis=1)

    def eight(i, carry):
        at = pl.multiple_of(8 * i, 8)
        group([basis[at + j] for j in range(8)], at, 8)
        return carry

    full = count // 8 * 8
    lax.fori_loop(0, count // 8, eight, 0)
    group([basis[k] for k in range(full, count)] + [snaps[0], snaps[1]], full, count + 2 - full)
    for q in (q0, q1):
        q[count + 2 :] = jnp.zeros((ny - count - 2, ny), F32)
    ones = jnp.ones((8, ny), F32)
    over_lanes = (((1,), (1,)), ((), ()))
    for m, q in enumerate((q0, q1)):
        line = lax.dot_general(
            ones, q[...], over_lanes, precision=lax.Precision.HIGHEST, preferred_element_type=F32
        )
        sums[m : m + 1, :] = line[0:1, :]
    for copy in keep:
        copy.wait()


def split(basis, snaps, upper, lower):
    rows, ny = snaps.shape[0] // 2, snaps.shape[1]
    count = basis.shape[0] // rows
    for r in range(rows):
        pair, half = r // 2, r % 2
        lanes = slice(half * ny, (half + 1) * ny)
        v = jnp.concatenate(
            [basis[pl.ds(r, count, stride=rows), :], snaps[pl.ds(r, 2, stride=rows), :]], axis=0
        )
        hi = v.astype(BF16)
        upper[pair, :, lanes] = hi
        lower[pair, :, lanes] = (v - hi.astype(F32)).astype(BF16)


def load_kernel(src, dst, sem):
    copy = pltpu.make_async_copy(src, dst, sem)
    copy.start()
    copy.wait()


def sweep(diff, velocity, src, dst, col_left, col_right, chunks, after_chunk):
    nx, ny = velocity.shape[1:]
    pitch = nx + 16
    nz = src.shape[0] // pitch
    size = nz // chunks
    vx, vy = velocity[0], velocity[1]
    east, north = vx > 0.0, vy > 0.0
    speed_x, speed_y = jnp.abs(vx), jnp.abs(vy)
    stay = 1.0 - speed_x - speed_y
    lane = lanes_of((nx, ny))
    first, last = lane == 0, lane == ny - 1
    is_even = (lane & 1) == 0
    shifted = pltpu.roll(col_right, nz - 1, 1)
    columns = (jnp.where(is_even, col_left, shifted), jnp.where(is_even, shifted, col_left))

    def rows_at(z, by):
        return pl.ds(pl.multiple_of(z * pitch, 8) + 8 + by, nx)

    def turned(c, z, which):
        side = pltpu.roll(columns[which], (nz - z) & (nz - 1), 1)
        return pltpu.roll(c, 1, 1), pltpu.roll(c, ny - 1, 1), side

    def level(z, next_parity, state):
        zm, c, south, north_side, side = state
        zn = (z + 1) & (nz - 1)
        zp = src[rows_at(zn, 0), :]
        ahead = turned(zp, zn, next_parity)
        ym = jnp.where(first, side, south)
        yp = jnp.where(last, side, north_side)
        xm = src[rows_at(z, -1), :]
        xp = src[rows_at(z, 1), :]
        d = diff[z]
        moved = speed_x * jnp.where(east, xm, xp) + speed_y * jnp.where(north, ym, yp)
        spread = ((xm + xp) + (ym + yp)) + (zm + zp)
        dst[rows_at(z, 0), :] = (c * (stay - 6.0 * d) + moved) + d * spread
        return (c, zp, *ahead)

    def pair(i, state):
        return level(2 * i + 1, 0, level(2 * i, 1, state))

    c = src[rows_at(0, 0), :]
    state = (src[rows_at(nz - 1, 0), :], c, *turned(c, 0, 0))
    for k in range(chunks):
        state = lax.fori_loop(k * size // 2, (k + 1) * size // 2, pair, state, unroll=2)
        after_chunk(k)


def chunk_stores(src, out, sems, chunks, nx):
    pitch = nx + 16
    nz = src.shape[0] // pitch
    size = nz // chunks
    view = src.reshape(nz, pitch, src.shape[1])
    stores = []

    def store(k):
        part = pl.ds(k * size, size)
        copy = pltpu.make_async_copy(view.at[part, pl.ds(8, nx), :], out.at[part], sems.at[k])
        copy.start()
        stores.append(copy)

    return store, stores


def first_kernel(
    chunks, diff, tracer, velocity, sides_near, sides_far, rows_near, rows_far,
    sent_near, sent_far, out, rows_out, now, then, rows, sems,
):
    nz, nx, ny = tracer.shape
    pitch = nx + 16
    view = now.reshape(nz, pitch, ny)
    load = pltpu.make_async_copy(tracer, view.at[:, pl.ds(8, nx), :], sems.at[chunks])
    load.start()
    even = gx_is_even()
    for i in range(2):
        rows[i], rows[2 + i] = from_pairs(even, rows_near[i], rows_far[i])
    rows[4] = jnp.where(even, sent_far[0], sent_near[0])
    rows[5] = jnp.where(even, sent_near[0], sent_far[0])
    keep = pltpu.make_async_copy(rows, rows_out, sems.at[chunks + 1])
    keep.start()
    now[pl.ds(7, nz, stride=pitch), :] = rows[0]
    now[pl.ds(8 + nx, nz, stride=pitch), :] = rows[2]
    from_left, from_right = from_pairs(gy_is_even(), sides_near[0], sides_far[0])
    load.wait()
    store, stores = chunk_stores(then, out, sems, chunks, nx)
    sweep(diff, velocity, now, then, from_left, from_right, chunks, store)
    keep.wait()
    for copy in stores:
        copy.wait()


def second_kernel(
    chunks, diff, first, basis, kept_hbm, rows_hbm, velocity, diff_row, singular,
    out, upper, lower, line, now, then, vectors, kept, rows, sems,
):
    nz, nx, ny = first.shape
    pitch = nx + 16
    count = singular.shape[1]
    view = now.reshape(nz, pitch, ny)
    loads = [
        pltpu.make_async_copy(src, dst, sems.at[chunks + i])
        for i, (src, dst) in enumerate((
            (first, view.at[:, pl.ds(8, nx), :]), (kept_hbm, kept), (rows_hbm, rows),
            (basis, vectors),
        ))
    ]
    for load in loads:
        load.start()
    line[...] = jnp.zeros_like(line)
    line[0:1, :count] = singular[...]
    eye = rows_of((nz, nz)) == lanes_of((nz, nz))
    d_all = jnp.sum(jnp.where(eye, diff_row[...], 0.0), axis=1, keepdims=True)
    for load in loads[1:3]:
        load.wait()
    for i, own, is_top, at in ((0, 4, True, 6 * nx), (2, 5, False, 6 * nx + 8)):
        gin = kept[at : at + 8, :]
        c, beyond, inside = rows[i], rows[i + 1], rows[own]
        xm, xp = (beyond, inside) if is_top else (inside, beyond)
        west = jnp.sum(jnp.where(eye, gin[2:3, :], 0.0), axis=1, keepdims=True)
        east = jnp.sum(jnp.where(eye, gin[3:4, :], 0.0), axis=1, keepdims=True)
        parts = signed_parts(gin[0:1, :], gin[1:2, :])
        now[pl.ds(7 if is_top else 8 + nx, nz, stride=pitch), :] = step(
            c, xm, xp, before(c, west, 1), after(c, east, 1),
            pltpu.roll(c, 1, 0), pltpu.roll(c, nz - 1, 0), d_all, *parts
        )
    loads[0].wait()
    store, stores = chunk_stores(then, out, sems, chunks, nx)
    sweep(
        diff, velocity, now, then, kept[4 * nx : 5 * nx, :], kept[5 * nx : 6 * nx, :], chunks, store
    )
    loads[3].wait()
    split(vectors, kept.at[0 : 4 * nx], upper, lower)
    for copy in stores:
        copy.wait()


def spread_kernel(mine, other, out):
    both = mine[...] + other[...]
    out[...] = jnp.broadcast_to(both[None], out.shape)


def core_kernel(rows_all, parts, singular, upper, lower, out, block, sems):
    count = out.shape[0] - 2
    n = parts.shape[2]
    total = jnp.sum(parts[...], axis=0)
    total = total + pltpu.roll(total, 2, 0)
    total = total + pltpu.roll(total, 4, 0)
    total = total * (1.0 / rows_all)
    lane = lanes_of((1, n))
    zero = jnp.zeros((1, n), F32)

    def add(x):
        return jnp.sum(x, axis=1, keepdims=True)

    def pick(x, at):
        return add(jnp.where(lane == at, x, zero))

    p0 = jnp.where(lane < count, total[0:1, :], zero)
    p1 = jnp.where(lane < count, total[1:2, :], zero)
    g00 = pick(total[0:1, :], count) - add(p0 * p0) + 1e-06
    g01 = pick(total[0:1, :], count + 1) - add(p0 * p1)
    g11 = pick(total[1:2, :], count + 1) - add(p1 * p1) + 1e-06
    r11 = jnp.sqrt(g00)
    r12 = g01 / r11
    r22 = jnp.sqrt(g11 - r12 * r12)
    u0 = jnp.where(lane == count, r11, p0)
    u1 = jnp.where(lane == count, r12, jnp.where(lane == count + 1, r22, p1))
    s = singular[0:1, :]
    squares = s * s
    sigma = add(squares + u0 * u0 + u1 * u1) / (count + 2)
    root = jnp.sqrt(sigma)
    d = squares / sigma
    v0 = u0 / root
    v1 = u1 / root

    half = POLES + 1
    row = rows_of((half, n))
    pole = jnp.zeros((half, n), F32)
    for j in range(POLES):
        pole = jnp.where(row == j, math.tan(math.pi * (j + 1) / SHIFTS) ** 2, pole)
    last = row == POLES
    pole = jnp.where(last, 1.0, pole)
    inverse = jnp.where(last, 1.0, 1.0 / (d + pole))
    weight = 2.0 * (1.0 + pole)
    w0 = inverse * v0
    w1 = inverse * v1
    last_one = last[:, 0:1]
    a = jnp.where(last_one, 1.0, 1.0 + add(w0 * v0))
    b = jnp.where(last_one, 0.0, add(w0 * v1))
    c = jnp.where(last_one, 1.0, 1.0 + add(w1 * v1))
    e = b / a
    c = c - b * e
    strength = jnp.where(last, 1.0, weight * pole)
    w1 = jnp.sqrt(strength / c) * (w1 - e * w0)
    w0 = jnp.sqrt(strength / a) * w0
    low_rank = jnp.concatenate([w0, w1], axis=0)
    gains = 1.0 + d + jnp.sum(jnp.where(last, 0.0, weight * d * inverse), axis=0, keepdims=True)
    square = (n, n)
    core = lax.dot_general(
        low_rank, low_rank, (((0,), (0,)), ((), ())),
        precision=lax.Precision.HIGHEST, preferred_element_type=F32,
    )
    core = core + jnp.where(rows_of(square) == lanes_of(square), gains, 0.0)
    core = core * (root * (1.0 / SHIFTS))
    t0 = jnp.where(lane == count, 1.0, -p0) / r11
    q_lane = jnp.where(lane == count + 1, 1.0, -p1)
    t1 = (q_lane - r12 * t0) / r22
    full = jnp.where(lanes_of(square) < count, core, 0.0)
    full = full + core[:, count : count + 1] * t0 + core[:, count + 1 : count + 2] * t1
    full = full[: count + 2, : count + 2]
    hi = full.astype(BF16)
    lo = (full - hi.astype(F32)).astype(BF16)
    both = jnp.concatenate([hi, lo], axis=0)

    size = count + 2
    rows = out.shape[1]
    view = block.reshape(size, rows, n)
    copies = []
    for b in range(rows // 8):
        for pair in range(4 * b, 4 * b + 4):
            r = jnp.dot(both, upper[pair], preferred_element_type=F32)
            r = r[:size] + r[size:] + jnp.dot(hi, lower[pair], preferred_element_type=F32)
            for half in range(2):
                at = pl.ds(2 * pair + half, size, stride=rows)
                block[at, :] = r[:, half * n : (half + 1) * n]
        part = pl.ds(8 * b, 8)
        copy = pltpu.make_async_copy(view.at[:, part, :], out.at[:, part, :], sems.at[b])
        copy.start()
        copies.append(copy)
    for copy in copies:
        copy.wait()


def whole(n):
    return [pl.BlockSpec(memory_space=VMEM)] * n


SMEM_SPEC = pl.BlockSpec(memory_space=pltpu.SMEM)


def shaped(*shape, dtype=F32):
    return jax.ShapeDtypeStruct(shape, dtype)


def in_hbm(x):
    return pltpu.with_memory_space_constraint(x, pltpu.HBM)


def cost(flops, moved):
    return pl.CostEstimate(flops=flops, bytes_accessed=moved, transcendentals=0)


def limit(mib):
    return pltpu.CompilerParams(vmem_limit_bytes=mib * 2**20)


def swap(x, axes, far):
    count = lax.axis_size(axes)
    shift = 1 if far else 0
    pairs = [((i + shift) % count, ((i ^ 1) + shift) % count) for i in range(count)]
    return lax.ppermute(x, axes, pairs)


def steps(tracer, velocity, diffusivity, singular, basis_vectors):
    nz, nx, ny = tracer.shape
    count, window = basis_vectors.shape[:2]
    rows = window * nx
    basis = basis_vectors.reshape(count, rows, ny)
    rows_all = rows * ny * lax.axis_size(GX) * lax.axis_size(GY)
    chips = lax.axis_size(CHIPS)
    diff_row = diffusivity.reshape(1, nz)

    columns = shaped(3, nx, ny)
    bulk_rows = shaped(2, nz, ny)
    hbm_space, any_space = (pl.BlockSpec(memory_space=m) for m in (pltpu.HBM, pl.ANY))
    columns_near, columns_far, near, sent_near, sent_far, mine = pl.pallas_call(
        lambda *refs: pack_columns_kernel(4, *refs),
        out_shape=(columns, columns, shaped(6 * nx, ny), bulk_rows, bulk_rows, shaped(2, nx, ny)),
        in_specs=[hbm_space] * 2, out_specs=tuple(whole(6)),
        scratch_shapes=[
            VMEM((nz * nx, ny), F32), VMEM((2, nx, ny), F32), pltpu.SemaphoreType.DMA((5,)),
        ],
        compiler_params=limit(4), cost_estimate=cost(10**6, 2 * 2**20), name="columns",
    )(in_hbm(tracer.reshape(nz * nx, ny)), in_hbm(velocity))
    sides_far = swap(columns_far, GY, True)
    sides_near = swap(columns_near, GY, False)
    rows_far = swap(sent_far, GX, True)
    rows_near = swap(sent_near, GX, False)

    edge = shaped(24, ny)
    edges_near, edges_far, own_up, own_down = pl.pallas_call(
        pack_rows_kernel, out_shape=(edge,) * 4, in_specs=whole(4), out_specs=tuple(whole(4)),
        compiler_params=limit(2), cost_estimate=cost(10**4, 2**17), name="edges",
    )(near, velocity, sides_near, sides_far)
    window_far = swap(edges_far, GX, True)
    window_near = swap(edges_near, GX, False)

    vectors = pl.pallas_call(
        load_kernel, out_shape=shaped(count, rows, ny),
        in_specs=[hbm_space], out_specs=whole(1)[0],
        scratch_shapes=[pltpu.SemaphoreType.DMA],
        compiler_params=limit(2), cost_estimate=cost(0, 6 * 2**20), name="load",
    )(in_hbm(basis))
    padded = VMEM((nz * (nx + 16), ny), F32)
    first, rows_kept = pl.pallas_call(
        lambda *refs: first_kernel(4, *refs),
        out_shape=(pltpu.HBM((nz, nx, ny), F32), pltpu.HBM((6, nz, ny), F32)),
        in_specs=[SMEM_SPEC, hbm_space] + whole(7), out_specs=(hbm_space, hbm_space),
        scratch_shapes=[padded, padded, VMEM((6, nz, ny), F32), pltpu.SemaphoreType.DMA((6,))],
        compiler_params=limit(8), cost_estimate=cost(10**8, 4 * 2**20), name="first",
    )(
        diffusivity, in_hbm(tracer), velocity, sides_near, sides_far, rows_near, rows_far,
        sent_near, sent_far,
    )

    kept, local = pl.pallas_call(
        window_kernel,
        out_shape=(pltpu.HBM((6 * nx + 16, ny), F32), shaped(2, ny)),
        in_specs=[SMEM_SPEC] + whole(11), out_specs=(hbm_space, *whole(1)),
        scratch_shapes=[
            VMEM((2, rows, ny), F32), VMEM((rows + 16, ny), F32), VMEM((ny, ny), F32),
            VMEM((ny, ny), F32), pltpu.SemaphoreType.DMA((3,)),
        ],
        compiler_params=limit(4), cost_estimate=cost(10**7, 4 * 2**20), name="window",
    )(
        diffusivity, near, velocity, diff_row, mine, sides_near, sides_far,
        own_up, own_down, window_near, window_far, vectors,
    )

    other = lax.ppermute(local, "c", [(0, 1), (1, 0)])
    sent = pl.pallas_call(
        spread_kernel, out_shape=shaped(chips, 2, ny), in_specs=whole(2), out_specs=whole(1)[0],
        compiler_params=limit(4), cost_estimate=cost(10**4, 2**17), name="spread",
    )(local, other)
    parts = lax.all_to_all(sent, CHIPS, 0, 0, tiled=True)

    halves = shaped(rows // 2, count + 2, 2 * ny, dtype=BF16)
    tracer_next, upper, lower, line = pl.pallas_call(
        lambda *refs: second_kernel(4, *refs),
        out_shape=(shaped(nz, nx, ny), halves, halves, shaped(8, ny)),
        in_specs=[SMEM_SPEC] + [hbm_space] * 4 + whole(3), out_specs=(any_space, *whole(3)),
        scratch_shapes=[
            padded, padded, VMEM((count * rows, ny), F32), VMEM((6 * nx + 16, ny), F32),
            VMEM((6, nz, ny), F32), pltpu.SemaphoreType.DMA((8,)),
        ],
        compiler_params=limit(12), cost_estimate=cost(10**8, 10 * 2**20), name="second",
    )(
        diffusivity, in_hbm(first), in_hbm(basis_vectors.reshape(count * rows, ny)), in_hbm(kept),
        in_hbm(rows_kept), velocity, diff_row, singular.reshape(1, count),
    )

    basis_next = pl.pallas_call(
        lambda *refs: core_kernel(rows_all, *refs),
        out_shape=shaped(count + 2, rows, ny),
        in_specs=whole(4), out_specs=pl.BlockSpec(memory_space=pl.ANY),
        scratch_shapes=[
            VMEM(((count + 2) * rows, ny), F32),
            pltpu.SemaphoreType.DMA((rows // 8,)),
        ],
        compiler_params=limit(16), cost_estimate=cost(10**8, 6 * 2**20), name="core",
    )(
        parts.reshape(chips // 4, 8, ny), line, upper, lower,
    )
    return tracer_next, basis_next.reshape(count + 2, window, nx, ny)


def solution(mesh):
    finer = Mesh(mesh.devices.reshape(8, 4, 4, 2), ("z", "y", "x", "c"))
    in_specs = (P(None, GX, GY), P(None, GX, GY), P(), P(), P(None, None, GX, GY))
    out_specs = (P(None, GX, GY), P(None, None, GX, GY))
    return jax.shard_map(steps, mesh=finer, in_specs=in_specs, out_specs=out_specs, check_vma=False)
```

```python
import math

import jax
import jax.numpy as jnp
from jax import lax
from jax.experimental import pallas as pl
from jax.experimental.pallas import tpu as pltpu
from jax.sharding import Mesh
from jax.sharding import PartitionSpec as P


F32 = jnp.float32
BF16 = jnp.bfloat16
GX = ("z", "y")
GY = ("x", "c")
CHIPS = ("z", "y", "x")
ROOT_ITERS = 5
SHIFTS = 2**ROOT_ITERS
POLES = SHIFTS // 2 - 1
VMEM = pltpu.VMEM


def lanes_of(shape):
    return lax.broadcasted_iota(jnp.int32, shape, len(shape) - 1)


def rows_of(shape):
    return lax.broadcasted_iota(jnp.int32, shape, len(shape) - 2)


def step(c, xm, xp, ym, yp, zm, zp, d, vxp, vxn, vyp, vyn):
    spread = (xm + xp) + (ym + yp) + (zm + zp) - 6.0 * c
    carried = (vxp * (c - xm) + vxn * (xp - c)) + (vyp * (c - ym) + vyn * (yp - c))
    return c + d * spread - carried


def signed_parts(vx, vy):
    return jnp.maximum(vx, 0.0), jnp.minimum(vx, 0.0), jnp.maximum(vy, 0.0), jnp.minimum(vy, 0.0)


def before(c, ghost, axis):
    at = lax.broadcasted_iota(jnp.int32, c.shape, axis)
    return jnp.where(at == 0, ghost, pltpu.roll(c, 1, axis))


def after(c, ghost, axis):
    n = c.shape[axis]
    at = lax.broadcasted_iota(jnp.int32, c.shape, axis)
    return jnp.where(at == n - 1, ghost, pltpu.roll(c, n - 1, axis))


def gx_is_even():
    return lax.axis_index("y") % 2 == 0


def gy_is_even():
    return lax.axis_index("c") == 0


def to_pairs(even, up, down):
    return jnp.where(even, down, up), jnp.where(even, up, down)


def from_pairs(even, near, far):
    return jnp.where(even, far, near), jnp.where(even, near, far)


def pack_columns_kernel(
    chunks, tracer_hbm, velocity_hbm, near, far, window, rows_near, rows_far, mine,
    tracer, velocity, sems,
):
    nx, ny = velocity.shape[1:]
    nz = tracer.shape[0] // nx
    size = nz // chunks
    loads = [
        pltpu.make_async_copy(
            tracer_hbm.at[pl.ds(i * size * nx, size * nx)],
            tracer.at[pl.ds(i * size * nx, size * nx)], sems.at[i],
        )
        for i in range(chunks)
    ]
    loads.append(pltpu.make_async_copy(velocity_hbm, velocity, sems.at[chunks]))
    for load in loads:
        load.start()
    lane = lanes_of((nx, ny))

    def level(z, carry):
        a, b, y, w = carry
        r = pltpu.roll(tracer[pl.ds(pl.multiple_of(z * nx, nx), nx), :], z, 1)
        rel = (lane - z) & (ny - 1)
        a = jnp.where(rel == 0, r, a)
        b = jnp.where(rel == 1, r, b)
        y = jnp.where(rel == ny - 1, r, y)
        w = jnp.where(rel == ny - 2, r, w)
        return a, b, y, w

    carry = (jnp.zeros((nx, ny), F32),) * 4
    for i in range(chunks):
        loads[i].wait()
        carry = lax.fori_loop(i * size, (i + 1) * size, level, carry, unroll=8)
    a, b, y, w = carry
    loads[chunks].wait()
    vx, vy = velocity[0], velocity[1]
    left = (a, pltpu.roll(b, ny - 1, 1), jnp.where(lane == 0, vx, pltpu.roll(vy, 1, 1)))
    right = (
        pltpu.roll(y, 1, 1), pltpu.roll(w, 2, 1),
        jnp.where(lane == ny - 1, vx, pltpu.roll(vy, ny - 1, 1)),
    )
    even = gy_is_even()
    for i in range(3):
        near[i], far[i] = to_pairs(even, left[i], right[i])
    mine[0], mine[1] = left[0], right[0]
    window[0 : 2 * nx] = tracer[(nz - 2) * nx : nz * nx]
    window[2 * nx : 6 * nx] = tracer[0 : 4 * nx]
    even = gx_is_even()
    for i in range(2):
        top = tracer[pl.ds(i, nz, stride=nx), :]
        bottom = tracer[pl.ds(nx - 1 - i, nz, stride=nx), :]
        rows_near[i], rows_far[i] = to_pairs(even, top, bottom)


def pack_rows_kernel(window, velocity, sides_near, sides_far, near, far, up, down):
    nx, ny = velocity.shape[1:]
    from_left, from_right = from_pairs(gy_is_even(), sides_near[0], sides_far[0])
    for edge, inner, out in ((0, 1, up), (nx - 1, nx - 2, down)):
        for s in range(6):
            out[s : s + 1, :] = window[s * nx + edge : s * nx + edge + 1, :]
            out[8 + s : 9 + s, :] = window[s * nx + inner : s * nx + inner + 1, :]
        for s in (6, 7, 14, 15, 20, 21, 22, 23):
            out[s : s + 1, :] = jnp.zeros((1, ny), F32)
        out[16:17, :] = velocity[0, edge : edge + 1, :]
        out[17:18, :] = velocity[1, edge : edge + 1, :]
        out[18:19, :] = from_left[edge : edge + 1, :]
        out[19:20, :] = from_right[edge : edge + 1, :]
    near[...], far[...] = to_pairs(gx_is_even(), up[...], down[...])


def window_kernel(
    diff, near, velocity, diff_row, mine, sides_near, sides_far,
    own_up, own_down, rows_near, rows_far, basis,
    kept_hbm, sums, snaps, sides, q0, q1, sems,
):
    nz, nx, ny = diff.shape[0], velocity.shape[1], velocity.shape[2]
    count = basis.shape[0]
    dz = diff_row[...]
    even = gy_is_even()
    pairs = [from_pairs(even, sides_near[i], sides_far[i]) for i in range(3)]
    from_left, from_right = [p[0] for p in pairs], [p[1] for p in pairs]
    from_up, from_down = from_pairs(gx_is_even(), rows_near[...], rows_far[...])
    for gin, inner, outer, corner, vx_at, vy_at, out in (
        (from_left, None, mine[0], 18, ny - 1, ny - 2, sides.at[0:nx]),
        (from_right, mine[1], None, 19, 0, 1, sides.at[nx : 2 * nx]),
    ):
        c = gin[0]
        ym = gin[1] if inner is None else inner
        yp = gin[1] if outer is None else outer
        vx = gin[2][:, vx_at : vx_at + 1]
        vy = gin[2][:, vy_at : vy_at + 1]
        parts = signed_parts(vx, vy)
        xm = before(c, from_up[corner : corner + 1, :], 0)
        xp = after(c, from_down[corner : corner + 1, :], 0)
        out[...] = step(c, xm, xp, ym, yp, pltpu.roll(c, 1, 1), pltpu.roll(c, nz - 1, 1), dz, *parts)

    sub = rows_of((8, ny))
    lane = lanes_of((8, ny))
    d_rows = jnp.where(sub == 2, diff[0], diff[1])
    ghost_rows = []
    for gin, own, top in ((from_up, own_up, True), (from_down, own_down, False)):
        c = gin[0:8, :]
        beyond, inside = gin[8:16, :], own[0:8, :]
        xm, xp = (beyond, inside) if top else (inside, beyond)
        west = jnp.where(sub == 2, gin[18:19, 0:1], gin[18:19, 1:2])
        east = jnp.where(sub == 2, gin[19:20, 0:1], gin[19:20, 1:2])
        parts = signed_parts(gin[16:17, :], gin[17:18, :])
        ghost_rows.append(
            step(c, xm, xp, before(c, west, 1), after(c, east, 1),
                 pltpu.roll(c, 1, 0), pltpu.roll(c, 7, 0), d_rows, *parts)
        )

    parts = signed_parts(velocity[0], velocity[1])
    u = [near[s * nx : (s + 1) * nx] for s in range(6)]
    first = []
    for s in range(1, 5):
        z = (s - 2) % nz
        c = u[s]
        xm = before(c, from_up[s : s + 1, :], 0)
        xp = after(c, from_down[s : s + 1, :], 0)
        ym = before(c, from_left[0][:, z : z + 1], 1)
        yp = after(c, from_right[0][:, z : z + 1], 1)
        first.append(step(c, xm, xp, ym, yp, u[s - 1], u[s + 1], diff[z], *parts))
    for z in range(2):
        c = first[z + 1]
        snaps[0, z * nx : (z + 1) * nx, :] = c
        xm = before(c, ghost_rows[0][z + 2 : z + 3, :], 0)
        xp = after(c, ghost_rows[1][z + 2 : z + 3, :], 0)
        ym = before(c, sides[0:nx, z : z + 1], 1)
        yp = after(c, sides[nx : 2 * nx, z : z + 1], 1)
        snaps[1, z * nx : (z + 1) * nx, :] = step(
            c, xm, xp, ym, yp, first[z], first[z + 2], diff[z], *parts
        )

    rows = 2 * nx
    pieces = rows // 8
    sides[rows : rows + 8] = from_up[16:24, :]
    sides[rows + 8 : rows + 16] = from_down[16:24, :]
    keep = [
        pltpu.make_async_copy(ref, kept_hbm.at[pl.ds(at, ref.shape[0])], sems.at[i])
        for i, (ref, at) in enumerate(
            ((snaps.at[0], 0), (snaps.at[1], rows), (sides, 2 * rows))
        )
    ]
    for copy in keep:
        copy.start()

    def folded(a, b):
        total = a[0:8, :] * b[0:8, :]
        for i in range(1, pieces):
            total = total + a[8 * i : 8 * i + 8, :] * b[8 * i : 8 * i + 8, :]
        return total

    def group(vectors, start, size):
        for m, q in enumerate((q0, q1)):
            lines = jnp.stack([folded(v, snaps[m]) for v in vectors])
            q[pl.ds(start, size), :] = jnp.sum(lines, axis=1)

    def eight(i, carry):
        at = pl.multiple_of(8 * i, 8)
        group([basis[at + j] for j in range(8)], at, 8)
        return carry

    full = count // 8 * 8
    lax.fori_loop(0, count // 8, eight, 0)
    group([basis[k] for k in range(full, count)] + [snaps[0], snaps[1]], full, count + 2 - full)
    for q in (q0, q1):
        q[count + 2 :] = jnp.zeros((ny - count - 2, ny), F32)
    ones = jnp.ones((8, ny), F32)
    over_lanes = (((1,), (1,)), ((), ()))
    for m, q in enumerate((q0, q1)):
        line = lax.dot_general(
            ones, q[...], over_lanes, precision=lax.Precision.HIGHEST, preferred_element_type=F32
        )
        sums[m : m + 1, :] = line[0:1, :]
    for copy in keep:
        copy.wait()


def split(vectors, snaps, upper, lower):
    rows, ny = vectors.shape[0], vectors.shape[2]
    for r in range(rows):
        pair, half = r // 2, r % 2
        lanes = slice(half * ny, (half + 1) * ny)
        v = jnp.concatenate(
            [vectors[r], snaps[r : r + 1, :], snaps[rows + r : rows + r + 1, :]], axis=0
        )
        hi = v.astype(BF16)
        upper[pair, :, lanes] = hi
        lower[pair, :, lanes] = (v - hi.astype(F32)).astype(BF16)


def load_kernel(src, dst, sems):
    parts = sems.shape[0]
    size = src.shape[0] // parts
    copies = [
        pltpu.make_async_copy(src.at[pl.ds(i * size, size)], dst.at[pl.ds(i * size, size)], sems.at[i])
        for i in range(parts)
    ]
    for copy in copies:
        copy.start()
    for copy in copies:
        copy.wait()


def level_loads(src, dst, sems, chunks, nx):
    pitch = nx + 16
    nz = src.shape[0]
    size = nz // chunks
    view = dst.reshape(nz, pitch, dst.shape[1])

    def copy(at, length, sem):
        part = pl.ds(at, length)
        return pltpu.make_async_copy(src.at[part], view.at[part, pl.ds(8, nx), :], sem)

    def chunk(k):
        return copy(k * size, size, sems.at[k])

    end = copy(nz - size, size - 1, sems.at[chunks - 1])
    last = copy(nz - 1, 1, sems.at[chunks])
    return chunk, end, last


def sweep(diff, velocity, src, dst, col_left, col_right, wait, after_block, chunks):
    nx, ny = velocity.shape[1:]
    pitch = nx + 16
    nz = src.shape[0] // pitch
    size = nz // chunks
    vx, vy = velocity[0], velocity[1]
    east, north = vx > 0.0, vy > 0.0
    speed_x, speed_y = jnp.abs(vx), jnp.abs(vy)
    stay = 1.0 - speed_x - speed_y
    lane = lanes_of((nx, ny))
    first, last = lane == 0, lane == ny - 1
    is_even = (lane & 1) == 0
    shifted = pltpu.roll(col_right, nz - 1, 1)
    columns = (jnp.where(is_even, col_left, shifted), jnp.where(is_even, shifted, col_left))

    def rows_at(z, by):
        return pl.ds(pl.multiple_of(z * pitch, 8) + 8 + by, nx)

    def turned(c, z, which):
        side = pltpu.roll(columns[which], (nz - z) & (nz - 1), 1)
        return pltpu.roll(c, 1, 1), pltpu.roll(c, ny - 1, 1), side

    def level(z, next_parity, state):
        zm, c, south, north_side, side = state
        zn = (z + 1) & (nz - 1)
        zp = src[rows_at(zn, 0), :]
        ahead = turned(zp, zn, next_parity)
        ym = jnp.where(first, side, south)
        yp = jnp.where(last, side, north_side)
        xm = src[rows_at(z, -1), :]
        xp = src[rows_at(z, 1), :]
        d = diff[z]
        moved = speed_x * jnp.where(east, xm, xp) + speed_y * jnp.where(north, ym, yp)
        spread = ((xm + xp) + (ym + yp)) + (zm + zp)
        dst[rows_at(z, 0), :] = (c * (stay - 6.0 * d) + moved) + d * spread
        return (c, zp, *ahead)

    def block(k, state):
        wait(k)
        for i in range(0, size, 2):
            z = k * size + i
            state = level(z + 1, 0, level(z, 1, state))
        after_block(k)
        return state

    c = src[rows_at(0, 0), :]
    state = (src[rows_at(nz - 1, 0), :], c, *turned(c, 0, 0))
    lax.fori_loop(0, chunks, block, state)


def level_store(src, out, sems, chunks, nx):
    pitch = nx + 16
    nz = src.shape[0] // pitch
    size = nz // chunks
    view = src.reshape(nz, pitch, src.shape[1])

    def store(k):
        part = pl.ds(k * size, size)
        return pltpu.make_async_copy(view.at[part, pl.ds(8, nx), :], out.at[part], sems.at[k])

    return store


def start_loads(loads, chunks):
    chunk, end, last = loads
    last.start()
    for k in range(chunks - 1):
        chunk(k).start()
    end.start()


def bulk_kernel(
    chunks, diff, tracer, basis, kept_hbm, rows_near, rows_far, velocity, diff_row, singular,
    sides_near, sides_far, out, upper, lower, line, now, then, vectors, kept, got_near, got_far,
    load_sems, store_sems, sems,
):
    nz, nx, _ = tracer.shape
    pitch = nx + 16
    count = singular.shape[1]
    small = [
        pltpu.make_async_copy(src, dst, sems.at[i])
        for i, (src, dst) in enumerate(
            ((rows_near, got_near), (rows_far, got_far), (kept_hbm, kept))
        )
    ]
    for load in small:
        load.start()
    loads = level_loads(tracer, now, load_sems, chunks, nx)
    start_loads(loads, chunks)
    gathers = [
        pltpu.make_async_copy(basis.at[:, r, 0, :], vectors.at[r], sems.at[3 + r])
        for r in range(vectors.shape[0])
    ]
    for gather in gathers:
        gather.start()
    line[...] = jnp.zeros_like(line)
    line[0:1, :count] = singular[...]
    eye = rows_of((nz, nz)) == lanes_of((nz, nz))
    d_all = jnp.sum(jnp.where(eye, diff_row[...], 0.0), axis=1, keepdims=True)
    small[0].wait()
    small[1].wait()
    even = gx_is_even()
    from_up, from_down = from_pairs(even, got_near[0], got_far[0])
    now[pl.ds(7, nz, stride=pitch), :] = from_up
    now[pl.ds(8 + nx, nz, stride=pitch), :] = from_down
    chunk, end, final = loads
    final.wait()
    chunk(0).wait()

    def wait(k):
        @pl.when(k < chunks - 2)
        def _():
            chunk(k + 1).wait()

        @pl.when(k == chunks - 2)
        def _():
            end.wait()

    from_left, from_right = from_pairs(gy_is_even(), sides_near[0], sides_far[0])
    sweep(diff, velocity, now, then, from_left, from_right, wait, lambda k: None, chunks)
    small[2].wait()
    nearest = from_pairs(even, got_near[0], got_far[0])
    beyonds = from_pairs(even, got_near[1], got_far[1])
    for is_top, c, beyond, at in zip((True, False), nearest, beyonds, (6 * nx, 6 * nx + 8)):
        gin = kept[at : at + 8, :]
        inside = now[pl.ds(8 if is_top else 7 + nx, nz, stride=pitch), :]
        xm, xp = (beyond, inside) if is_top else (inside, beyond)
        west = jnp.sum(jnp.where(eye, gin[2:3, :], 0.0), axis=1, keepdims=True)
        east = jnp.sum(jnp.where(eye, gin[3:4, :], 0.0), axis=1, keepdims=True)
        parts = signed_parts(gin[0:1, :], gin[1:2, :])
        then[pl.ds(7 if is_top else 8 + nx, nz, stride=pitch), :] = step(
            c, xm, xp, before(c, west, 1), after(c, east, 1),
            pltpu.roll(c, 1, 0), pltpu.roll(c, nz - 1, 0), d_all, *parts
        )
    store = level_store(now, out, store_sems, chunks, nx)
    col_left, col_right = kept[4 * nx : 5 * nx, :], kept[5 * nx : 6 * nx, :]
    sweep(
        diff, velocity, then, now, col_left, col_right, lambda k: None,
        lambda k: store(k).start(), chunks,
    )
    for gather in gathers:
        gather.wait()
    split(vectors, kept, upper, lower)
    for k in range(chunks):
        store(k).wait()


def spread_kernel(mine, other, out):
    both = mine[...] + other[...]
    out[...] = jnp.broadcast_to(both[None], out.shape)


def core_kernel(rows_all, parts, singular, upper, lower, out, block, sems):
    count = out.shape[0] - 2
    n = parts.shape[2]
    total = jnp.sum(parts[...], axis=0)
    total = total + pltpu.roll(total, 2, 0)
    total = total + pltpu.roll(total, 4, 0)
    total = total * (1.0 / rows_all)
    lane = lanes_of((1, n))
    zero = jnp.zeros((1, n), F32)

    def add(x):
        return jnp.sum(x, axis=1, keepdims=True)

    def pick(x, at):
        return add(jnp.where(lane == at, x, zero))

    p0 = jnp.where(lane < count, total[0:1, :], zero)
    p1 = jnp.where(lane < count, total[1:2, :], zero)
    g00 = pick(total[0:1, :], count) - add(p0 * p0) + 1e-06
    g01 = pick(total[0:1, :], count + 1) - add(p0 * p1)
    g11 = pick(total[1:2, :], count + 1) - add(p1 * p1) + 1e-06
    r11 = jnp.sqrt(g00)
    r12 = g01 / r11
    r22 = jnp.sqrt(g11 - r12 * r12)
    u0 = jnp.where(lane == count, r11, p0)
    u1 = jnp.where(lane == count, r12, jnp.where(lane == count + 1, r22, p1))
    s = singular[0:1, :]
    squares = s * s
    sigma = add(squares + u0 * u0 + u1 * u1) / (count + 2)
    root = jnp.sqrt(sigma)
    d = squares / sigma
    v0 = u0 / root
    v1 = u1 / root

    half = POLES + 1
    row = rows_of((half, n))
    pole = jnp.zeros((half, n), F32)
    for j in range(POLES):
        pole = jnp.where(row == j, math.tan(math.pi * (j + 1) / SHIFTS) ** 2, pole)
    last = row == POLES
    pole = jnp.where(last, 1.0, pole)
    inverse = jnp.where(last, 1.0, 1.0 / (d + pole))
    weight = 2.0 * (1.0 + pole)
    w0 = inverse * v0
    w1 = inverse * v1
    last_one = last[:, 0:1]
    a = jnp.where(last_one, 1.0, 1.0 + add(w0 * v0))
    b = jnp.where(last_one, 0.0, add(w0 * v1))
    c = jnp.where(last_one, 1.0, 1.0 + add(w1 * v1))
    e = b / a
    c = c - b * e
    strength = jnp.where(last, 1.0, weight * pole)
    w1 = jnp.sqrt(strength / c) * (w1 - e * w0)
    w0 = jnp.sqrt(strength / a) * w0
    low_rank = jnp.concatenate([w0, w1], axis=0)
    gains = 1.0 + d + jnp.sum(jnp.where(last, 0.0, weight * d * inverse), axis=0, keepdims=True)
    square = (n, n)
    core = lax.dot_general(
        low_rank, low_rank, (((0,), (0,)), ((), ())),
        precision=lax.Precision.HIGHEST, preferred_element_type=F32,
    )
    core = core + jnp.where(rows_of(square) == lanes_of(square), gains, 0.0)
    core = core * (root * (1.0 / SHIFTS))
    t0 = jnp.where(lane == count, 1.0, -p0) / r11
    q_lane = jnp.where(lane == count + 1, 1.0, -p1)
    t1 = (q_lane - r12 * t0) / r22
    full = jnp.where(lanes_of(square) < count, core, 0.0)
    full = full + core[:, count : count + 1] * t0 + core[:, count + 1 : count + 2] * t1
    full = full[: count + 2, : count + 2]
    hi = full.astype(BF16)
    lo = (full - hi.astype(F32)).astype(BF16)
    both = jnp.concatenate([hi, lo], axis=0)

    size = count + 2
    copies = []
    for pair in range(upper.shape[0]):
        r = jnp.dot(both, upper[pair], preferred_element_type=F32)
        r = r[:size] + r[size:] + jnp.dot(hi, lower[pair], preferred_element_type=F32)
        for half in range(2):
            at = 2 * pair + half
            block[at] = r[:, half * n : (half + 1) * n]
            copy = pltpu.make_async_copy(block.at[at], out.at[:, at, 0, :], sems.at[at])
            copy.start()
            copies.append(copy)
    for copy in copies:
        copy.wait()


def whole(n):
    return [pl.BlockSpec(memory_space=VMEM)] * n


SMEM_SPEC = pl.BlockSpec(memory_space=pltpu.SMEM)


def shaped(*shape, dtype=F32):
    return jax.ShapeDtypeStruct(shape, dtype)


def in_hbm(x):
    return pltpu.with_memory_space_constraint(x, pltpu.HBM)


def cost(flops, moved):
    return pl.CostEstimate(flops=flops, bytes_accessed=moved, transcendentals=0)


def limit(mib):
    return pltpu.CompilerParams(vmem_limit_bytes=mib * 2**20)


def swap(x, axes, far):
    count = lax.axis_size(axes)
    shift = 1 if far else 0
    pairs = [((i + shift) % count, ((i ^ 1) + shift) % count) for i in range(count)]
    return lax.ppermute(x, axes, pairs)


def steps(tracer, velocity, diffusivity, singular, basis_vectors):
    nz, nx, ny = tracer.shape
    count, window = basis_vectors.shape[:2]
    rows = window * nx
    basis = basis_vectors.reshape(count, rows, ny)
    rows_all = rows * ny * lax.axis_size(GX) * lax.axis_size(GY)
    chips = lax.axis_size(CHIPS)
    diff_row = diffusivity.reshape(1, nz)

    columns = shaped(3, nx, ny)
    bulk_rows = shaped(2, nz, ny)
    hbm_space, any_space = (pl.BlockSpec(memory_space=m) for m in (pltpu.HBM, pl.ANY))
    columns_near, columns_far, near, sent_near, sent_far, mine = pl.pallas_call(
        lambda *refs: pack_columns_kernel(8, *refs),
        out_shape=(
            columns, columns, shaped(6 * nx, ny), bulk_rows, bulk_rows, shaped(2, nx, ny),
        ),
        in_specs=[hbm_space] * 2, out_specs=tuple(whole(6)),
        scratch_shapes=[
            VMEM((nz * nx, ny), F32), VMEM((2, nx, ny), F32), pltpu.SemaphoreType.DMA((9,)),
        ],
        compiler_params=limit(4), cost_estimate=cost(10**6, 2 * 2**20), name="columns",
    )(in_hbm(tracer.reshape(nz * nx, ny)), in_hbm(velocity))
    sides_far = swap(columns_far, GY, True)
    sides_near = swap(columns_near, GY, False)
    sent_near, sent_far = in_hbm(sent_near), in_hbm(sent_far)
    rows_far = in_hbm(swap(sent_far, GX, True))
    rows_near = in_hbm(swap(sent_near, GX, False))

    edge = shaped(24, ny)
    edges_near, edges_far, own_up, own_down = pl.pallas_call(
        pack_rows_kernel, out_shape=(edge,) * 4, in_specs=whole(4), out_specs=tuple(whole(4)),
        compiler_params=limit(2), cost_estimate=cost(10**4, 2**17), name="edges",
    )(near, velocity, sides_near, sides_far)
    window_far = swap(edges_far, GX, True)
    window_near = swap(edges_near, GX, False)

    vectors = pl.pallas_call(
        load_kernel, out_shape=shaped(count, rows, ny),
        in_specs=[hbm_space], out_specs=whole(1)[0],
        scratch_shapes=[pltpu.SemaphoreType.DMA((2,))],
        compiler_params=limit(2), cost_estimate=cost(0, 6 * 2**20), name="load",
    )(in_hbm(basis))
    kept, local = pl.pallas_call(
        window_kernel,
        out_shape=(pltpu.HBM((6 * nx + 16, ny), F32), shaped(2, ny)),
        in_specs=[SMEM_SPEC] + whole(11), out_specs=(hbm_space, *whole(1)),
        scratch_shapes=[
            VMEM((2, rows, ny), F32), VMEM((rows + 16, ny), F32), VMEM((ny, ny), F32),
            VMEM((ny, ny), F32), pltpu.SemaphoreType.DMA((3,)),
        ],
        compiler_params=limit(4), cost_estimate=cost(10**7, 4 * 2**20), name="window",
    )(
        diffusivity, near, velocity, diff_row, mine, sides_near, sides_far,
        own_up, own_down, window_near, window_far, vectors,
    )

    other = lax.ppermute(local, "c", [(0, 1), (1, 0)])
    sent = pl.pallas_call(
        spread_kernel, out_shape=shaped(chips, 2, ny), in_specs=whole(2), out_specs=whole(1)[0],
        compiler_params=limit(4), cost_estimate=cost(10**4, 2**17), name="spread",
    )(local, other)
    parts = lax.all_to_all(sent, CHIPS, 0, 0, tiled=True)

    halves = shaped(rows // 2, count + 2, 2 * ny, dtype=BF16)
    padded = VMEM((nz * (nx + 16), ny), F32)
    tracer_next, upper, lower, line = pl.pallas_call(
        lambda *refs: bulk_kernel(8, *refs),
        out_shape=(shaped(nz, nx, ny), halves, halves, shaped(8, ny)),
        in_specs=[SMEM_SPEC] + [hbm_space] * 3 + [hbm_space] * 2 + whole(5),
        out_specs=(any_space, *whole(3)),
        scratch_shapes=[
            padded, padded, VMEM((rows, count, ny), F32), VMEM((6 * nx + 16, ny), F32),
            VMEM((2, nz, ny), F32), VMEM((2, nz, ny), F32), pltpu.SemaphoreType.DMA((9,)),
            pltpu.SemaphoreType.DMA((8,)), pltpu.SemaphoreType.DMA((3 + rows,)),
        ],
        compiler_params=limit(12), cost_estimate=cost(10**8, 10 * 2**20), name="bulk",
    )(
        diffusivity, in_hbm(tracer), in_hbm(basis.reshape(count, rows, 1, ny)), in_hbm(kept),
        rows_near, rows_far, velocity, diff_row, singular.reshape(1, count), sides_near, sides_far,
    )

    basis_next = pl.pallas_call(
        lambda *refs: core_kernel(rows_all, *refs),
        out_shape=shaped(count + 2, rows, 1, ny),
        in_specs=whole(4), out_specs=pl.BlockSpec(memory_space=pl.ANY),
        scratch_shapes=[
            VMEM((rows, count + 2, ny), F32),
            pltpu.SemaphoreType.DMA((rows,)),
        ],
        compiler_params=limit(16), cost_estimate=cost(10**8, 6 * 2**20), name="core",
    )(
        parts.reshape(chips // 4, 8, ny), line, upper, lower,
    )
    return tracer_next, basis_next.reshape(count + 2, window, nx, ny)


def solution(mesh):
    finer = Mesh(mesh.devices.reshape(8, 4, 4, 2), ("z", "y", "x", "c"))
    in_specs = (P(None, GX, GY), P(None, GX, GY), P(), P(), P(None, None, GX, GY))
    out_specs = (P(None, GX, GY), P(None, None, GX, GY))
    return jax.shard_map(steps, mesh=finer, in_specs=in_specs, out_specs=out_specs, check_vma=False)
```

```python
import math

import jax
import jax.numpy as jnp
from jax import lax
from jax.experimental import pallas as pl
from jax.experimental.pallas import tpu as pltpu
from jax.sharding import Mesh
from jax.sharding import PartitionSpec as P


F32 = jnp.float32
BF16 = jnp.bfloat16
GX = ("z", "y")
GY = ("x", "c")
CHIPS = ("z", "y", "x")
ROOT_ITERS = 5
SHIFTS = 2**ROOT_ITERS
POLES = SHIFTS // 2 - 1
VMEM = pltpu.VMEM


def lanes_of(shape):
    return lax.broadcasted_iota(jnp.int32, shape, len(shape) - 1)


def rows_of(shape):
    return lax.broadcasted_iota(jnp.int32, shape, len(shape) - 2)


def step(c, xm, xp, ym, yp, zm, zp, d, vxp, vxn, vyp, vyn):
    spread = (xm + xp) + (ym + yp) + (zm + zp) - 6.0 * c
    carried = (vxp * (c - xm) + vxn * (xp - c)) + (vyp * (c - ym) + vyn * (yp - c))
    return c + d * spread - carried


def signed_parts(vx, vy):
    return jnp.maximum(vx, 0.0), jnp.minimum(vx, 0.0), jnp.maximum(vy, 0.0), jnp.minimum(vy, 0.0)


def before(c, ghost, axis):
    at = lax.broadcasted_iota(jnp.int32, c.shape, axis)
    return jnp.where(at == 0, ghost, pltpu.roll(c, 1, axis))


def after(c, ghost, axis):
    n = c.shape[axis]
    at = lax.broadcasted_iota(jnp.int32, c.shape, axis)
    return jnp.where(at == n - 1, ghost, pltpu.roll(c, n - 1, axis))


def gx_is_even():
    return lax.axis_index("y") % 2 == 0


def gy_is_even():
    return lax.axis_index("c") == 0


def to_pairs(even, up, down):
    return jnp.where(even, down, up), jnp.where(even, up, down)


def from_pairs(even, near, far):
    return jnp.where(even, far, near), jnp.where(even, near, far)


def pack_columns_kernel(
    chunks, tracer_hbm, by_row_hbm, velocity_hbm, near, far, window, tops, bottoms, mine, velocity,
    tracer, sems,
):
    nx, ny = velocity.shape[1:]
    nz = tracer.shape[0] // nx
    size = nz // chunks

    def rows_of_level(at, count, dst):
        return tracer_hbm.at[pl.ds(at * nx, count * nx)], dst

    moves = [
        rows_of_level(i * size, size, tracer.at[pl.ds(i * size * nx, size * nx)])
        for i in range(chunks)
    ]
    moves.append((velocity_hbm, velocity))
    moves.append(rows_of_level(nz - 2, 2, window.at[0 : 2 * nx]))
    moves.append(rows_of_level(0, 4, window.at[2 * nx : 6 * nx]))
    for i in range(2):
        part = pl.ds(i * nz, nz)
        moves.append((by_row_hbm.at[:, i, 0, :], tops.at[part]))
        moves.append((by_row_hbm.at[:, nx - 1 - i, 0, :], bottoms.at[part]))
    loads = [pltpu.make_async_copy(src, dst, sems.at[i]) for i, (src, dst) in enumerate(moves)]
    for load in loads:
        load.start()
    lane = lanes_of((nx, ny))

    def four(i, carry):
        out = []
        for j in range(4):
            z = 4 * i + j
            r = pltpu.roll(tracer[z * nx : (z + 1) * nx], z, 1)
            out.append(jnp.where(((lane - z + 2) & (ny - 1)) < 4, r, carry[j]))
        return tuple(out)

    carry = (jnp.zeros((nx, ny), F32),) * 4
    for i in range(chunks):
        loads[i].wait()
        for k in range(i * size // 4, (i + 1) * size // 4):
            carry = four(k, carry)
    phase = lane & 3

    def column(shift):
        c = [pltpu.roll(x, shift, 1) if shift else x for x in carry]
        return jnp.where(
            phase < 2, jnp.where(phase == 0, c[0], c[1]), jnp.where(phase == 2, c[2], c[3])
        )

    loads[chunks].wait()
    vx, vy = velocity[0], velocity[1]
    left = (column(0), column(ny - 1), jnp.where(lane == 0, vx, pltpu.roll(vy, 1, 1)))
    right = (
        column(1), column(2),
        jnp.where(lane == ny - 1, vx, pltpu.roll(vy, ny - 1, 1)),
    )
    even = gy_is_even()
    for i in range(3):
        near[i], far[i] = to_pairs(even, left[i], right[i])
    mine[0], mine[1] = left[0], right[0]
    for load in loads[chunks + 1 :]:
        load.wait()


def pack_rows_kernel(
    window, velocity, tops, bottoms, sides_near, sides_far, near, far, up, down
):
    nx, ny = velocity.shape[1:]
    from_left, from_right = from_pairs(gy_is_even(), sides_near[0], sides_far[0])
    for edge, inner, out in ((0, 1, up), (nx - 1, nx - 2, down)):
        for s in range(6):
            out[s : s + 1, :] = window[s * nx + edge : s * nx + edge + 1, :]
            out[8 + s : 9 + s, :] = window[s * nx + inner : s * nx + inner + 1, :]
        for s in (6, 7, 14, 15, 20, 21, 22, 23):
            out[s : s + 1, :] = jnp.zeros((1, ny), F32)
        out[16:17, :] = velocity[0, edge : edge + 1, :]
        out[17:18, :] = velocity[1, edge : edge + 1, :]
        out[18:19, :] = from_left[edge : edge + 1, :]
        out[19:20, :] = from_right[edge : edge + 1, :]
    even = gx_is_even()
    near[0:24], far[0:24] = to_pairs(even, up[...], down[...])
    near[24:], far[24:] = to_pairs(even, tops[...], bottoms[...])


def window_kernel(
    diff, near, velocity, diff_row, mine, sides_near, sides_far,
    own_up, own_down, rows_near, rows_far, basis,
    kept_hbm, sums, near_hbm, far_hbm, snaps, sides, q0, q1, sems,
):
    nz, nx, ny = diff.shape[0], velocity.shape[1], velocity.shape[2]
    count = basis.shape[0]
    dz = diff_row[...]
    even = gy_is_even()
    pairs = [from_pairs(even, sides_near[i], sides_far[i]) for i in range(3)]
    from_left, from_right = [p[0] for p in pairs], [p[1] for p in pairs]
    from_up, from_down = from_pairs(gx_is_even(), rows_near[0:24], rows_far[0:24])
    for gin, inner, outer, corner, vx_at, vy_at, out in (
        (from_left, None, mine[0], 18, ny - 1, ny - 2, sides.at[0:nx]),
        (from_right, mine[1], None, 19, 0, 1, sides.at[nx : 2 * nx]),
    ):
        c = gin[0]
        ym = gin[1] if inner is None else inner
        yp = gin[1] if outer is None else outer
        vx = gin[2][:, vx_at : vx_at + 1]
        vy = gin[2][:, vy_at : vy_at + 1]
        parts = signed_parts(vx, vy)
        xm = before(c, from_up[corner : corner + 1, :], 0)
        xp = after(c, from_down[corner : corner + 1, :], 0)
        out[...] = step(c, xm, xp, ym, yp, pltpu.roll(c, 1, 1), pltpu.roll(c, nz - 1, 1), dz, *parts)

    sub = rows_of((8, ny))
    lane = lanes_of((8, ny))
    d_rows = jnp.where(sub == 2, diff[0], diff[1])
    ghost_rows = []
    for gin, own, top in ((from_up, own_up, True), (from_down, own_down, False)):
        c = gin[0:8, :]
        beyond, inside = gin[8:16, :], own[0:8, :]
        xm, xp = (beyond, inside) if top else (inside, beyond)
        west = jnp.where(sub == 2, gin[18:19, 0:1], gin[18:19, 1:2])
        east = jnp.where(sub == 2, gin[19:20, 0:1], gin[19:20, 1:2])
        parts = signed_parts(gin[16:17, :], gin[17:18, :])
        ghost_rows.append(
            step(c, xm, xp, before(c, west, 1), after(c, east, 1),
                 pltpu.roll(c, 1, 0), pltpu.roll(c, 7, 0), d_rows, *parts)
        )

    parts = signed_parts(velocity[0], velocity[1])
    u = [near[s * nx : (s + 1) * nx] for s in range(6)]
    first = []
    for s in range(1, 5):
        z = (s - 2) % nz
        c = u[s]
        xm = before(c, from_up[s : s + 1, :], 0)
        xp = after(c, from_down[s : s + 1, :], 0)
        ym = before(c, from_left[0][:, z : z + 1], 1)
        yp = after(c, from_right[0][:, z : z + 1], 1)
        first.append(step(c, xm, xp, ym, yp, u[s - 1], u[s + 1], diff[z], *parts))
    for z in range(2):
        c = first[z + 1]
        snaps[0, z * nx : (z + 1) * nx, :] = c
        xm = before(c, ghost_rows[0][z + 2 : z + 3, :], 0)
        xp = after(c, ghost_rows[1][z + 2 : z + 3, :], 0)
        ym = before(c, sides[0:nx, z : z + 1], 1)
        yp = after(c, sides[nx : 2 * nx, z : z + 1], 1)
        snaps[1, z * nx : (z + 1) * nx, :] = step(
            c, xm, xp, ym, yp, first[z], first[z + 2], diff[z], *parts
        )

    rows = 2 * nx
    pieces = rows // 8
    sides[rows : rows + 8] = from_up[16:24, :]
    sides[rows + 8 : rows + 16] = from_down[16:24, :]
    keep = [
        pltpu.make_async_copy(ref, kept_hbm.at[pl.ds(at, ref.shape[0])], sems.at[i])
        for i, (ref, at) in enumerate(
            ((snaps.at[0], 0), (snaps.at[1], rows), (sides, 2 * rows))
        )
    ]
    bulk = pl.ds(24, 2 * nz)
    keep.append(pltpu.make_async_copy(rows_near.at[bulk], near_hbm, sems.at[3]))
    keep.append(pltpu.make_async_copy(rows_far.at[bulk], far_hbm, sems.at[4]))
    for copy in keep:
        copy.start()

    def folded(a, b):
        total = a[0:8, :] * b[0:8, :]
        for i in range(1, pieces):
            total = total + a[8 * i : 8 * i + 8, :] * b[8 * i : 8 * i + 8, :]
        return total

    def group(vectors, start, size):
        for m, q in enumerate((q0, q1)):
            lines = jnp.stack([folded(v, snaps[m]) for v in vectors])
            q[pl.ds(start, size), :] = jnp.sum(lines, axis=1)

    def eight(i, carry):
        at = pl.multiple_of(8 * i, 8)
        group([basis[at + j] for j in range(8)], at, 8)
        return carry

    full = count // 8 * 8
    lax.fori_loop(0, count // 8, eight, 0)
    group([basis[k] for k in range(full, count)] + [snaps[0], snaps[1]], full, count + 2 - full)
    for q in (q0, q1):
        q[count + 2 :] = jnp.zeros((ny - count - 2, ny), F32)
    ones = jnp.ones((8, ny), F32)
    over_lanes = (((1,), (1,)), ((), ()))
    for m, q in enumerate((q0, q1)):
        line = lax.dot_general(
            ones, q[...], over_lanes, precision=lax.Precision.HIGHEST, preferred_element_type=F32
        )
        sums[m : m + 1, :] = line[0:1, :]
    for copy in keep:
        copy.wait()


def split(vectors, snaps, halves):
    rows, ny = vectors.shape[0], vectors.shape[2]
    size = halves.shape[1] // 2
    for r in range(rows):
        pair, half = r // 2, r % 2
        lanes = slice(half * ny, (half + 1) * ny)
        v = jnp.concatenate(
            [vectors[r], snaps[r : r + 1, :], snaps[rows + r : rows + r + 1, :]], axis=0
        )
        hi = v.astype(BF16)
        halves[pair, :size, lanes] = hi
        halves[pair, size:, lanes] = (v - hi.astype(F32)).astype(BF16)


def load_kernel(src, dst, sems):
    parts = sems.shape[0]
    size = src.shape[0] // parts
    copies = [
        pltpu.make_async_copy(src.at[pl.ds(i * size, size)], dst.at[pl.ds(i * size, size)], sems.at[i])
        for i in range(parts)
    ]
    for copy in copies:
        copy.start()
    for copy in copies:
        copy.wait()


def level_loads(src, dst, sems, chunks, nx):
    pitch = nx + 16
    nz = src.shape[0]
    size = nz // chunks
    view = dst.reshape(nz, pitch, dst.shape[1])

    def copy(at, length, sem):
        part = pl.ds(at, length)
        return pltpu.make_async_copy(src.at[part], view.at[part, pl.ds(8, nx), :], sem)

    def chunk(k):
        return copy(k * size, size, sems.at[k])

    end = copy(nz - size, size - 1, sems.at[chunks - 1])
    last = copy(nz - 1, 1, sems.at[chunks])
    return chunk, end, last


def sweep(diff, velocity, src, dst, col_left, col_right, wait, after_block, chunks):
    nx, ny = velocity.shape[1:]
    pitch = nx + 16
    nz = src.shape[0] // pitch
    size = nz // chunks
    vx, vy = velocity[0], velocity[1]
    east, north = vx > 0.0, vy > 0.0
    speed_x, speed_y = jnp.abs(vx), jnp.abs(vy)
    stay = 1.0 - speed_x - speed_y
    lane = lanes_of((nx, ny))
    first, last = lane == 0, lane == ny - 1
    is_even = (lane & 1) == 0
    shifted = pltpu.roll(col_right, nz - 1, 1)
    columns = (jnp.where(is_even, col_left, shifted), jnp.where(is_even, shifted, col_left))

    def rows_at(z, by):
        return pl.ds(pl.multiple_of(z * pitch, 8) + 8 + by, nx)

    def turned(c, z, which):
        side = pltpu.roll(columns[which], (nz - z) & (nz - 1), 1)
        return pltpu.roll(c, 1, 1), pltpu.roll(c, ny - 1, 1), side

    def level(z, next_parity, state):
        zm, c, south, north_side, side = state
        zn = (z + 1) & (nz - 1)
        zp = src[rows_at(zn, 0), :]
        ahead = turned(zp, zn, next_parity)
        ym = jnp.where(first, side, south)
        yp = jnp.where(last, side, north_side)
        xm = src[rows_at(z, -1), :]
        xp = src[rows_at(z, 1), :]
        d = diff[z]
        moved = speed_x * jnp.where(east, xm, xp) + speed_y * jnp.where(north, ym, yp)
        spread = ((xm + xp) + (ym + yp)) + (zm + zp)
        dst[rows_at(z, 0), :] = (c * (stay - 6.0 * d) + moved) + d * spread
        return (c, zp, *ahead)

    def block(k, state):
        wait(k)
        for i in range(0, size, 2):
            z = k * size + i
            state = level(z + 1, 0, level(z, 1, state))
        after_block(k)
        return state

    c = src[rows_at(0, 0), :]
    state = (src[rows_at(nz - 1, 0), :], c, *turned(c, 0, 0))
    lax.fori_loop(0, chunks, block, state)


def level_store(src, out, sems, chunks, nx):
    pitch = nx + 16
    nz = src.shape[0] // pitch
    size = nz // chunks
    view = src.reshape(nz, pitch, src.shape[1])

    def store(k):
        part = pl.ds(k * size, size)
        return pltpu.make_async_copy(view.at[part, pl.ds(8, nx), :], out.at[part], sems.at[k])

    return store


def start_loads(loads, chunks):
    chunk, end, last = loads
    last.start()
    for k in range(chunks - 1):
        chunk(k).start()
    end.start()


def bulk_kernel(
    chunks, diff, tracer, basis, kept_hbm, rows_near, rows_far, velocity, diff_row, singular,
    sides_near, sides_far, out, halves, line, now, then, vectors, kept, got_near, got_far,
    load_sems, store_sems, sems,
):
    nz, nx, _ = tracer.shape
    pitch = nx + 16
    count = singular.shape[1]
    small = [
        pltpu.make_async_copy(src, dst, sems.at[i])
        for i, (src, dst) in enumerate(
            ((rows_near, got_near), (rows_far, got_far), (kept_hbm, kept))
        )
    ]
    for load in small:
        load.start()
    loads = level_loads(tracer, now, load_sems, chunks, nx)
    start_loads(loads, chunks)
    gathers = [
        pltpu.make_async_copy(basis.at[:, r, 0, :], vectors.at[r], sems.at[3 + r])
        for r in range(vectors.shape[0])
    ]
    for gather in gathers:
        gather.start()
    line[...] = jnp.zeros_like(line)
    line[0:1, :count] = singular[...]
    eye = rows_of((nz, nz)) == lanes_of((nz, nz))
    d_all = jnp.sum(jnp.where(eye, diff_row[...], 0.0), axis=1, keepdims=True)
    small[0].wait()
    small[1].wait()
    even = gx_is_even()
    from_up, from_down = from_pairs(even, got_near[0:nz], got_far[0:nz])
    now[pl.ds(7, nz, stride=pitch), :] = from_up
    now[pl.ds(8 + nx, nz, stride=pitch), :] = from_down
    chunk, end, final = loads
    final.wait()
    chunk(0).wait()

    def wait(k):
        @pl.when(k < chunks - 2)
        def _():
            chunk(k + 1).wait()

        @pl.when(k == chunks - 2)
        def _():
            end.wait()

    from_left, from_right = from_pairs(gy_is_even(), sides_near[0], sides_far[0])
    sweep(diff, velocity, now, then, from_left, from_right, wait, lambda k: None, chunks)
    small[2].wait()
    nearest = from_pairs(even, got_near[0:nz], got_far[0:nz])
    beyonds = from_pairs(even, got_near[nz:], got_far[nz:])
    for is_top, c, beyond, at in zip((True, False), nearest, beyonds, (6 * nx, 6 * nx + 8)):
        gin = kept[at : at + 8, :]
        inside = now[pl.ds(8 if is_top else 7 + nx, nz, stride=pitch), :]
        xm, xp = (beyond, inside) if is_top else (inside, beyond)
        west = jnp.sum(jnp.where(eye, gin[2:3, :], 0.0), axis=1, keepdims=True)
        east = jnp.sum(jnp.where(eye, gin[3:4, :], 0.0), axis=1, keepdims=True)
        parts = signed_parts(gin[0:1, :], gin[1:2, :])
        then[pl.ds(7 if is_top else 8 + nx, nz, stride=pitch), :] = step(
            c, xm, xp, before(c, west, 1), after(c, east, 1),
            pltpu.roll(c, 1, 0), pltpu.roll(c, nz - 1, 0), d_all, *parts
        )
    store = level_store(now, out, store_sems, chunks, nx)
    col_left, col_right = kept[4 * nx : 5 * nx, :], kept[5 * nx : 6 * nx, :]
    sweep(
        diff, velocity, then, now, col_left, col_right, lambda k: None,
        lambda k: store(k).start(), chunks,
    )
    for gather in gathers:
        gather.wait()
    split(vectors, kept, halves)
    for k in range(chunks):
        store(k).wait()


def spread_kernel(mine, other, out):
    both = mine[...] + other[...]
    out[...] = jnp.broadcast_to(both[None], out.shape)


def core_kernel(rows_all, parts, singular, halves, out, block, sems):
    count = out.shape[0] - 2
    n = parts.shape[2]
    total = jnp.sum(parts[...], axis=0)
    total = total + pltpu.roll(total, 2, 0)
    total = total + pltpu.roll(total, 4, 0)
    total = total * (1.0 / rows_all)
    lane = lanes_of((1, n))
    zero = jnp.zeros((1, n), F32)

    def add(x):
        return jnp.sum(x, axis=1, keepdims=True)

    def pick(x, at):
        return add(jnp.where(lane == at, x, zero))

    p0 = jnp.where(lane < count, total[0:1, :], zero)
    p1 = jnp.where(lane < count, total[1:2, :], zero)
    g00 = pick(total[0:1, :], count) - add(p0 * p0) + 1e-06
    g01 = pick(total[0:1, :], count + 1) - add(p0 * p1)
    g11 = pick(total[1:2, :], count + 1) - add(p1 * p1) + 1e-06
    r11 = jnp.sqrt(g00)
    r12 = g01 / r11
    r22 = jnp.sqrt(g11 - r12 * r12)
    u0 = jnp.where(lane == count, r11, p0)
    u1 = jnp.where(lane == count, r12, jnp.where(lane == count + 1, r22, p1))
    s = singular[0:1, :]
    squares = s * s
    sigma = add(squares + u0 * u0 + u1 * u1) / (count + 2)
    root = jnp.sqrt(sigma)
    d = squares / sigma
    v0 = u0 / root
    v1 = u1 / root

    half = POLES + 1
    row = rows_of((half, n))
    pole = jnp.zeros((half, n), F32)
    for j in range(POLES):
        pole = jnp.where(row == j, math.tan(math.pi * (j + 1) / SHIFTS) ** 2, pole)
    last = row == POLES
    pole = jnp.where(last, 1.0, pole)
    inverse = jnp.where(last, 1.0, 1.0 / (d + pole))
    weight = 2.0 * (1.0 + pole)
    w0 = inverse * v0
    w1 = inverse * v1
    last_one = last[:, 0:1]
    a = jnp.where(last_one, 1.0, 1.0 + add(w0 * v0))
    b = jnp.where(last_one, 0.0, add(w0 * v1))
    c = jnp.where(last_one, 1.0, 1.0 + add(w1 * v1))
    e = b / a
    c = c - b * e
    strength = jnp.where(last, 1.0, weight * pole)
    w1 = jnp.sqrt(strength / c) * (w1 - e * w0)
    w0 = jnp.sqrt(strength / a) * w0
    low_rank = jnp.concatenate([w0, w1], axis=0)
    gains = 1.0 + d + jnp.sum(jnp.where(last, 0.0, weight * d * inverse), axis=0, keepdims=True)
    square = (n, n)
    core = lax.dot_general(
        low_rank, low_rank, (((0,), (0,)), ((), ())),
        precision=lax.Precision.HIGHEST, preferred_element_type=F32,
    )
    core = core + jnp.where(rows_of(square) == lanes_of(square), gains, 0.0)
    core = core * (root * (1.0 / SHIFTS))
    t0 = jnp.where(lane == count, 1.0, -p0) / r11
    q_lane = jnp.where(lane == count + 1, 1.0, -p1)
    t1 = (q_lane - r12 * t0) / r22
    full = jnp.where(lanes_of(square) < count, core, 0.0)
    full = full + core[:, count : count + 1] * t0 + core[:, count + 1 : count + 2] * t1
    full = full[: count + 2, : count + 2]
    hi = full.astype(BF16)
    lo = (full - hi.astype(F32)).astype(BF16)
    twice = jnp.concatenate([hi, hi], axis=1)
    size = count + 2
    blocks = block.shape[1] // 8
    copies = []
    for b in range(blocks):
        tiles = []
        for pair in range(4 * b, 4 * b + 4):
            r = jnp.dot(twice, halves[pair], preferred_element_type=F32)
            r = r + jnp.dot(lo, halves[pair, :size], preferred_element_type=F32)
            tiles.append(r[:, :n])
            tiles.append(r[:, n:])
        block[:, 8 * b : 8 * b + 8, :] = jnp.swapaxes(jnp.stack(tiles), 0, 1)
        copy = pltpu.make_async_copy(
            block.at[:, pl.ds(8 * b, 8), :], out.at[:, pl.ds(8 * b, 8), :], sems.at[b]
        )
        copy.start()
        copies.append(copy)
    for copy in copies:
        copy.wait()


def whole(n):
    return [pl.BlockSpec(memory_space=VMEM)] * n


SMEM_SPEC = pl.BlockSpec(memory_space=pltpu.SMEM)


def shaped(*shape, dtype=F32):
    return jax.ShapeDtypeStruct(shape, dtype)


def in_hbm(x):
    return pltpu.with_memory_space_constraint(x, pltpu.HBM)


def cost(flops, moved):
    return pl.CostEstimate(flops=flops, bytes_accessed=moved, transcendentals=0)


def limit(mib):
    return pltpu.CompilerParams(vmem_limit_bytes=mib * 2**20)


def swap(x, axes, far):
    count = lax.axis_size(axes)
    shift = 1 if far else 0
    pairs = [((i + shift) % count, ((i ^ 1) + shift) % count) for i in range(count)]
    return lax.ppermute(x, axes, pairs)


def steps(tracer, velocity, diffusivity, singular, basis_vectors):
    nz, nx, ny = tracer.shape
    count, window = basis_vectors.shape[:2]
    rows = window * nx
    basis = basis_vectors.reshape(count, rows, ny)
    rows_all = rows * ny * lax.axis_size(GX) * lax.axis_size(GY)
    chips = lax.axis_size(CHIPS)
    diff_row = diffusivity.reshape(1, nz)

    columns = shaped(3, nx, ny)
    bulk_rows = shaped(2 * nz, ny)
    hbm_space, any_space = (pl.BlockSpec(memory_space=m) for m in (pltpu.HBM, pl.ANY))
    columns_near, columns_far, near, tops, bottoms, mine, speeds = pl.pallas_call(
        lambda *refs: pack_columns_kernel(4, *refs),
        out_shape=(
            columns, columns, shaped(6 * nx, ny), bulk_rows, bulk_rows, shaped(2, nx, ny),
            shaped(2, nx, ny),
        ),
        in_specs=[hbm_space] * 3, out_specs=tuple(whole(7)),
        scratch_shapes=[
            VMEM((nz * nx, ny), F32), pltpu.SemaphoreType.DMA((11,)),
        ],
        compiler_params=limit(4), cost_estimate=cost(10**6, 2 * 2**20), name="columns",
    )(
        in_hbm(tracer.reshape(nz * nx, ny)), in_hbm(tracer.reshape(nz, nx, 1, ny)), in_hbm(velocity)
    )
    sides_far = swap(columns_far, GY, True)
    sides_near = swap(columns_near, GY, False)
    edge, message = shaped(24, ny), shaped(24 + 2 * nz, ny)
    edges_near, edges_far, own_up, own_down = pl.pallas_call(
        pack_rows_kernel, out_shape=(message, message, edge, edge),
        in_specs=whole(6), out_specs=tuple(whole(4)),
        compiler_params=limit(2), cost_estimate=cost(10**4, 2**17), name="edges",
    )(near, speeds, tops, bottoms, sides_near, sides_far)
    window_far = swap(edges_far, GX, True)
    window_near = swap(edges_near, GX, False)

    vectors = pl.pallas_call(
        load_kernel, out_shape=shaped(count, rows, ny),
        in_specs=[hbm_space], out_specs=whole(1)[0],
        scratch_shapes=[pltpu.SemaphoreType.DMA((2,))],
        compiler_params=limit(2), cost_estimate=cost(0, 6 * 2**20), name="load",
    )(in_hbm(basis))
    kept, local, rows_near, rows_far = pl.pallas_call(
        window_kernel,
        out_shape=(
            pltpu.HBM((6 * nx + 16, ny), F32), shaped(2, ny),
            pltpu.HBM((2 * nz, ny), F32), pltpu.HBM((2 * nz, ny), F32),
        ),
        in_specs=[SMEM_SPEC] + whole(11), out_specs=(hbm_space, *whole(1), hbm_space, hbm_space),
        scratch_shapes=[
            VMEM((2, rows, ny), F32), VMEM((rows + 16, ny), F32), VMEM((ny, ny), F32),
            VMEM((ny, ny), F32), pltpu.SemaphoreType.DMA((5,)),
        ],
        compiler_params=limit(4), cost_estimate=cost(10**7, 4 * 2**20), name="window",
    )(
        diffusivity, near, speeds, diff_row, mine, sides_near, sides_far,
        own_up, own_down, window_near, window_far, vectors,
    )

    other = lax.ppermute(local, "c", [(0, 1), (1, 0)])
    sent = pl.pallas_call(
        spread_kernel, out_shape=shaped(chips, 2, ny), in_specs=whole(2), out_specs=whole(1)[0],
        compiler_params=limit(4), cost_estimate=cost(10**4, 2**17), name="spread",
    )(local, other)
    parts = lax.all_to_all(sent, CHIPS, 0, 0, tiled=True)

    halves = shaped(rows // 2, 2 * (count + 2), 2 * ny, dtype=BF16)
    padded = VMEM((nz * (nx + 16), ny), F32)
    tracer_next, split_halves, line = pl.pallas_call(
        lambda *refs: bulk_kernel(8, *refs),
        out_shape=(shaped(nz, nx, ny), halves, shaped(8, ny)),
        in_specs=[SMEM_SPEC] + [hbm_space] * 5 + whole(5),
        out_specs=(any_space, *whole(2)),
        scratch_shapes=[
            padded, padded, VMEM((rows, count, ny), F32), VMEM((6 * nx + 16, ny), F32),
            VMEM((2 * nz, ny), F32), VMEM((2 * nz, ny), F32), pltpu.SemaphoreType.DMA((9,)),
            pltpu.SemaphoreType.DMA((8,)), pltpu.SemaphoreType.DMA((3 + rows,)),
        ],
        compiler_params=limit(12), cost_estimate=cost(10**8, 10 * 2**20), name="bulk",
    )(
        diffusivity, in_hbm(tracer), in_hbm(basis.reshape(count, rows, 1, ny)), in_hbm(kept),
        in_hbm(rows_near), in_hbm(rows_far), velocity, diff_row, singular.reshape(1, count), sides_near, sides_far,
    )

    basis_next = pl.pallas_call(
        lambda *refs: core_kernel(rows_all, *refs),
        out_shape=shaped(count + 2, rows, ny),
        in_specs=whole(3), out_specs=pl.BlockSpec(memory_space=pl.ANY),
        scratch_shapes=[
            VMEM((count + 2, rows, ny), F32),
            pltpu.SemaphoreType.DMA((rows // 8,)),
        ],
        compiler_params=limit(16), cost_estimate=cost(10**8, 6 * 2**20), name="core",
    )(
        parts.reshape(chips // 4, 8, ny), line, split_halves,
    )
    return tracer_next, basis_next.reshape(count + 2, window, nx, ny)


def solution(mesh):
    finer = Mesh(mesh.devices.reshape(8, 4, 4, 2), ("z", "y", "x", "c"))
    in_specs = (P(None, GX, GY), P(None, GX, GY), P(), P(), P(None, None, GX, GY))
    out_specs = (P(None, GX, GY), P(None, None, GX, GY))
    return jax.shard_map(steps, mesh=finer, in_specs=in_specs, out_specs=out_specs, check_vma=False)
```

```python
import math

import jax
import jax.numpy as jnp
from jax import lax
from jax.experimental import pallas as pl
from jax.experimental.pallas import tpu as pltpu
from jax.sharding import Mesh
from jax.sharding import PartitionSpec as P


F32 = jnp.float32
BF16 = jnp.bfloat16
GX = ("z", "y")
GY = ("x", "c")
CHIPS = ("z", "y", "x")
ROOT_ITERS = 5
SHIFTS = 2**ROOT_ITERS
POLES = SHIFTS // 2 - 1
VMEM = pltpu.VMEM


def lanes_of(shape):
    return lax.broadcasted_iota(jnp.int32, shape, len(shape) - 1)


def rows_of(shape):
    return lax.broadcasted_iota(jnp.int32, shape, len(shape) - 2)


def step(c, xm, xp, ym, yp, zm, zp, d, vxp, vxn, vyp, vyn):
    spread = (xm + xp) + (ym + yp) + (zm + zp) - 6.0 * c
    carried = (vxp * (c - xm) + vxn * (xp - c)) + (vyp * (c - ym) + vyn * (yp - c))
    return c + d * spread - carried


def signed_parts(vx, vy):
    return jnp.maximum(vx, 0.0), jnp.minimum(vx, 0.0), jnp.maximum(vy, 0.0), jnp.minimum(vy, 0.0)


def before(c, ghost, axis):
    at = lax.broadcasted_iota(jnp.int32, c.shape, axis)
    return jnp.where(at == 0, ghost, pltpu.roll(c, 1, axis))


def after(c, ghost, axis):
    n = c.shape[axis]
    at = lax.broadcasted_iota(jnp.int32, c.shape, axis)
    return jnp.where(at == n - 1, ghost, pltpu.roll(c, n - 1, axis))


def gx_is_even():
    return lax.axis_index("y") % 2 == 0


def gy_is_even():
    return lax.axis_index("c") == 0


def to_pairs(even, up, down):
    return jnp.where(even, down, up), jnp.where(even, up, down)


def from_pairs(even, near, far):
    return jnp.where(even, far, near), jnp.where(even, near, far)


def pack_columns_kernel(
    chunks, tracer_hbm, by_row_hbm, velocity_hbm, near, far, window, rows_near, rows_far, mine, velocity,
    tracer, sems,
):
    nx, ny = velocity.shape[1:]
    nz = tracer.shape[0] // nx
    size = nz // chunks

    def rows_of_level(at, count, dst):
        return tracer_hbm.at[pl.ds(at * nx, count * nx)], dst

    moves = [
        rows_of_level(i * size, size, tracer.at[pl.ds(i * size * nx, size * nx)])
        for i in range(chunks)
    ]
    moves.append((velocity_hbm, velocity))
    moves.append(rows_of_level(nz - 2, 2, window.at[0 : 2 * nx]))
    moves.append(rows_of_level(0, 4, window.at[2 * nx : 6 * nx]))
    even = gx_is_even()
    for i in range(2):
        part, first, last = pl.ds(i * nz, nz), i, nx - 1 - i
        at_near, at_far = jnp.where(even, last, first), jnp.where(even, first, last)
        moves.append((by_row_hbm.at[:, at_near, 0, :], rows_near.at[part]))
        moves.append((by_row_hbm.at[:, at_far, 0, :], rows_far.at[part]))
    loads = [pltpu.make_async_copy(src, dst, sems.at[i]) for i, (src, dst) in enumerate(moves)]
    for load in loads:
        load.start()
    lane = lanes_of((nx, ny))

    def four(i, carry):
        out = []
        for j in range(4):
            z = 4 * i + j
            r = pltpu.roll(tracer[z * nx : (z + 1) * nx], z, 1)
            out.append(jnp.where(((lane - z + 2) & (ny - 1)) < 4, r, carry[j]))
        return tuple(out)

    carry = (jnp.zeros((nx, ny), F32),) * 4
    for i in range(chunks):
        loads[i].wait()
        for k in range(i * size // 4, (i + 1) * size // 4):
            carry = four(k, carry)
    phase = lane & 3

    def column(shift):
        c = [pltpu.roll(x, shift, 1) if shift else x for x in carry]
        return jnp.where(
            phase < 2, jnp.where(phase == 0, c[0], c[1]), jnp.where(phase == 2, c[2], c[3])
        )

    loads[chunks].wait()
    vx, vy = velocity[0], velocity[1]
    left = (column(0), column(ny - 1), jnp.where(lane == 0, vx, pltpu.roll(vy, 1, 1)))
    right = (
        column(1), column(2),
        jnp.where(lane == ny - 1, vx, pltpu.roll(vy, ny - 1, 1)),
    )
    even = gy_is_even()
    for i in range(3):
        near[i], far[i] = to_pairs(even, left[i], right[i])
    mine[0], mine[1] = left[0], right[0]
    for load in loads[chunks + 1 :]:
        load.wait()


def pack_rows_kernel(window, velocity, sides_near, sides_far, near, far, up, down):
    nx, ny = velocity.shape[1:]
    from_left, from_right = from_pairs(gy_is_even(), sides_near[0], sides_far[0])
    for edge, inner, out in ((0, 1, up), (nx - 1, nx - 2, down)):
        for s in range(6):
            out[s : s + 1, :] = window[s * nx + edge : s * nx + edge + 1, :]
            out[8 + s : 9 + s, :] = window[s * nx + inner : s * nx + inner + 1, :]
        for s in (6, 7, 14, 15, 20, 21, 22, 23):
            out[s : s + 1, :] = jnp.zeros((1, ny), F32)
        out[16:17, :] = velocity[0, edge : edge + 1, :]
        out[17:18, :] = velocity[1, edge : edge + 1, :]
        out[18:19, :] = from_left[edge : edge + 1, :]
        out[19:20, :] = from_right[edge : edge + 1, :]
    near[...], far[...] = to_pairs(gx_is_even(), up[...], down[...])


def window_kernel(
    diff, near, velocity, diff_row, mine, sides_near, sides_far,
    own_up, own_down, rows_near, rows_far, basis,
    kept_hbm, sums, snaps, sides, q0, q1, sems,
):
    nz, nx, ny = diff.shape[0], velocity.shape[1], velocity.shape[2]
    count = basis.shape[0]
    dz = diff_row[...]
    even = gy_is_even()
    pairs = [from_pairs(even, sides_near[i], sides_far[i]) for i in range(3)]
    from_left, from_right = [p[0] for p in pairs], [p[1] for p in pairs]
    from_up, from_down = from_pairs(gx_is_even(), rows_near[...], rows_far[...])
    for gin, inner, outer, corner, vx_at, vy_at, out in (
        (from_left, None, mine[0], 18, ny - 1, ny - 2, sides.at[0:nx]),
        (from_right, mine[1], None, 19, 0, 1, sides.at[nx : 2 * nx]),
    ):
        c = gin[0]
        ym = gin[1] if inner is None else inner
        yp = gin[1] if outer is None else outer
        vx = gin[2][:, vx_at : vx_at + 1]
        vy = gin[2][:, vy_at : vy_at + 1]
        parts = signed_parts(vx, vy)
        xm = before(c, from_up[corner : corner + 1, :], 0)
        xp = after(c, from_down[corner : corner + 1, :], 0)
        out[...] = step(c, xm, xp, ym, yp, pltpu.roll(c, 1, 1), pltpu.roll(c, nz - 1, 1), dz, *parts)

    sub = rows_of((8, ny))
    lane = lanes_of((8, ny))
    d_rows = jnp.where(sub == 2, diff[0], diff[1])
    ghost_rows = []
    for gin, own, top in ((from_up, own_up, True), (from_down, own_down, False)):
        c = gin[0:8, :]
        beyond, inside = gin[8:16, :], own[0:8, :]
        xm, xp = (beyond, inside) if top else (inside, beyond)
        west = jnp.where(sub == 2, gin[18:19, 0:1], gin[18:19, 1:2])
        east = jnp.where(sub == 2, gin[19:20, 0:1], gin[19:20, 1:2])
        parts = signed_parts(gin[16:17, :], gin[17:18, :])
        ghost_rows.append(
            step(c, xm, xp, before(c, west, 1), after(c, east, 1),
                 pltpu.roll(c, 1, 0), pltpu.roll(c, 7, 0), d_rows, *parts)
        )

    parts = signed_parts(velocity[0], velocity[1])
    u = [near[s * nx : (s + 1) * nx] for s in range(6)]
    first = []
    for s in range(1, 5):
        z = (s - 2) % nz
        c = u[s]
        xm = before(c, from_up[s : s + 1, :], 0)
        xp = after(c, from_down[s : s + 1, :], 0)
        ym = before(c, from_left[0][:, z : z + 1], 1)
        yp = after(c, from_right[0][:, z : z + 1], 1)
        first.append(step(c, xm, xp, ym, yp, u[s - 1], u[s + 1], diff[z], *parts))
    for z in range(2):
        c = first[z + 1]
        snaps[0, z * nx : (z + 1) * nx, :] = c
        xm = before(c, ghost_rows[0][z + 2 : z + 3, :], 0)
        xp = after(c, ghost_rows[1][z + 2 : z + 3, :], 0)
        ym = before(c, sides[0:nx, z : z + 1], 1)
        yp = after(c, sides[nx : 2 * nx, z : z + 1], 1)
        snaps[1, z * nx : (z + 1) * nx, :] = step(
            c, xm, xp, ym, yp, first[z], first[z + 2], diff[z], *parts
        )

    rows = 2 * nx
    pieces = rows // 8
    sides[rows : rows + 8] = from_up[16:24, :]
    sides[rows + 8 : rows + 16] = from_down[16:24, :]
    keep = [
        pltpu.make_async_copy(ref, kept_hbm.at[pl.ds(at, ref.shape[0])], sems.at[i])
        for i, (ref, at) in enumerate(
            ((snaps.at[0], 0), (snaps.at[1], rows), (sides, 2 * rows))
        )
    ]
    for copy in keep:
        copy.start()

    def folded(a, b):
        total = a[0:8, :] * b[0:8, :]
        for i in range(1, pieces):
            total = total + a[8 * i : 8 * i + 8, :] * b[8 * i : 8 * i + 8, :]
        return total

    def group(vectors, start, size):
        for m, q in enumerate((q0, q1)):
            lines = jnp.stack([folded(v, snaps[m]) for v in vectors])
            q[pl.ds(start, size), :] = jnp.sum(lines, axis=1)

    def eight(i, carry):
        at = pl.multiple_of(8 * i, 8)
        group([basis[at + j] for j in range(8)], at, 8)
        return carry

    full = count // 8 * 8
    lax.fori_loop(0, count // 8, eight, 0)
    group([basis[k] for k in range(full, count)] + [snaps[0], snaps[1]], full, count + 2 - full)
    for q in (q0, q1):
        q[count + 2 :] = jnp.zeros((ny - count - 2, ny), F32)
    ones = jnp.ones((8, ny), F32)
    over_lanes = (((1,), (1,)), ((), ()))
    for m, q in enumerate((q0, q1)):
        line = lax.dot_general(
            ones, q[...], over_lanes, precision=lax.Precision.HIGHEST, preferred_element_type=F32
        )
        sums[m : m + 1, :] = line[0:1, :]
    for copy in keep:
        copy.wait()


def split(vectors, snaps, halves):
    rows, ny = vectors.shape[0], vectors.shape[2]
    size = halves.shape[1] // 2
    for r in range(rows):
        pair, half = r // 2, r % 2
        lanes = slice(half * ny, (half + 1) * ny)
        v = jnp.concatenate(
            [vectors[r], snaps[r : r + 1, :], snaps[rows + r : rows + r + 1, :]], axis=0
        )
        hi = v.astype(BF16)
        halves[pair, :size, lanes] = hi
        halves[pair, size:, lanes] = (v - hi.astype(F32)).astype(BF16)


def load_kernel(src, dst, sems):
    parts = sems.shape[0]
    size = src.shape[0] // parts
    copies = [
        pltpu.make_async_copy(src.at[pl.ds(i * size, size)], dst.at[pl.ds(i * size, size)], sems.at[i])
        for i in range(parts)
    ]
    for copy in copies:
        copy.start()
    for copy in copies:
        copy.wait()


def level_loads(src, dst, sems, chunks, nx):
    pitch = nx + 16
    nz = src.shape[0]
    size = nz // chunks
    view = dst.reshape(nz, pitch, dst.shape[1])

    def copy(at, length, sem):
        part = pl.ds(at, length)
        return pltpu.make_async_copy(src.at[part], view.at[part, pl.ds(8, nx), :], sem)

    def chunk(k):
        return copy(k * size, size, sems.at[k])

    end = copy(nz - size, size - 1, sems.at[chunks - 1])
    last = copy(nz - 1, 1, sems.at[chunks])
    return chunk, end, last


def sweep(diff, velocity, src, dst, col_left, col_right, wait, after_block, chunks):
    nx, ny = velocity.shape[1:]
    pitch = nx + 16
    nz = src.shape[0] // pitch
    size = nz // chunks
    vx, vy = velocity[0], velocity[1]
    east, north = vx > 0.0, vy > 0.0
    speed_x, speed_y = jnp.abs(vx), jnp.abs(vy)
    stay = 1.0 - speed_x - speed_y
    lane = lanes_of((nx, ny))
    first, last = lane == 0, lane == ny - 1
    is_even = (lane & 1) == 0
    shifted = pltpu.roll(col_right, nz - 1, 1)
    columns = (jnp.where(is_even, col_left, shifted), jnp.where(is_even, shifted, col_left))

    def rows_at(z, by):
        return pl.ds(pl.multiple_of(z * pitch, 8) + 8 + by, nx)

    def turned(c, z, which):
        side = pltpu.roll(columns[which], (nz - z) & (nz - 1), 1)
        return pltpu.roll(c, 1, 1), pltpu.roll(c, ny - 1, 1), side

    def level(z, next_parity, state):
        zm, c, south, north_side, side = state
        zn = (z + 1) & (nz - 1)
        zp = src[rows_at(zn, 0), :]
        ahead = turned(zp, zn, next_parity)
        ym = jnp.where(first, side, south)
        yp = jnp.where(last, side, north_side)
        xm = src[rows_at(z, -1), :]
        xp = src[rows_at(z, 1), :]
        d = diff[z]
        moved = speed_x * jnp.where(east, xm, xp) + speed_y * jnp.where(north, ym, yp)
        spread = ((xm + xp) + (ym + yp)) + (zm + zp)
        dst[rows_at(z, 0), :] = (c * (stay - 6.0 * d) + moved) + d * spread
        return (c, zp, *ahead)

    def block(k, state):
        wait(k)
        for i in range(0, size, 2):
            z = k * size + i
            state = level(z + 1, 0, level(z, 1, state))
        after_block(k)
        return state

    c = src[rows_at(0, 0), :]
    state = (src[rows_at(nz - 1, 0), :], c, *turned(c, 0, 0))
    lax.fori_loop(0, chunks, block, state)


def level_store(src, out, sems, chunks, nx):
    pitch = nx + 16
    nz = src.shape[0] // pitch
    size = nz // chunks
    view = src.reshape(nz, pitch, src.shape[1])

    def store(k):
        part = pl.ds(k * size, size)
        return pltpu.make_async_copy(view.at[part, pl.ds(8, nx), :], out.at[part], sems.at[k])

    return store


def start_loads(loads, chunks):
    chunk, end, last = loads
    last.start()
    for k in range(chunks - 1):
        chunk(k).start()
    end.start()


def bulk_kernel(
    chunks, diff, tracer, basis, kept_hbm, rows_near, rows_far, velocity, diff_row, singular,
    sides_near, sides_far, out, halves, line, now, then, vectors, kept, got_near, got_far,
    load_sems, store_sems, sems,
):
    nz, nx, _ = tracer.shape
    pitch = nx + 16
    count = singular.shape[1]
    small = [
        pltpu.make_async_copy(src, dst, sems.at[i])
        for i, (src, dst) in enumerate(
            ((rows_near, got_near), (rows_far, got_far), (kept_hbm, kept))
        )
    ]
    for load in small:
        load.start()
    loads = level_loads(tracer, now, load_sems, chunks, nx)
    start_loads(loads, chunks)
    gathers = [
        pltpu.make_async_copy(basis.at[:, r, 0, :], vectors.at[r], sems.at[3 + r])
        for r in range(vectors.shape[0])
    ]
    for gather in gathers:
        gather.start()
    line[...] = jnp.zeros_like(line)
    line[0:1, :count] = singular[...]
    eye = rows_of((nz, nz)) == lanes_of((nz, nz))
    d_all = jnp.sum(jnp.where(eye, diff_row[...], 0.0), axis=1, keepdims=True)
    small[0].wait()
    small[1].wait()
    even = gx_is_even()
    from_up, from_down = from_pairs(even, got_near[0:nz], got_far[0:nz])
    now[pl.ds(7, nz, stride=pitch), :] = from_up
    now[pl.ds(8 + nx, nz, stride=pitch), :] = from_down
    chunk, end, final = loads
    final.wait()
    chunk(0).wait()

    def wait(k):
        @pl.when(k < chunks - 2)
        def _():
            chunk(k + 1).wait()

        @pl.when(k == chunks - 2)
        def _():
            end.wait()

    from_left, from_right = from_pairs(gy_is_even(), sides_near[0], sides_far[0])
    sweep(diff, velocity, now, then, from_left, from_right, wait, lambda k: None, chunks)
    small[2].wait()
    nearest = from_pairs(even, got_near[0:nz], got_far[0:nz])
    beyonds = from_pairs(even, got_near[nz:], got_far[nz:])
    for is_top, c, beyond, at in zip((True, False), nearest, beyonds, (6 * nx, 6 * nx + 8)):
        gin = kept[at : at + 8, :]
        inside = now[pl.ds(8 if is_top else 7 + nx, nz, stride=pitch), :]
        xm, xp = (beyond, inside) if is_top else (inside, beyond)
        west = jnp.sum(jnp.where(eye, gin[2:3, :], 0.0), axis=1, keepdims=True)
        east = jnp.sum(jnp.where(eye, gin[3:4, :], 0.0), axis=1, keepdims=True)
        parts = signed_parts(gin[0:1, :], gin[1:2, :])
        then[pl.ds(7 if is_top else 8 + nx, nz, stride=pitch), :] = step(
            c, xm, xp, before(c, west, 1), after(c, east, 1),
            pltpu.roll(c, 1, 0), pltpu.roll(c, nz - 1, 0), d_all, *parts
        )
    store = level_store(now, out, store_sems, chunks, nx)
    col_left, col_right = kept[4 * nx : 5 * nx, :], kept[5 * nx : 6 * nx, :]
    sweep(
        diff, velocity, then, now, col_left, col_right, lambda k: None,
        lambda k: store(k).start(), chunks,
    )
    for gather in gathers:
        gather.wait()
    split(vectors, kept, halves)
    for k in range(chunks):
        store(k).wait()


def spread_kernel(mine, other, out):
    both = mine[...] + other[...]
    out[...] = jnp.broadcast_to(both[None], out.shape)


def core_kernel(rows_all, parts, singular, halves, out, block, sems):
    count = out.shape[0] - 2
    n = parts.shape[2]
    total = jnp.sum(parts[...], axis=0)
    total = total + pltpu.roll(total, 2, 0)
    total = total + pltpu.roll(total, 4, 0)
    total = total * (1.0 / rows_all)
    lane = lanes_of((1, n))
    zero = jnp.zeros((1, n), F32)

    def add(x):
        return jnp.sum(x, axis=1, keepdims=True)

    def pick(x, at):
        return add(jnp.where(lane == at, x, zero))

    p0 = jnp.where(lane < count, total[0:1, :], zero)
    p1 = jnp.where(lane < count, total[1:2, :], zero)
    g00 = pick(total[0:1, :], count) - add(p0 * p0) + 1e-06
    g01 = pick(total[0:1, :], count + 1) - add(p0 * p1)
    g11 = pick(total[1:2, :], count + 1) - add(p1 * p1) + 1e-06
    r11 = jnp.sqrt(g00)
    r12 = g01 / r11
    r22 = jnp.sqrt(g11 - r12 * r12)
    u0 = jnp.where(lane == count, r11, p0)
    u1 = jnp.where(lane == count, r12, jnp.where(lane == count + 1, r22, p1))
    s = singular[0:1, :]
    squares = s * s
    sigma = add(squares + u0 * u0 + u1 * u1) / (count + 2)
    root = jnp.sqrt(sigma)
    d = squares / sigma
    v0 = u0 / root
    v1 = u1 / root

    half = POLES + 1
    row = rows_of((half, n))
    pole = jnp.zeros((half, n), F32)
    for j in range(POLES):
        pole = jnp.where(row == j, math.tan(math.pi * (j + 1) / SHIFTS) ** 2, pole)
    last = row == POLES
    pole = jnp.where(last, 1.0, pole)
    inverse = jnp.where(last, 1.0, 1.0 / (d + pole))
    weight = 2.0 * (1.0 + pole)
    w0 = inverse * v0
    w1 = inverse * v1
    last_one = last[:, 0:1]
    a = jnp.where(last_one, 1.0, 1.0 + add(w0 * v0))
    b = jnp.where(last_one, 0.0, add(w0 * v1))
    c = jnp.where(last_one, 1.0, 1.0 + add(w1 * v1))
    e = b / a
    c = c - b * e
    strength = jnp.where(last, 1.0, weight * pole)
    w1 = jnp.sqrt(strength / c) * (w1 - e * w0)
    w0 = jnp.sqrt(strength / a) * w0
    low_rank = jnp.concatenate([w0, w1], axis=0)
    gains = 1.0 + d + jnp.sum(jnp.where(last, 0.0, weight * d * inverse), axis=0, keepdims=True)
    square = (n, n)
    core = lax.dot_general(
        low_rank, low_rank, (((0,), (0,)), ((), ())),
        precision=lax.Precision.HIGHEST, preferred_element_type=F32,
    )
    core = core + jnp.where(rows_of(square) == lanes_of(square), gains, 0.0)
    core = core * (root * (1.0 / SHIFTS))
    t0 = jnp.where(lane == count, 1.0, -p0) / r11
    q_lane = jnp.where(lane == count + 1, 1.0, -p1)
    t1 = (q_lane - r12 * t0) / r22
    full = jnp.where(lanes_of(square) < count, core, 0.0)
    full = full + core[:, count : count + 1] * t0 + core[:, count + 1 : count + 2] * t1
    full = full[: count + 2, : count + 2]
    hi = full.astype(BF16)
    lo = (full - hi.astype(F32)).astype(BF16)
    twice = jnp.concatenate([hi, hi], axis=1)
    size = count + 2
    blocks = block.shape[1] // 8
    copies = []
    for b in range(blocks):
        tiles = []
        for pair in range(4 * b, 4 * b + 4):
            r = jnp.dot(twice, halves[pair], preferred_element_type=F32)
            r = r + jnp.dot(lo, halves[pair, :size], preferred_element_type=F32)
            tiles.append(r[:, :n])
            tiles.append(r[:, n:])
        block[:, 8 * b : 8 * b + 8, :] = jnp.swapaxes(jnp.stack(tiles), 0, 1)
        copy = pltpu.make_async_copy(
            block.at[:, pl.ds(8 * b, 8), :], out.at[:, pl.ds(8 * b, 8), :], sems.at[b]
        )
        copy.start()
        copies.append(copy)
    for copy in copies:
        copy.wait()


def whole(n):
    return [pl.BlockSpec(memory_space=VMEM)] * n


SMEM_SPEC = pl.BlockSpec(memory_space=pltpu.SMEM)


def shaped(*shape, dtype=F32):
    return jax.ShapeDtypeStruct(shape, dtype)


def in_hbm(x):
    return pltpu.with_memory_space_constraint(x, pltpu.HBM)


def cost(flops, moved):
    return pl.CostEstimate(flops=flops, bytes_accessed=moved, transcendentals=0)


def limit(mib):
    return pltpu.CompilerParams(vmem_limit_bytes=mib * 2**20)


def swap(x, axes, far):
    count = lax.axis_size(axes)
    shift = 1 if far else 0
    pairs = [((i + shift) % count, ((i ^ 1) + shift) % count) for i in range(count)]
    return lax.ppermute(x, axes, pairs)


def steps(tracer, velocity, diffusivity, singular, basis_vectors):
    nz, nx, ny = tracer.shape
    count, window = basis_vectors.shape[:2]
    rows = window * nx
    basis = basis_vectors.reshape(count, rows, ny)
    rows_all = rows * ny * lax.axis_size(GX) * lax.axis_size(GY)
    chips = lax.axis_size(CHIPS)
    diff_row = diffusivity.reshape(1, nz)

    columns = shaped(3, nx, ny)
    bulk_rows = shaped(2 * nz, ny)
    hbm_space, any_space = (pl.BlockSpec(memory_space=m) for m in (pltpu.HBM, pl.ANY))
    columns_near, columns_far, near, sent_near, sent_far, mine, speeds = pl.pallas_call(
        lambda *refs: pack_columns_kernel(4, *refs),
        out_shape=(
            columns, columns, shaped(6 * nx, ny), bulk_rows, bulk_rows, shaped(2, nx, ny),
            shaped(2, nx, ny),
        ),
        in_specs=[hbm_space] * 3, out_specs=tuple(whole(7)),
        scratch_shapes=[
            VMEM((nz * nx, ny), F32), pltpu.SemaphoreType.DMA((11,)),
        ],
        compiler_params=limit(4), cost_estimate=cost(10**6, 2 * 2**20), name="columns",
    )(
        in_hbm(tracer.reshape(nz * nx, ny)), in_hbm(tracer.reshape(nz, nx, 1, ny)), in_hbm(velocity)
    )
    sides_far = swap(columns_far, GY, True)
    sides_near = swap(columns_near, GY, False)
    edge = shaped(24, ny)
    edges_near, edges_far, own_up, own_down = pl.pallas_call(
        pack_rows_kernel, out_shape=(edge,) * 4, in_specs=whole(4), out_specs=tuple(whole(4)),
        compiler_params=limit(2), cost_estimate=cost(10**4, 2**17), name="edges",
    )(near, speeds, sides_near, sides_far)
    window_far = swap(edges_far, GX, True)
    window_near = swap(edges_near, GX, False)

    rows_far = in_hbm(swap(in_hbm(sent_far), GX, True))
    rows_near = in_hbm(swap(in_hbm(sent_near), GX, False))

    vectors = pl.pallas_call(
        load_kernel, out_shape=shaped(count, rows, ny),
        in_specs=[hbm_space], out_specs=whole(1)[0],
        scratch_shapes=[pltpu.SemaphoreType.DMA((2,))],
        compiler_params=limit(2), cost_estimate=cost(0, 6 * 2**20), name="load",
    )(in_hbm(basis))
    kept, local = pl.pallas_call(
        window_kernel,
        out_shape=(pltpu.HBM((6 * nx + 16, ny), F32), shaped(2, ny)),
        in_specs=[SMEM_SPEC] + whole(11), out_specs=(hbm_space, *whole(1)),
        scratch_shapes=[
            VMEM((2, rows, ny), F32), VMEM((rows + 16, ny), F32), VMEM((ny, ny), F32),
            VMEM((ny, ny), F32), pltpu.SemaphoreType.DMA((3,)),
        ],
        compiler_params=limit(4), cost_estimate=cost(10**7, 4 * 2**20), name="window",
    )(
        diffusivity, near, speeds, diff_row, mine, sides_near, sides_far,
        own_up, own_down, window_near, window_far, vectors,
    )

    other = lax.ppermute(local, "c", [(0, 1), (1, 0)])
    sent = pl.pallas_call(
        spread_kernel, out_shape=shaped(chips, 2, ny), in_specs=whole(2), out_specs=whole(1)[0],
        compiler_params=limit(4), cost_estimate=cost(10**4, 2**17), name="spread",
    )(local, other)
    parts = lax.all_to_all(sent, CHIPS, 0, 0, tiled=True)

    halves = shaped(rows // 2, 2 * (count + 2), 2 * ny, dtype=BF16)
    padded = VMEM((nz * (nx + 16), ny), F32)
    tracer_next, split_halves, line = pl.pallas_call(
        lambda *refs: bulk_kernel(8, *refs),
        out_shape=(shaped(nz, nx, ny), halves, shaped(8, ny)),
        in_specs=[SMEM_SPEC] + [hbm_space] * 5 + whole(5),
        out_specs=(any_space, *whole(2)),
        scratch_shapes=[
            padded, padded, VMEM((rows, count, ny), F32), VMEM((6 * nx + 16, ny), F32),
            VMEM((2 * nz, ny), F32), VMEM((2 * nz, ny), F32), pltpu.SemaphoreType.DMA((9,)),
            pltpu.SemaphoreType.DMA((8,)), pltpu.SemaphoreType.DMA((3 + rows,)),
        ],
        compiler_params=limit(12), cost_estimate=cost(10**8, 10 * 2**20), name="bulk",
    )(
        diffusivity, in_hbm(tracer), in_hbm(basis.reshape(count, rows, 1, ny)), in_hbm(kept),
        in_hbm(rows_near), in_hbm(rows_far), velocity, diff_row, singular.reshape(1, count), sides_near, sides_far,
    )

    basis_next = pl.pallas_call(
        lambda *refs: core_kernel(rows_all, *refs),
        out_shape=shaped(count + 2, rows, ny),
        in_specs=whole(3), out_specs=pl.BlockSpec(memory_space=pl.ANY),
        scratch_shapes=[
            VMEM((count + 2, rows, ny), F32),
            pltpu.SemaphoreType.DMA((rows // 8,)),
        ],
        compiler_params=limit(16), cost_estimate=cost(10**8, 6 * 2**20), name="core",
    )(
        parts.reshape(chips // 4, 8, ny), line, split_halves,
    )
    return tracer_next, basis_next.reshape(count + 2, window, nx, ny)


def solution(mesh):
    finer = Mesh(mesh.devices.reshape(8, 4, 4, 2), ("z", "y", "x", "c"))
    in_specs = (P(None, GX, GY), P(None, GX, GY), P(), P(), P(None, None, GX, GY))
    out_specs = (P(None, GX, GY), P(None, None, GX, GY))
    return jax.shard_map(steps, mesh=finer, in_specs=in_specs, out_specs=out_specs, check_vma=False)
```

```python
import math

import jax
import jax.numpy as jnp
from jax import lax
from jax.experimental import pallas as pl
from jax.experimental.pallas import tpu as pltpu
from jax.sharding import Mesh
from jax.sharding import PartitionSpec as P


F32 = jnp.float32
BF16 = jnp.bfloat16
GX = ("z", "y")
GY = ("x", "c")
CHIPS = ("z", "y", "x")
ROOT_ITERS = 5
SHIFTS = 2**ROOT_ITERS
POLES = SHIFTS // 2 - 1
VMEM = pltpu.VMEM


def lanes_of(shape):
    return lax.broadcasted_iota(jnp.int32, shape, len(shape) - 1)


def rows_of(shape):
    return lax.broadcasted_iota(jnp.int32, shape, len(shape) - 2)


def step(c, xm, xp, ym, yp, zm, zp, d, vxp, vxn, vyp, vyn):
    spread = (xm + xp) + (ym + yp) + (zm + zp) - 6.0 * c
    carried = (vxp * (c - xm) + vxn * (xp - c)) + (vyp * (c - ym) + vyn * (yp - c))
    return c + d * spread - carried


def signed_parts(vx, vy):
    return jnp.maximum(vx, 0.0), jnp.minimum(vx, 0.0), jnp.maximum(vy, 0.0), jnp.minimum(vy, 0.0)


def before(c, ghost, axis):
    at = lax.broadcasted_iota(jnp.int32, c.shape, axis)
    return jnp.where(at == 0, ghost, pltpu.roll(c, 1, axis))


def after(c, ghost, axis):
    n = c.shape[axis]
    at = lax.broadcasted_iota(jnp.int32, c.shape, axis)
    return jnp.where(at == n - 1, ghost, pltpu.roll(c, n - 1, axis))


def gx_is_even():
    return lax.axis_index("y") % 2 == 0


def gy_is_even():
    return lax.axis_index("c") == 0


def to_pairs(even, up, down):
    return jnp.where(even, down, up), jnp.where(even, up, down)


def from_pairs(even, near, far):
    return jnp.where(even, far, near), jnp.where(even, near, far)


def pack_columns_kernel(
    chunks, tracer_hbm, by_row_hbm, velocity_hbm, near, far, window, rows_near, rows_far, mine, velocity,
    tracer, sems,
):
    nx, ny = velocity.shape[1:]
    nz = tracer.shape[0] // nx
    size = nz // chunks

    def rows_of_level(at, count, dst):
        return tracer_hbm.at[pl.ds(at * nx, count * nx)], dst

    moves = [
        rows_of_level(i * size, size, tracer.at[pl.ds(i * size * nx, size * nx)])
        for i in range(chunks)
    ]
    moves.append((velocity_hbm, velocity))
    moves.append(rows_of_level(nz - 2, 2, window.at[0 : 2 * nx]))
    moves.append(rows_of_level(0, 4, window.at[2 * nx : 6 * nx]))
    even = gx_is_even()
    for i in range(2):
        part, first, last = pl.ds(i * nz, nz), i, nx - 1 - i
        at_near, at_far = jnp.where(even, last, first), jnp.where(even, first, last)
        moves.append((by_row_hbm.at[:, at_near, 0, :], rows_near.at[part]))
        moves.append((by_row_hbm.at[:, at_far, 0, :], rows_far.at[part]))
    loads = [pltpu.make_async_copy(src, dst, sems.at[i]) for i, (src, dst) in enumerate(moves)]
    for load in loads:
        load.start()
    lane = lanes_of((nx, ny))

    def four(i, carry):
        out = []
        for j in range(4):
            z = 4 * i + j
            r = pltpu.roll(tracer[z * nx : (z + 1) * nx], z, 1)
            out.append(jnp.where(((lane - z + 2) & (ny - 1)) < 4, r, carry[j]))
        return tuple(out)

    carry = (jnp.zeros((nx, ny), F32),) * 4
    for i in range(chunks):
        loads[i].wait()
        for k in range(i * size // 4, (i + 1) * size // 4):
            carry = four(k, carry)
    phase = lane & 3

    def column(shift):
        c = [pltpu.roll(x, shift, 1) if shift else x for x in carry]
        return jnp.where(
            phase < 2, jnp.where(phase == 0, c[0], c[1]), jnp.where(phase == 2, c[2], c[3])
        )

    loads[chunks].wait()
    vx, vy = velocity[0], velocity[1]
    left = (column(0), column(ny - 1), jnp.where(lane == 0, vx, pltpu.roll(vy, 1, 1)))
    right = (
        column(1), column(2),
        jnp.where(lane == ny - 1, vx, pltpu.roll(vy, ny - 1, 1)),
    )
    even = gy_is_even()
    for i in range(3):
        near[i], far[i] = to_pairs(even, left[i], right[i])
    mine[0], mine[1] = left[0], right[0]
    for load in loads[chunks + 1 :]:
        load.wait()


def pack_rows_kernel(window, velocity, sides_near, sides_far, near, far, up, down):
    nx, ny = velocity.shape[1:]
    from_left, from_right = from_pairs(gy_is_even(), sides_near[0], sides_far[0])
    for edge, inner, out in ((0, 1, up), (nx - 1, nx - 2, down)):
        for s in range(6):
            out[s : s + 1, :] = window[s * nx + edge : s * nx + edge + 1, :]
            out[8 + s : 9 + s, :] = window[s * nx + inner : s * nx + inner + 1, :]
        for s in (6, 7, 14, 15, 20, 21, 22, 23):
            out[s : s + 1, :] = jnp.zeros((1, ny), F32)
        out[16:17, :] = velocity[0, edge : edge + 1, :]
        out[17:18, :] = velocity[1, edge : edge + 1, :]
        out[18:19, :] = from_left[edge : edge + 1, :]
        out[19:20, :] = from_right[edge : edge + 1, :]
    near[...], far[...] = to_pairs(gx_is_even(), up[...], down[...])


def window_kernel(
    diff, near, velocity, diff_row, mine, sides_near, sides_far,
    own_up, own_down, rows_near, rows_far, basis,
    kept_hbm, sums, snaps, sides, q0, q1, sems,
):
    nz, nx, ny = diff.shape[0], velocity.shape[1], velocity.shape[2]
    count = basis.shape[0]
    dz = diff_row[...]
    even = gy_is_even()
    pairs = [from_pairs(even, sides_near[i], sides_far[i]) for i in range(3)]
    from_left, from_right = [p[0] for p in pairs], [p[1] for p in pairs]
    from_up, from_down = from_pairs(gx_is_even(), rows_near[...], rows_far[...])
    for gin, inner, outer, corner, vx_at, vy_at, out in (
        (from_left, None, mine[0], 18, ny - 1, ny - 2, sides.at[0:nx]),
        (from_right, mine[1], None, 19, 0, 1, sides.at[nx : 2 * nx]),
    ):
        c = gin[0]
        ym = gin[1] if inner is None else inner
        yp = gin[1] if outer is None else outer
        vx = gin[2][:, vx_at : vx_at + 1]
        vy = gin[2][:, vy_at : vy_at + 1]
        parts = signed_parts(vx, vy)
        xm = before(c, from_up[corner : corner + 1, :], 0)
        xp = after(c, from_down[corner : corner + 1, :], 0)
        out[...] = step(c, xm, xp, ym, yp, pltpu.roll(c, 1, 1), pltpu.roll(c, nz - 1, 1), dz, *parts)

    sub = rows_of((8, ny))
    lane = lanes_of((8, ny))
    d_rows = jnp.where(sub == 2, diff[0], diff[1])
    ghost_rows = []
    for gin, own, top in ((from_up, own_up, True), (from_down, own_down, False)):
        c = gin[0:8, :]
        beyond, inside = gin[8:16, :], own[0:8, :]
        xm, xp = (beyond, inside) if top else (inside, beyond)
        west = jnp.where(sub == 2, gin[18:19, 0:1], gin[18:19, 1:2])
        east = jnp.where(sub == 2, gin[19:20, 0:1], gin[19:20, 1:2])
        parts = signed_parts(gin[16:17, :], gin[17:18, :])
        ghost_rows.append(
            step(c, xm, xp, before(c, west, 1), after(c, east, 1),
                 pltpu.roll(c, 1, 0), pltpu.roll(c, 7, 0), d_rows, *parts)
        )

    parts = signed_parts(velocity[0], velocity[1])
    u = [near[s * nx : (s + 1) * nx] for s in range(6)]
    first = []
    for s in range(1, 5):
        z = (s - 2) % nz
        c = u[s]
        xm = before(c, from_up[s : s + 1, :], 0)
        xp = after(c, from_down[s : s + 1, :], 0)
        ym = before(c, from_left[0][:, z : z + 1], 1)
        yp = after(c, from_right[0][:, z : z + 1], 1)
        first.append(step(c, xm, xp, ym, yp, u[s - 1], u[s + 1], diff[z], *parts))
    for z in range(2):
        c = first[z + 1]
        snaps[0, z * nx : (z + 1) * nx, :] = c
        xm = before(c, ghost_rows[0][z + 2 : z + 3, :], 0)
        xp = after(c, ghost_rows[1][z + 2 : z + 3, :], 0)
        ym = before(c, sides[0:nx, z : z + 1], 1)
        yp = after(c, sides[nx : 2 * nx, z : z + 1], 1)
        snaps[1, z * nx : (z + 1) * nx, :] = step(
            c, xm, xp, ym, yp, first[z], first[z + 2], diff[z], *parts
        )

    rows = 2 * nx
    pieces = rows // 8
    sides[rows : rows + 8] = from_up[16:24, :]
    sides[rows + 8 : rows + 16] = from_down[16:24, :]
    keep = [
        pltpu.make_async_copy(ref, kept_hbm.at[pl.ds(at, ref.shape[0])], sems.at[i])
        for i, (ref, at) in enumerate(
            ((snaps.at[0], 0), (snaps.at[1], rows), (sides, 2 * rows))
        )
    ]
    for copy in keep:
        copy.start()

    def folded(a, b):
        total = a[0:8, :] * b[0:8, :]
        for i in range(1, pieces):
            total = total + a[8 * i : 8 * i + 8, :] * b[8 * i : 8 * i + 8, :]
        return total

    def group(vectors, start, size):
        for m, q in enumerate((q0, q1)):
            lines = jnp.stack([folded(v, snaps[m]) for v in vectors])
            q[pl.ds(start, size), :] = jnp.sum(lines, axis=1)

    def eight(i, carry):
        at = pl.multiple_of(8 * i, 8)
        group([basis[at + j] for j in range(8)], at, 8)
        return carry

    full = count // 8 * 8
    lax.fori_loop(0, count // 8, eight, 0)
    group([basis[k] for k in range(full, count)] + [snaps[0], snaps[1]], full, count + 2 - full)
    for q in (q0, q1):
        q[count + 2 :] = jnp.zeros((ny - count - 2, ny), F32)
    ones = jnp.ones((8, ny), F32)
    over_lanes = (((1,), (1,)), ((), ()))
    for m, q in enumerate((q0, q1)):
        line = lax.dot_general(
            ones, q[...], over_lanes, precision=lax.Precision.HIGHEST, preferred_element_type=F32
        )
        sums[m : m + 1, :] = line[0:1, :]
    for copy in keep:
        copy.wait()


def split(vectors, snaps, halves):
    rows, ny = vectors.shape[0], vectors.shape[2]
    size = halves.shape[1] // 2
    for r in range(rows):
        pair, half = r // 2, r % 2
        lanes = slice(half * ny, (half + 1) * ny)
        v = jnp.concatenate(
            [vectors[r], snaps[r : r + 1, :], snaps[rows + r : rows + r + 1, :]], axis=0
        )
        hi = v.astype(BF16)
        halves[pair, :size, lanes] = hi
        halves[pair, size:, lanes] = (v - hi.astype(F32)).astype(BF16)


def load_kernel(src, dst, sems):
    parts = sems.shape[0]
    size = src.shape[0] // parts
    copies = [
        pltpu.make_async_copy(src.at[pl.ds(i * size, size)], dst.at[pl.ds(i * size, size)], sems.at[i])
        for i in range(parts)
    ]
    for copy in copies:
        copy.start()
    for copy in copies:
        copy.wait()


def level_loads(src, dst, sems, chunks, nx):
    pitch = nx + 16
    nz = src.shape[0]
    size = nz // chunks
    view = dst.reshape(nz, pitch, dst.shape[1])

    def copy(at, length, sem):
        part = pl.ds(at, length)
        return pltpu.make_async_copy(src.at[part], view.at[part, pl.ds(8, nx), :], sem)

    def chunk(k):
        return copy(k * size, size, sems.at[k])

    end = copy(nz - size, size - 1, sems.at[chunks - 1])
    last = copy(nz - 1, 1, sems.at[chunks])
    return chunk, end, last


def sweep(diff, velocity, src, dst, col_left, col_right, wait, after_block, chunks):
    nx, ny = velocity.shape[1:]
    pitch = nx + 16
    nz = src.shape[0] // pitch
    size = nz // chunks
    vx, vy = velocity[0], velocity[1]
    east, north = vx > 0.0, vy > 0.0
    speed_x, speed_y = jnp.abs(vx), jnp.abs(vy)
    stay = 1.0 - speed_x - speed_y
    lane = lanes_of((nx, ny))
    first, last = lane == 0, lane == ny - 1
    is_even = (lane & 1) == 0
    shifted = pltpu.roll(col_right, nz - 1, 1)
    columns = (jnp.where(is_even, col_left, shifted), jnp.where(is_even, shifted, col_left))

    def rows_at(z, by):
        return pl.ds(pl.multiple_of(z * pitch, 8) + 8 + by, nx)

    def turned(c, z, which):
        side = pltpu.roll(columns[which], (nz - z) & (nz - 1), 1)
        return pltpu.roll(c, 1, 1), pltpu.roll(c, ny - 1, 1), side

    def level(z, next_parity, state):
        zm, c, south, north_side, side = state
        zn = (z + 1) & (nz - 1)
        zp = src[rows_at(zn, 0), :]
        ahead = turned(zp, zn, next_parity)
        ym = jnp.where(first, side, south)
        yp = jnp.where(last, side, north_side)
        xm = src[rows_at(z, -1), :]
        xp = src[rows_at(z, 1), :]
        d = diff[z]
        moved = speed_x * jnp.where(east, xm, xp) + speed_y * jnp.where(north, ym, yp)
        spread = ((xm + xp) + (ym + yp)) + (zm + zp)
        dst[rows_at(z, 0), :] = (c * (stay - 6.0 * d) + moved) + d * spread
        return (c, zp, *ahead)

    def block(k, state):
        wait(k)
        for i in range(0, size, 2):
            z = k * size + i
            state = level(z + 1, 0, level(z, 1, state))
        after_block(k)
        return state

    c = src[rows_at(0, 0), :]
    state = (src[rows_at(nz - 1, 0), :], c, *turned(c, 0, 0))
    lax.fori_loop(0, chunks, block, state)


def level_store(src, out, sems, chunks, nx):
    pitch = nx + 16
    nz = src.shape[0] // pitch
    size = nz // chunks
    view = src.reshape(nz, pitch, src.shape[1])

    def store(k):
        part = pl.ds(k * size, size)
        return pltpu.make_async_copy(view.at[part, pl.ds(8, nx), :], out.at[part], sems.at[k])

    return store


def start_loads(loads, chunks):
    chunk, end, last = loads
    last.start()
    for k in range(chunks - 1):
        chunk(k).start()
    end.start()


def bulk_kernel(
    chunks, diff, tracer, basis, kept_hbm, rows_near, rows_far, velocity, diff_row, singular,
    sides_near, sides_far, out, halves, line, now, then, vectors, kept, got_near, got_far,
    load_sems, store_sems, sems,
):
    nz, nx, _ = tracer.shape
    pitch = nx + 16
    count = singular.shape[1]
    small = [
        pltpu.make_async_copy(src, dst, sems.at[i])
        for i, (src, dst) in enumerate(
            ((rows_near, got_near), (rows_far, got_far), (kept_hbm, kept))
        )
    ]
    for load in small:
        load.start()
    loads = level_loads(tracer, now, load_sems, chunks, nx)
    start_loads(loads, chunks)
    gathers = [
        pltpu.make_async_copy(basis.at[:, r, 0, :], vectors.at[r], sems.at[3 + r])
        for r in range(vectors.shape[0])
    ]
    for gather in gathers:
        gather.start()
    line[...] = jnp.zeros_like(line)
    line[0:1, :count] = singular[...]
    eye = rows_of((nz, nz)) == lanes_of((nz, nz))
    d_all = jnp.sum(jnp.where(eye, diff_row[...], 0.0), axis=1, keepdims=True)
    small[0].wait()
    small[1].wait()
    even = gx_is_even()
    from_up, from_down = from_pairs(even, got_near[0:nz], got_far[0:nz])
    now[pl.ds(7, nz, stride=pitch), :] = from_up
    now[pl.ds(8 + nx, nz, stride=pitch), :] = from_down
    chunk, end, final = loads
    final.wait()
    chunk(0).wait()

    def wait(k):
        @pl.when(k < chunks - 2)
        def _():
            chunk(k + 1).wait()

        @pl.when(k == chunks - 2)
        def _():
            end.wait()

    from_left, from_right = from_pairs(gy_is_even(), sides_near[0], sides_far[0])
    sweep(diff, velocity, now, then, from_left, from_right, wait, lambda k: None, chunks)
    small[2].wait()
    nearest = from_pairs(even, got_near[0:nz], got_far[0:nz])
    beyonds = from_pairs(even, got_near[nz:], got_far[nz:])
    for is_top, c, beyond, at in zip((True, False), nearest, beyonds, (6 * nx, 6 * nx + 8)):
        gin = kept[at : at + 8, :]
        inside = now[pl.ds(8 if is_top else 7 + nx, nz, stride=pitch), :]
        xm, xp = (beyond, inside) if is_top else (inside, beyond)
        west = jnp.sum(jnp.where(eye, gin[2:3, :], 0.0), axis=1, keepdims=True)
        east = jnp.sum(jnp.where(eye, gin[3:4, :], 0.0), axis=1, keepdims=True)
        parts = signed_parts(gin[0:1, :], gin[1:2, :])
        then[pl.ds(7 if is_top else 8 + nx, nz, stride=pitch), :] = step(
            c, xm, xp, before(c, west, 1), after(c, east, 1),
            pltpu.roll(c, 1, 0), pltpu.roll(c, nz - 1, 0), d_all, *parts
        )
    store = level_store(now, out, store_sems, chunks, nx)
    col_left, col_right = kept[4 * nx : 5 * nx, :], kept[5 * nx : 6 * nx, :]
    sweep(
        diff, velocity, then, now, col_left, col_right, lambda k: None,
        lambda k: store(k).start(), chunks,
    )
    for gather in gathers:
        gather.wait()
    split(vectors, kept, halves)
    for k in range(chunks):
        store(k).wait()


def spread_kernel(mine, other, out):
    both = mine[...] + other[...]
    out[...] = jnp.broadcast_to(both[None], out.shape)


def core_kernel(rows_all, parts, singular, halves, out, block, sems):
    count = out.shape[0] - 2
    n = parts.shape[2]
    total = jnp.sum(parts[...], axis=0)
    total = total + pltpu.roll(total, 2, 0)
    total = total + pltpu.roll(total, 4, 0)
    total = total * (1.0 / rows_all)
    lane = lanes_of((1, n))
    zero = jnp.zeros((1, n), F32)

    def add(x):
        return jnp.sum(x, axis=1, keepdims=True)

    def pick(x, at):
        return add(jnp.where(lane == at, x, zero))

    p0 = jnp.where(lane < count, total[0:1, :], zero)
    p1 = jnp.where(lane < count, total[1:2, :], zero)
    g00 = pick(total[0:1, :], count) - add(p0 * p0) + 1e-06
    g01 = pick(total[0:1, :], count + 1) - add(p0 * p1)
    g11 = pick(total[1:2, :], count + 1) - add(p1 * p1) + 1e-06
    r11 = jnp.sqrt(g00)
    r12 = g01 / r11
    r22 = jnp.sqrt(g11 - r12 * r12)
    u0 = jnp.where(lane == count, r11, p0)
    u1 = jnp.where(lane == count, r12, jnp.where(lane == count + 1, r22, p1))
    s = singular[0:1, :]
    squares = s * s
    sigma = add(squares + u0 * u0 + u1 * u1) / (count + 2)
    root = jnp.sqrt(sigma)
    d = squares / sigma
    v0 = u0 / root
    v1 = u1 / root

    half = POLES + 1
    row = rows_of((half, n))
    pole = jnp.zeros((half, n), F32)
    for j in range(POLES):
        pole = jnp.where(row == j, math.tan(math.pi * (j + 1) / SHIFTS) ** 2, pole)
    last = row == POLES
    pole = jnp.where(last, 1.0, pole)
    inverse = jnp.where(last, 1.0, 1.0 / (d + pole))
    weight = 2.0 * (1.0 + pole)
    w0 = inverse * v0
    w1 = inverse * v1
    last_one = last[:, 0:1]
    a = jnp.where(last_one, 1.0, 1.0 + add(w0 * v0))
    b = jnp.where(last_one, 0.0, add(w0 * v1))
    c = jnp.where(last_one, 1.0, 1.0 + add(w1 * v1))
    e = b / a
    c = c - b * e
    strength = jnp.where(last, 1.0, weight * pole)
    w1 = jnp.sqrt(strength / c) * (w1 - e * w0)
    w0 = jnp.sqrt(strength / a) * w0
    low_rank = jnp.concatenate([w0, w1], axis=0)
    gains = 1.0 + d + jnp.sum(jnp.where(last, 0.0, weight * d * inverse), axis=0, keepdims=True)
    square = (n, n)
    core = lax.dot_general(
        low_rank, low_rank, (((0,), (0,)), ((), ())),
        precision=lax.Precision.HIGHEST, preferred_element_type=F32,
    )
    core = core + jnp.where(rows_of(square) == lanes_of(square), gains, 0.0)
    core = core * (root * (1.0 / SHIFTS))
    t0 = jnp.where(lane == count, 1.0, -p0) / r11
    q_lane = jnp.where(lane == count + 1, 1.0, -p1)
    t1 = (q_lane - r12 * t0) / r22
    full = jnp.where(lanes_of(square) < count, core, 0.0)
    full = full + core[:, count : count + 1] * t0 + core[:, count + 1 : count + 2] * t1
    full = full[: count + 2, : count + 2]
    hi = full.astype(BF16)
    lo = (full - hi.astype(F32)).astype(BF16)
    stacked = jnp.concatenate(
        [jnp.concatenate([hi, hi], axis=1), jnp.concatenate([lo, jnp.zeros_like(lo)], axis=1)], axis=0
    )
    size = count + 2

    def row_copy(at):
        return pltpu.make_async_copy(block.at[at], out.at[:, at, 0, :], sems.at[at])

    def product(pair, carry):
        r = jnp.dot(stacked, halves[pair], preferred_element_type=F32)
        r = r[:size] + r[size:]
        for half in range(2):
            at = 2 * pair + half
            block[at] = r[:, half * n : (half + 1) * n]
            row_copy(at).start()
        return carry

    pairs = halves.shape[0]
    lax.fori_loop(0, pairs, product, 0, unroll=8)
    for at in range(2 * pairs):
        row_copy(at).wait()


def whole(n):
    return [pl.BlockSpec(memory_space=VMEM)] * n


SMEM_SPEC = pl.BlockSpec(memory_space=pltpu.SMEM)


def shaped(*shape, dtype=F32):
    return jax.ShapeDtypeStruct(shape, dtype)


def in_hbm(x):
    return pltpu.with_memory_space_constraint(x, pltpu.HBM)


def cost(flops, moved):
    return pl.CostEstimate(flops=flops, bytes_accessed=moved, transcendentals=0)


def limit(mib):
    return pltpu.CompilerParams(vmem_limit_bytes=mib * 2**20)


def swap(x, axes, far):
    count = lax.axis_size(axes)
    shift = 1 if far else 0
    pairs = [((i + shift) % count, ((i ^ 1) + shift) % count) for i in range(count)]
    return lax.ppermute(x, axes, pairs)


def steps(tracer, velocity, diffusivity, singular, basis_vectors):
    nz, nx, ny = tracer.shape
    count, window = basis_vectors.shape[:2]
    rows = window * nx
    basis = basis_vectors.reshape(count, rows, ny)
    rows_all = rows * ny * lax.axis_size(GX) * lax.axis_size(GY)
    chips = lax.axis_size(CHIPS)
    diff_row = diffusivity.reshape(1, nz)

    columns = shaped(3, nx, ny)
    bulk_rows = shaped(2 * nz, ny)
    hbm_space, any_space = (pl.BlockSpec(memory_space=m) for m in (pltpu.HBM, pl.ANY))
    columns_near, columns_far, near, sent_near, sent_far, mine, speeds = pl.pallas_call(
        lambda *refs: pack_columns_kernel(4, *refs),
        out_shape=(
            columns, columns, shaped(6 * nx, ny), bulk_rows, bulk_rows, shaped(2, nx, ny),
            shaped(2, nx, ny),
        ),
        in_specs=[hbm_space] * 3, out_specs=tuple(whole(7)),
        scratch_shapes=[
            VMEM((nz * nx, ny), F32), pltpu.SemaphoreType.DMA((11,)),
        ],
        compiler_params=limit(4), cost_estimate=cost(10**6, 2 * 2**20), name="columns",
    )(
        in_hbm(tracer.reshape(nz * nx, ny)), in_hbm(tracer.reshape(nz, nx, 1, ny)), in_hbm(velocity)
    )
    sides_far = swap(columns_far, GY, True)
    sides_near = swap(columns_near, GY, False)
    edge = shaped(24, ny)
    edges_near, edges_far, own_up, own_down = pl.pallas_call(
        pack_rows_kernel, out_shape=(edge,) * 4, in_specs=whole(4), out_specs=tuple(whole(4)),
        compiler_params=limit(2), cost_estimate=cost(10**4, 2**17), name="edges",
    )(near, speeds, sides_near, sides_far)
    window_far = swap(edges_far, GX, True)
    window_near = swap(edges_near, GX, False)

    rows_far = in_hbm(swap(in_hbm(sent_far), GX, True))
    rows_near = in_hbm(swap(in_hbm(sent_near), GX, False))

    vectors = pl.pallas_call(
        load_kernel, out_shape=shaped(count, rows, ny),
        in_specs=[hbm_space], out_specs=whole(1)[0],
        scratch_shapes=[pltpu.SemaphoreType.DMA((2,))],
        compiler_params=limit(2), cost_estimate=cost(0, 6 * 2**20), name="load",
    )(in_hbm(basis))
    kept, local = pl.pallas_call(
        window_kernel,
        out_shape=(pltpu.HBM((6 * nx + 16, ny), F32), shaped(2, ny)),
        in_specs=[SMEM_SPEC] + whole(11), out_specs=(hbm_space, *whole(1)),
        scratch_shapes=[
            VMEM((2, rows, ny), F32), VMEM((rows + 16, ny), F32), VMEM((ny, ny), F32),
            VMEM((ny, ny), F32), pltpu.SemaphoreType.DMA((3,)),
        ],
        compiler_params=limit(4), cost_estimate=cost(10**7, 4 * 2**20), name="window",
    )(
        diffusivity, near, speeds, diff_row, mine, sides_near, sides_far,
        own_up, own_down, window_near, window_far, vectors,
    )

    other = lax.ppermute(local, "c", [(0, 1), (1, 0)])
    sent = pl.pallas_call(
        spread_kernel, out_shape=VMEM((chips, 2, ny), F32), in_specs=whole(2), out_specs=whole(1)[0],
        compiler_params=limit(4), cost_estimate=cost(10**4, 2**17), name="spread",
    )(local, other)
    parts = lax.all_to_all(sent, CHIPS, 0, 0, tiled=True)

    halves = shaped(rows // 2, 2 * (count + 2), 2 * ny, dtype=BF16)
    padded = VMEM((nz * (nx + 16), ny), F32)
    tracer_next, split_halves, line = pl.pallas_call(
        lambda *refs: bulk_kernel(8, *refs),
        out_shape=(shaped(nz, nx, ny), halves, shaped(8, ny)),
        in_specs=[SMEM_SPEC] + [hbm_space] * 5 + whole(5),
        out_specs=(any_space, *whole(2)),
        scratch_shapes=[
            padded, padded, VMEM((rows, count, ny), F32), VMEM((6 * nx + 16, ny), F32),
            VMEM((2 * nz, ny), F32), VMEM((2 * nz, ny), F32), pltpu.SemaphoreType.DMA((9,)),
            pltpu.SemaphoreType.DMA((8,)), pltpu.SemaphoreType.DMA((3 + rows,)),
        ],
        compiler_params=limit(12), cost_estimate=cost(10**8, 10 * 2**20), name="bulk",
    )(
        diffusivity, in_hbm(tracer), in_hbm(basis.reshape(count, rows, 1, ny)), in_hbm(kept),
        in_hbm(rows_near), in_hbm(rows_far), velocity, diff_row, singular.reshape(1, count), sides_near, sides_far,
    )

    basis_next = pl.pallas_call(
        lambda *refs: core_kernel(rows_all, *refs),
        out_shape=shaped(count + 2, rows, 1, ny),
        in_specs=whole(3), out_specs=pl.BlockSpec(memory_space=pl.ANY),
        scratch_shapes=[
            VMEM((rows, count + 2, ny), F32),
            pltpu.SemaphoreType.DMA((rows,)),
        ],
        compiler_params=limit(16), cost_estimate=cost(10**8, 6 * 2**20), name="core",
    )(
        parts.reshape(chips // 4, 8, ny), line, split_halves,
    )
    return tracer_next, basis_next.reshape(count + 2, window, nx, ny)


def solution(mesh):
    finer = Mesh(mesh.devices.reshape(8, 4, 4, 2), ("z", "y", "x", "c"))
    in_specs = (P(None, GX, GY), P(None, GX, GY), P(), P(), P(None, None, GX, GY))
    out_specs = (P(None, GX, GY), P(None, None, GX, GY))
    return jax.shard_map(steps, mesh=finer, in_specs=in_specs, out_specs=out_specs, check_vma=False)
```

```python
import math

import jax
import jax.numpy as jnp
from jax import lax
from jax.experimental import pallas as pl
from jax.experimental.pallas import tpu as pltpu
from jax.sharding import Mesh
from jax.sharding import PartitionSpec as P


F32 = jnp.float32
BF16 = jnp.bfloat16
GX = ("z", "y")
GY = ("x", "c")
CHIPS = ("z", "y", "x")
ROOT_ITERS = 5
SHIFTS = 2**ROOT_ITERS
POLES = SHIFTS // 2 - 1
VMEM = pltpu.VMEM


def lanes_of(shape):
    return lax.broadcasted_iota(jnp.int32, shape, len(shape) - 1)


def rows_of(shape):
    return lax.broadcasted_iota(jnp.int32, shape, len(shape) - 2)


def step(c, xm, xp, ym, yp, zm, zp, d, vxp, vxn, vyp, vyn):
    spread = (xm + xp) + (ym + yp) + (zm + zp) - 6.0 * c
    carried = (vxp * (c - xm) + vxn * (xp - c)) + (vyp * (c - ym) + vyn * (yp - c))
    return c + d * spread - carried


def signed_parts(vx, vy):
    return jnp.maximum(vx, 0.0), jnp.minimum(vx, 0.0), jnp.maximum(vy, 0.0), jnp.minimum(vy, 0.0)


def before(c, ghost, axis):
    at = lax.broadcasted_iota(jnp.int32, c.shape, axis)
    return jnp.where(at == 0, ghost, pltpu.roll(c, 1, axis))


def after(c, ghost, axis):
    n = c.shape[axis]
    at = lax.broadcasted_iota(jnp.int32, c.shape, axis)
    return jnp.where(at == n - 1, ghost, pltpu.roll(c, n - 1, axis))


def gx_is_even():
    return lax.axis_index("y") % 2 == 0


def gy_is_even():
    return lax.axis_index("c") == 0


def to_pairs(even, up, down):
    return jnp.where(even, down, up), jnp.where(even, up, down)


def from_pairs(even, near, far):
    return jnp.where(even, far, near), jnp.where(even, near, far)


def pack_columns_kernel(
    chunks, tracer_hbm, velocity_hbm, near, far, window, mine, velocity,
    tracer, sems,
):
    nx, ny = velocity.shape[1:]
    nz = tracer.shape[0] // nx
    size = nz // chunks

    def rows_of_level(at, count, dst):
        return tracer_hbm.at[pl.ds(at * nx, count * nx)], dst

    moves = [
        rows_of_level(i * size, size, tracer.at[pl.ds(i * size * nx, size * nx)])
        for i in range(chunks)
    ]
    moves.append((velocity_hbm, velocity))
    moves.append(rows_of_level(nz - 2, 2, window.at[0 : 2 * nx]))
    moves.append(rows_of_level(0, 4, window.at[2 * nx : 6 * nx]))
    loads = [pltpu.make_async_copy(src, dst, sems.at[i]) for i, (src, dst) in enumerate(moves)]
    for load in loads:
        load.start()
    lane = lanes_of((nx, ny))

    def four(i, carry):
        out = []
        for j in range(4):
            z = 4 * i + j
            r = pltpu.roll(tracer[z * nx : (z + 1) * nx], z, 1)
            out.append(jnp.where(((lane - z + 2) & (ny - 1)) < 4, r, carry[j]))
        return tuple(out)

    carry = (jnp.zeros((nx, ny), F32),) * 4
    for i in range(chunks):
        loads[i].wait()
        for k in range(i * size // 4, (i + 1) * size // 4):
            carry = four(k, carry)
    phase = lane & 3

    def column(shift):
        c = [pltpu.roll(x, shift, 1) if shift else x for x in carry]
        return jnp.where(
            phase < 2, jnp.where(phase == 0, c[0], c[1]), jnp.where(phase == 2, c[2], c[3])
        )

    loads[chunks].wait()
    vx, vy = velocity[0], velocity[1]
    left = (column(0), column(ny - 1), jnp.where(lane == 0, vx, pltpu.roll(vy, 1, 1)))
    right = (
        column(1), column(2),
        jnp.where(lane == ny - 1, vx, pltpu.roll(vy, ny - 1, 1)),
    )
    even = gy_is_even()
    for i in range(3):
        near[i], far[i] = to_pairs(even, left[i], right[i])
    mine[0], mine[1] = left[0], right[0]
    for load in loads[chunks + 1 :]:
        load.wait()


def pack_rows_kernel(window, velocity, sides_near, sides_far, near, far, up, down):
    nx, ny = velocity.shape[1:]
    from_left, from_right = from_pairs(gy_is_even(), sides_near[0], sides_far[0])
    for edge, inner, out in ((0, 1, up), (nx - 1, nx - 2, down)):
        for s in range(6):
            out[s : s + 1, :] = window[s * nx + edge : s * nx + edge + 1, :]
            out[8 + s : 9 + s, :] = window[s * nx + inner : s * nx + inner + 1, :]
        for s in (6, 7, 14, 15, 20, 21, 22, 23):
            out[s : s + 1, :] = jnp.zeros((1, ny), F32)
        out[16:17, :] = velocity[0, edge : edge + 1, :]
        out[17:18, :] = velocity[1, edge : edge + 1, :]
        out[18:19, :] = from_left[edge : edge + 1, :]
        out[19:20, :] = from_right[edge : edge + 1, :]
    near[...], far[...] = to_pairs(gx_is_even(), up[...], down[...])


def window_kernel(
    diff, near, velocity, diff_row, mine, sides_near, sides_far,
    own_up, own_down, rows_near, rows_far, basis,
    kept_hbm, sums, snaps, sides, q0, q1, sems,
):
    nz, nx, ny = diff.shape[0], velocity.shape[1], velocity.shape[2]
    count = basis.shape[0]
    dz = diff_row[...]
    even = gy_is_even()
    pairs = [from_pairs(even, sides_near[i], sides_far[i]) for i in range(3)]
    from_left, from_right = [p[0] for p in pairs], [p[1] for p in pairs]
    from_up, from_down = from_pairs(gx_is_even(), rows_near[...], rows_far[...])
    for gin, inner, outer, corner, vx_at, vy_at, out in (
        (from_left, None, mine[0], 18, ny - 1, ny - 2, sides.at[0:nx]),
        (from_right, mine[1], None, 19, 0, 1, sides.at[nx : 2 * nx]),
    ):
        c = gin[0]
        ym = gin[1] if inner is None else inner
        yp = gin[1] if outer is None else outer
        vx = gin[2][:, vx_at : vx_at + 1]
        vy = gin[2][:, vy_at : vy_at + 1]
        parts = signed_parts(vx, vy)
        xm = before(c, from_up[corner : corner + 1, :], 0)
        xp = after(c, from_down[corner : corner + 1, :], 0)
        out[...] = step(c, xm, xp, ym, yp, pltpu.roll(c, 1, 1), pltpu.roll(c, nz - 1, 1), dz, *parts)

    sub = rows_of((8, ny))
    lane = lanes_of((8, ny))
    d_rows = jnp.where(sub == 2, diff[0], diff[1])
    ghost_rows = []
    for gin, own, top in ((from_up, own_up, True), (from_down, own_down, False)):
        c = gin[0:8, :]
        beyond, inside = gin[8:16, :], own[0:8, :]
        xm, xp = (beyond, inside) if top else (inside, beyond)
        west = jnp.where(sub == 2, gin[18:19, 0:1], gin[18:19, 1:2])
        east = jnp.where(sub == 2, gin[19:20, 0:1], gin[19:20, 1:2])
        parts = signed_parts(gin[16:17, :], gin[17:18, :])
        ghost_rows.append(
            step(c, xm, xp, before(c, west, 1), after(c, east, 1),
                 pltpu.roll(c, 1, 0), pltpu.roll(c, 7, 0), d_rows, *parts)
        )

    parts = signed_parts(velocity[0], velocity[1])
    u = [near[s * nx : (s + 1) * nx] for s in range(6)]
    first = []
    for s in range(1, 5):
        z = (s - 2) % nz
        c = u[s]
        xm = before(c, from_up[s : s + 1, :], 0)
        xp = after(c, from_down[s : s + 1, :], 0)
        ym = before(c, from_left[0][:, z : z + 1], 1)
        yp = after(c, from_right[0][:, z : z + 1], 1)
        first.append(step(c, xm, xp, ym, yp, u[s - 1], u[s + 1], diff[z], *parts))
    for z in range(2):
        c = first[z + 1]
        snaps[0, z * nx : (z + 1) * nx, :] = c
        xm = before(c, ghost_rows[0][z + 2 : z + 3, :], 0)
        xp = after(c, ghost_rows[1][z + 2 : z + 3, :], 0)
        ym = before(c, sides[0:nx, z : z + 1], 1)
        yp = after(c, sides[nx : 2 * nx, z : z + 1], 1)
        snaps[1, z * nx : (z + 1) * nx, :] = step(
            c, xm, xp, ym, yp, first[z], first[z + 2], diff[z], *parts
        )

    rows = 2 * nx
    pieces = rows // 8
    sides[rows : rows + 8] = from_up[16:24, :]
    sides[rows + 8 : rows + 16] = from_down[16:24, :]
    keep = [
        pltpu.make_async_copy(ref, kept_hbm.at[pl.ds(at, ref.shape[0])], sems.at[i])
        for i, (ref, at) in enumerate(
            ((snaps.at[0], 0), (snaps.at[1], rows), (sides, 2 * rows))
        )
    ]
    for copy in keep:
        copy.start()

    def folded(a, b):
        total = a[0:8, :] * b[0:8, :]
        for i in range(1, pieces):
            total = total + a[8 * i : 8 * i + 8, :] * b[8 * i : 8 * i + 8, :]
        return total

    def group(vectors, start, size):
        for m, q in enumerate((q0, q1)):
            lines = jnp.stack([folded(v, snaps[m]) for v in vectors])
            q[pl.ds(start, size), :] = jnp.sum(lines, axis=1)

    def eight(i, carry):
        at = pl.multiple_of(8 * i, 8)
        group([basis[at + j] for j in range(8)], at, 8)
        return carry

    full = count // 8 * 8
    lax.fori_loop(0, count // 8, eight, 0)
    group([basis[k] for k in range(full, count)] + [snaps[0], snaps[1]], full, count + 2 - full)
    for q in (q0, q1):
        q[count + 2 :] = jnp.zeros((ny - count - 2, ny), F32)
    ones = jnp.ones((8, ny), F32)
    over_lanes = (((1,), (1,)), ((), ()))
    for m, q in enumerate((q0, q1)):
        line = lax.dot_general(
            ones, q[...], over_lanes, precision=lax.Precision.HIGHEST, preferred_element_type=F32
        )
        sums[m : m + 1, :] = line[0:1, :]
    for copy in keep:
        copy.wait()


def split(vectors, snaps, halves):
    rows, ny = vectors.shape[0], vectors.shape[2]
    size = halves.shape[1] // 2
    for r in range(rows):
        pair, half = r // 2, r % 2
        lanes = slice(half * ny, (half + 1) * ny)
        v = jnp.concatenate(
            [vectors[r], snaps[r : r + 1, :], snaps[rows + r : rows + r + 1, :]], axis=0
        )
        hi = v.astype(BF16)
        halves[pair, :size, lanes] = hi
        halves[pair, size:, lanes] = (v - hi.astype(F32)).astype(BF16)


def load_kernel(src, by_row_hbm, dst, rows_near, rows_far, sems):
    nz, nx = by_row_hbm.shape[:2]
    parts = 2
    size = src.shape[0] // parts
    copies = [
        pltpu.make_async_copy(src.at[pl.ds(i * size, size)], dst.at[pl.ds(i * size, size)], sems.at[i])
        for i in range(parts)
    ]
    moves = []
    even = gx_is_even()
    for i in range(2):
        part, first, last = pl.ds(i * nz, nz), i, nx - 1 - i
        at_near, at_far = jnp.where(even, last, first), jnp.where(even, first, last)
        moves.append((by_row_hbm.at[:, at_near, 0, :], rows_near.at[part]))
        moves.append((by_row_hbm.at[:, at_far, 0, :], rows_far.at[part]))
    copies += [
        pltpu.make_async_copy(a, b, sems.at[parts + i]) for i, (a, b) in enumerate(moves)
    ]
    for copy in copies:
        copy.start()
    for copy in copies:
        copy.wait()


def level_loads(src, dst, sems, chunks, nx):
    pitch = nx + 16
    nz = src.shape[0]
    size = nz // chunks
    view = dst.reshape(nz, pitch, dst.shape[1])

    def copy(at, length, sem):
        part = pl.ds(at, length)
        return pltpu.make_async_copy(src.at[part], view.at[part, pl.ds(8, nx), :], sem)

    def chunk(k):
        return copy(k * size, size, sems.at[k])

    end = copy(nz - size, size - 1, sems.at[chunks - 1])
    last = copy(nz - 1, 1, sems.at[chunks])
    return chunk, end, last


def sweep(diff, velocity, src, dst, col_left, col_right, wait, after_block, chunks):
    nx, ny = velocity.shape[1:]
    pitch = nx + 16
    nz = src.shape[0] // pitch
    size = nz // chunks
    vx, vy = velocity[0], velocity[1]
    east, north = vx > 0.0, vy > 0.0
    speed_x, speed_y = jnp.abs(vx), jnp.abs(vy)
    stay = 1.0 - speed_x - speed_y
    lane = lanes_of((nx, ny))
    first, last = lane == 0, lane == ny - 1
    is_even = (lane & 1) == 0
    shifted = pltpu.roll(col_right, nz - 1, 1)
    columns = (jnp.where(is_even, col_left, shifted), jnp.where(is_even, shifted, col_left))

    def rows_at(z, by):
        return pl.ds(pl.multiple_of(z * pitch, 8) + 8 + by, nx)

    def turned(c, z, which):
        side = pltpu.roll(columns[which], (nz - z) & (nz - 1), 1)
        return pltpu.roll(c, 1, 1), pltpu.roll(c, ny - 1, 1), side

    def level(z, next_parity, state):
        zm, c, south, north_side, side = state
        zn = (z + 1) & (nz - 1)
        zp = src[rows_at(zn, 0), :]
        ahead = turned(zp, zn, next_parity)
        ym = jnp.where(first, side, south)
        yp = jnp.where(last, side, north_side)
        xm = src[rows_at(z, -1), :]
        xp = src[rows_at(z, 1), :]
        d = diff[z]
        moved = speed_x * jnp.where(east, xm, xp) + speed_y * jnp.where(north, ym, yp)
        spread = ((xm + xp) + (ym + yp)) + (zm + zp)
        dst[rows_at(z, 0), :] = (c * (stay - 6.0 * d) + moved) + d * spread
        return (c, zp, *ahead)

    def block(k, state):
        wait(k)
        for i in range(0, size, 2):
            z = k * size + i
            state = level(z + 1, 0, level(z, 1, state))
        after_block(k)
        return state

    c = src[rows_at(0, 0), :]
    state = (src[rows_at(nz - 1, 0), :], c, *turned(c, 0, 0))
    lax.fori_loop(0, chunks, block, state)


def level_store(src, out, sems, chunks, nx):
    pitch = nx + 16
    nz = src.shape[0] // pitch
    size = nz // chunks
    view = src.reshape(nz, pitch, src.shape[1])

    def store(k):
        part = pl.ds(k * size, size)
        return pltpu.make_async_copy(view.at[part, pl.ds(8, nx), :], out.at[part], sems.at[k])

    return store


def start_loads(loads, chunks):
    chunk, end, last = loads
    last.start()
    for k in range(chunks - 1):
        chunk(k).start()
    end.start()


def bulk_kernel(
    chunks, diff, tracer, basis, kept_hbm, rows_near, rows_far, velocity, diff_row, singular,
    sides_near, sides_far, out, halves, line, now, then, vectors, kept, got_near, got_far,
    load_sems, store_sems, sems,
):
    nz, nx, _ = tracer.shape
    pitch = nx + 16
    count = singular.shape[1]
    small = [
        pltpu.make_async_copy(src, dst, sems.at[i])
        for i, (src, dst) in enumerate(
            ((rows_near, got_near), (rows_far, got_far), (kept_hbm, kept))
        )
    ]
    for load in small:
        load.start()
    loads = level_loads(tracer, now, load_sems, chunks, nx)
    start_loads(loads, chunks)
    gathers = [
        pltpu.make_async_copy(basis.at[:, r, 0, :], vectors.at[r], sems.at[3 + r])
        for r in range(vectors.shape[0])
    ]
    for gather in gathers:
        gather.start()
    line[...] = jnp.zeros_like(line)
    line[0:1, :count] = singular[...]
    eye = rows_of((nz, nz)) == lanes_of((nz, nz))
    d_all = jnp.sum(jnp.where(eye, diff_row[...], 0.0), axis=1, keepdims=True)
    small[0].wait()
    small[1].wait()
    even = gx_is_even()
    from_up, from_down = from_pairs(even, got_near[0:nz], got_far[0:nz])
    now[pl.ds(7, nz, stride=pitch), :] = from_up
    now[pl.ds(8 + nx, nz, stride=pitch), :] = from_down
    chunk, end, final = loads
    final.wait()
    chunk(0).wait()

    def wait(k):
        @pl.when(k < chunks - 2)
        def _():
            chunk(k + 1).wait()

        @pl.when(k == chunks - 2)
        def _():
            end.wait()

    from_left, from_right = from_pairs(gy_is_even(), sides_near[0], sides_far[0])
    sweep(diff, velocity, now, then, from_left, from_right, wait, lambda k: None, chunks)
    small[2].wait()
    nearest = from_pairs(even, got_near[0:nz], got_far[0:nz])
    beyonds = from_pairs(even, got_near[nz:], got_far[nz:])
    for is_top, c, beyond, at in zip((True, False), nearest, beyonds, (6 * nx, 6 * nx + 8)):
        gin = kept[at : at + 8, :]
        inside = now[pl.ds(8 if is_top else 7 + nx, nz, stride=pitch), :]
        xm, xp = (beyond, inside) if is_top else (inside, beyond)
        west = jnp.sum(jnp.where(eye, gin[2:3, :], 0.0), axis=1, keepdims=True)
        east = jnp.sum(jnp.where(eye, gin[3:4, :], 0.0), axis=1, keepdims=True)
        parts = signed_parts(gin[0:1, :], gin[1:2, :])
        then[pl.ds(7 if is_top else 8 + nx, nz, stride=pitch), :] = step(
            c, xm, xp, before(c, west, 1), after(c, east, 1),
            pltpu.roll(c, 1, 0), pltpu.roll(c, nz - 1, 0), d_all, *parts
        )
    store = level_store(now, out, store_sems, chunks, nx)
    col_left, col_right = kept[4 * nx : 5 * nx, :], kept[5 * nx : 6 * nx, :]
    sweep(
        diff, velocity, then, now, col_left, col_right, lambda k: None,
        lambda k: store(k).start(), chunks,
    )
    for gather in gathers:
        gather.wait()
    split(vectors, kept, halves)
    for k in range(chunks):
        store(k).wait()


def spread_kernel(mine, other, out):
    both = mine[...] + other[...]
    out[...] = jnp.broadcast_to(both[None], out.shape)


def core_kernel(rows_all, parts, singular, halves, out, block, sems):
    count = out.shape[0] - 2
    n = parts.shape[2]
    total = jnp.sum(parts[...], axis=0)
    total = total + pltpu.roll(total, 2, 0)
    total = total + pltpu.roll(total, 4, 0)
    total = total * (1.0 / rows_all)
    lane = lanes_of((1, n))
    zero = jnp.zeros((1, n), F32)

    def add(x):
        return jnp.sum(x, axis=1, keepdims=True)

    def pick(x, at):
        return add(jnp.where(lane == at, x, zero))

    p0 = jnp.where(lane < count, total[0:1, :], zero)
    p1 = jnp.where(lane < count, total[1:2, :], zero)
    g00 = pick(total[0:1, :], count) - add(p0 * p0) + 1e-06
    g01 = pick(total[0:1, :], count + 1) - add(p0 * p1)
    g11 = pick(total[1:2, :], count + 1) - add(p1 * p1) + 1e-06
    r11 = jnp.sqrt(g00)
    r12 = g01 / r11
    r22 = jnp.sqrt(g11 - r12 * r12)
    u0 = jnp.where(lane == count, r11, p0)
    u1 = jnp.where(lane == count, r12, jnp.where(lane == count + 1, r22, p1))
    s = singular[0:1, :]
    squares = s * s
    sigma = add(squares + u0 * u0 + u1 * u1) / (count + 2)
    root = jnp.sqrt(sigma)
    d = squares / sigma
    v0 = u0 / root
    v1 = u1 / root

    half = POLES + 1
    row = rows_of((half, n))
    pole = jnp.zeros((half, n), F32)
    for j in range(POLES):
        pole = jnp.where(row == j, math.tan(math.pi * (j + 1) / SHIFTS) ** 2, pole)
    last = row == POLES
    pole = jnp.where(last, 1.0, pole)
    inverse = jnp.where(last, 1.0, 1.0 / (d + pole))
    weight = 2.0 * (1.0 + pole)
    w0 = inverse * v0
    w1 = inverse * v1
    last_one = last[:, 0:1]
    a = jnp.where(last_one, 1.0, 1.0 + add(w0 * v0))
    b = jnp.where(last_one, 0.0, add(w0 * v1))
    c = jnp.where(last_one, 1.0, 1.0 + add(w1 * v1))
    e = b / a
    c = c - b * e
    strength = jnp.where(last, 1.0, weight * pole)
    w1 = jnp.sqrt(strength / c) * (w1 - e * w0)
    w0 = jnp.sqrt(strength / a) * w0
    low_rank = jnp.concatenate([w0, w1], axis=0)
    gains = 1.0 + d + jnp.sum(jnp.where(last, 0.0, weight * d * inverse), axis=0, keepdims=True)
    square = (n, n)
    core = lax.dot_general(
        low_rank, low_rank, (((0,), (0,)), ((), ())),
        precision=lax.Precision.HIGHEST, preferred_element_type=F32,
    )
    core = core + jnp.where(rows_of(square) == lanes_of(square), gains, 0.0)
    core = core * (root * (1.0 / SHIFTS))
    t0 = jnp.where(lane == count, 1.0, -p0) / r11
    q_lane = jnp.where(lane == count + 1, 1.0, -p1)
    t1 = (q_lane - r12 * t0) / r22
    full = jnp.where(lanes_of(square) < count, core, 0.0)
    full = full + core[:, count : count + 1] * t0 + core[:, count + 1 : count + 2] * t1
    full = full[: count + 2, : count + 2]
    hi = full.astype(BF16)
    lo = (full - hi.astype(F32)).astype(BF16)
    twice = jnp.concatenate([hi, hi], axis=1)
    size = count + 2
    blocks = block.shape[1] // 8
    copies = []
    for b in range(blocks):
        tiles = []
        for pair in range(4 * b, 4 * b + 4):
            r = jnp.dot(twice, halves[pair], preferred_element_type=F32)
            r = r + jnp.dot(lo, halves[pair, :size], preferred_element_type=F32)
            tiles.append(r[:, :n])
            tiles.append(r[:, n:])
        block[:, 8 * b : 8 * b + 8, :] = jnp.swapaxes(jnp.stack(tiles), 0, 1)
        copy = pltpu.make_async_copy(
            block.at[:, pl.ds(8 * b, 8), :], out.at[:, pl.ds(8 * b, 8), :], sems.at[b]
        )
        copy.start()
        copies.append(copy)
    for copy in copies:
        copy.wait()


def whole(n):
    return [pl.BlockSpec(memory_space=VMEM)] * n


SMEM_SPEC = pl.BlockSpec(memory_space=pltpu.SMEM)


def shaped(*shape, dtype=F32):
    return jax.ShapeDtypeStruct(shape, dtype)


def in_hbm(x):
    return pltpu.with_memory_space_constraint(x, pltpu.HBM)


def cost(flops, moved):
    return pl.CostEstimate(flops=flops, bytes_accessed=moved, transcendentals=0)


def limit(mib):
    return pltpu.CompilerParams(vmem_limit_bytes=mib * 2**20)


def swap(x, axes, far):
    count = lax.axis_size(axes)
    shift = 1 if far else 0
    pairs = [((i + shift) % count, ((i ^ 1) + shift) % count) for i in range(count)]
    return lax.ppermute(x, axes, pairs)


def steps(tracer, velocity, diffusivity, singular, basis_vectors):
    nz, nx, ny = tracer.shape
    count, window = basis_vectors.shape[:2]
    rows = window * nx
    basis = basis_vectors.reshape(count, rows, ny)
    rows_all = rows * ny * lax.axis_size(GX) * lax.axis_size(GY)
    chips = lax.axis_size(CHIPS)
    diff_row = diffusivity.reshape(1, nz)

    columns = shaped(3, nx, ny)
    bulk_rows = shaped(2 * nz, ny)
    hbm_space, any_space = (pl.BlockSpec(memory_space=m) for m in (pltpu.HBM, pl.ANY))
    columns_near, columns_far, near, mine, speeds = pl.pallas_call(
        lambda *refs: pack_columns_kernel(4, *refs),
        out_shape=(
            columns, columns, shaped(6 * nx, ny), shaped(2, nx, ny),
            shaped(2, nx, ny),
        ),
        in_specs=[hbm_space] * 2, out_specs=tuple(whole(5)),
        scratch_shapes=[
            VMEM((nz * nx, ny), F32), pltpu.SemaphoreType.DMA((11,)),
        ],
        compiler_params=limit(4), cost_estimate=cost(10**6, 2 * 2**20), name="columns",
    )(
        in_hbm(tracer.reshape(nz * nx, ny)), in_hbm(velocity)
    )
    sides_far = swap(columns_far, GY, True)
    sides_near = swap(columns_near, GY, False)
    edge = shaped(24, ny)
    edges_near, edges_far, own_up, own_down = pl.pallas_call(
        pack_rows_kernel, out_shape=(edge,) * 4, in_specs=whole(4), out_specs=tuple(whole(4)),
        compiler_params=limit(2), cost_estimate=cost(10**4, 2**17), name="edges",
    )(near, speeds, sides_near, sides_far)
    window_far = swap(edges_far, GX, True)
    window_near = swap(edges_near, GX, False)

    vectors, sent_near, sent_far = pl.pallas_call(
        load_kernel, out_shape=(shaped(count, rows, ny), bulk_rows, bulk_rows),
        in_specs=[hbm_space] * 2, out_specs=tuple(whole(3)),
        scratch_shapes=[pltpu.SemaphoreType.DMA((6,))],
        compiler_params=limit(2), cost_estimate=cost(0, 6 * 2**20), name="load",
    )(in_hbm(basis), in_hbm(tracer.reshape(nz, nx, 1, ny)))
    rows_far = in_hbm(swap(in_hbm(sent_far), GX, True))
    rows_near = in_hbm(swap(in_hbm(sent_near), GX, False))

    kept, local = pl.pallas_call(
        window_kernel,
        out_shape=(pltpu.HBM((6 * nx + 16, ny), F32), shaped(2, ny)),
        in_specs=[SMEM_SPEC] + whole(11), out_specs=(hbm_space, *whole(1)),
        scratch_shapes=[
            VMEM((2, rows, ny), F32), VMEM((rows + 16, ny), F32), VMEM((ny, ny), F32),
            VMEM((ny, ny), F32), pltpu.SemaphoreType.DMA((3,)),
        ],
        compiler_params=limit(4), cost_estimate=cost(10**7, 4 * 2**20), name="window",
    )(
        diffusivity, near, speeds, diff_row, mine, sides_near, sides_far,
        own_up, own_down, window_near, window_far, vectors,
    )

    other = lax.ppermute(local, "c", [(0, 1), (1, 0)])
    sent = pl.pallas_call(
        spread_kernel, out_shape=shaped(chips, 2, ny), in_specs=whole(2), out_specs=whole(1)[0],
        compiler_params=limit(4), cost_estimate=cost(10**4, 2**17), name="spread",
    )(local, other)
    parts = lax.all_to_all(sent, CHIPS, 0, 0, tiled=True)

    halves = shaped(rows // 2, 2 * (count + 2), 2 * ny, dtype=BF16)
    padded = VMEM((nz * (nx + 16), ny), F32)
    tracer_next, split_halves, line = pl.pallas_call(
        lambda *refs: bulk_kernel(8, *refs),
        out_shape=(shaped(nz, nx, ny), halves, shaped(8, ny)),
        in_specs=[SMEM_SPEC] + [hbm_space] * 5 + whole(5),
        out_specs=(any_space, *whole(2)),
        scratch_shapes=[
            padded, padded, VMEM((rows, count, ny), F32), VMEM((6 * nx + 16, ny), F32),
            VMEM((2 * nz, ny), F32), VMEM((2 * nz, ny), F32), pltpu.SemaphoreType.DMA((9,)),
            pltpu.SemaphoreType.DMA((8,)), pltpu.SemaphoreType.DMA((3 + rows,)),
        ],
        compiler_params=limit(12), cost_estimate=cost(10**8, 10 * 2**20), name="bulk",
    )(
        diffusivity, in_hbm(tracer), in_hbm(basis.reshape(count, rows, 1, ny)), in_hbm(kept),
        in_hbm(rows_near), in_hbm(rows_far), velocity, diff_row, singular.reshape(1, count), sides_near, sides_far,
    )

    basis_next = pl.pallas_call(
        lambda *refs: core_kernel(rows_all, *refs),
        out_shape=shaped(count + 2, rows, ny),
        in_specs=whole(3), out_specs=pl.BlockSpec(memory_space=pl.ANY),
        scratch_shapes=[
            VMEM((count + 2, rows, ny), F32),
            pltpu.SemaphoreType.DMA((rows // 8,)),
        ],
        compiler_params=limit(16), cost_estimate=cost(10**8, 6 * 2**20), name="core",
    )(
        parts.reshape(chips // 4, 8, ny), line, split_halves,
    )
    return tracer_next, basis_next.reshape(count + 2, window, nx, ny)


def solution(mesh):
    finer = Mesh(mesh.devices.reshape(8, 4, 4, 2), ("z", "y", "x", "c"))
    in_specs = (P(None, GX, GY), P(None, GX, GY), P(), P(), P(None, None, GX, GY))
    out_specs = (P(None, GX, GY), P(None, None, GX, GY))
    return jax.shard_map(steps, mesh=finer, in_specs=in_specs, out_specs=out_specs, check_vma=False)
```
